256 devices in a mesh: pat: 4 (over z_lo), vox: 64 (over z_hi, x, y, core).
Axes of the slice: x: 4, y: 4, z: 8 (z_hi: 2, z_lo: 4; z = z_hi * 4 + z_lo), core: 2. Of those that a mesh axis runs over, the one named last changes fastest.
Arguments:
- conductivity: float32 [128, 128, 128], P('vox'), may hold values from 0.3 to 1.5
- warm_forward: float32 [128, 32, 128, 128], P('vox', 'pat'), may hold values from -3 to 3
- warm_adjoint: float32 [128, 32, 128, 128], P('vox', 'pat'), may hold values from -3 to 3
- electrodes: int32 [128], replicated, may hold values from 0 to 2097151
- patterns: int32 [32, 4], P('pat'), may hold values from 0 to 127, all different within a row
- observed: float32 [32], P('pat'), may hold values from -16 to 16
Outputs:
- gradient: float32 [128, 128, 128], P('vox')
- predicted: float32 [32], P('pat')
The draws below stay inside these ranges and needn't reach their ends.
All inputs are finite; a program needn't handle non-finite values.
Results may differ from the reference program's by a relative error of at most 0.0003.
Values sent between devices are 32-bit elements; how exact they have to be, the bound alone decides.
A program may use at most 64 MiB of HBM per device.

```python
import math
import jax
import jax.numpy as jnp
from jax import lax

GRID = 128
ELEC = 128
ITERS = 2
NZ = 128
PATTERNS = 32


def warm_potential(key):
    field_shape = (NZ, PATTERNS, GRID, GRID)
    height = 1.0 + 2.0 * jnp.arange(NZ, dtype=jnp.float32)[:, None, None, None] / max(NZ - 1, 1)
    baseline = jnp.clip(jax.random.normal(key, field_shape, jnp.float32), -4.0, 4.0)
    return 0.25 * baseline * height


def draw_warm_forward(key, part):
    return warm_potential(jax.random.fold_in(key, 21))


def draw_warm_adjoint(key, part):
    return warm_potential(jax.random.fold_in(key, 37))


def draw_electrodes(key, part):
    key_depth, key_rows, key_columns = jax.random.split(jax.random.fold_in(key, 11), 3)
    electrode_number = jnp.arange(ELEC, dtype=jnp.int32)
    cycle_depth = electrode_number * NZ // ELEC + jax.random.randint(key_depth, (ELEC,), 0, max(NZ // ELEC, 1))
    row_pick = jax.random.randint(key_rows, (ELEC,), 0, GRID)
    column_pick = jax.random.randint(key_columns, (ELEC,), 0, GRID)
    return ((cycle_depth * GRID + row_pick) * GRID + column_pick).astype(jnp.int32)


def steps_of(rng, dims, cuts, smallest, largest):
    gain = 1.0
    for axis_at, shards_of in cuts:
        heights = jax.random.uniform(jax.random.fold_in(jax.random.fold_in(rng, 6), axis_at), (shards_of,), jnp.float32, smallest / len(cuts), largest / len(cuts))
        gain = gain * jnp.repeat(jnp.exp(heights), dims[axis_at] // shards_of).reshape((-1,) + (1,) * (len(dims) - 1 - axis_at))
    return gain


def different_ones(key, rows, amount, top, lift):
    ranking = jax.random.permutation(jax.random.fold_in(key, 1), amount)
    favour = ranking
    for power in range(3):
        favour = favour * favour // amount
    favour = favour * lift // amount
    lots = jax.random.randint(jax.random.fold_in(key, 2), (rows, amount), 0, 4096) + favour
    sure = jax.random.permutation(jax.random.fold_in(key, 3), rows)[jnp.arange(amount) % rows]
    lots = jnp.where(jnp.arange(rows)[:, None] == sure[None, :], 1 << 14, lots)
    score = lots * amount + jnp.arange(amount)
    return lax.top_k(score.astype(jnp.int32), top)[1].astype(jnp.int32)


def centred(stream_key, shape, scale, most, cuts=(), kind=jnp.bfloat16):
    values = scale * jax.random.normal(stream_key, shape, jnp.float32)
    if cuts:
        values = values * steps_of(stream_key, shape, cuts, -0.22, 0.18)
    return jnp.clip(values, -most, most).astype(kind)


def setup_inputs(seed: int = 0) -> dict:
    splits = jax.random.split(jax.random.key(seed), 7)
    conductivity = jnp.clip(jnp.exp(math.log(1.5) - 1.60943787 * jax.random.uniform(splits[0], (NZ, GRID, GRID), jnp.float32) ** steps_of(splits[0], (NZ, GRID, GRID), ((0, 64),), -0.2, 0.2)), 0.3, 1.5)
    warm_forward = draw_warm_forward(jax.random.fold_in(splits[6], 71), 0)
    warm_adjoint = draw_warm_adjoint(jax.random.fold_in(splits[6], 71), 0)
    electrodes = draw_electrodes(jax.random.fold_in(splits[6], 71), 0)
    patterns = different_ones(splits[4], PATTERNS, ELEC, 4, 0)
    observed = centred(splits[5], (PATTERNS,), 4.0, 16.0, ((0, 4),), jnp.float32)
    return {"conductivity": conductivity, "warm_forward": warm_forward, "warm_adjoint": warm_adjoint, "electrodes": electrodes, "patterns": patterns, "observed": observed}


leakage = 0.05

def both_sides(values, along_axis):
    lower_pad = [(0, 0)] * values.ndim
    upper_pad = [(0, 0)] * values.ndim
    lower_pad[along_axis] = (1, 0)
    upper_pad[along_axis] = (0, 1)
    return jnp.pad(values, lower_pad) + jnp.pad(values, upper_pad)

def spread(values, along_axis):
    lower_pad = [(0, 0)] * values.ndim
    upper_pad = [(0, 0)] * values.ndim
    lower_pad[along_axis] = (1, 0)
    upper_pad[along_axis] = (0, 1)
    return jnp.pad(values, lower_pad) - jnp.pad(values, upper_pad)

def operate(values, coeffs):
    depth_faces, row_faces, column_faces = coeffs
    result = leakage * values
    result = result + spread(depth_faces * (values[1:] - values[:-1]), 0)
    result = result + spread(row_faces * (values[:, 1:] - values[:, :-1]), 1)
    result = result + spread(column_faces * (values[:, :, 1:] - values[:, :, :-1]), 2)
    return result

def solve(right_side, initial, coeffs, diagonal):
    solution = initial
    residue = right_side - operate(solution, coeffs)
    precond = residue / diagonal
    direction = precond
    current = jnp.sum(residue * precond)
    for iteration in range(ITERS):
        applied = operate(direction, coeffs)
        step_size = current / jnp.sum(direction * applied)
        solution = solution + step_size * direction
        residue = residue - step_size * applied
        if iteration + 1 < ITERS:
            precond = residue / diagonal
            following = jnp.sum(residue * precond)
            direction = precond + following / current * direction
            current = following
    return solution

def face_products(forward, adjoint):
    depth_products = (forward[1:] - forward[:-1]) * (adjoint[1:] - adjoint[:-1])
    row_products = (forward[:, 1:] - forward[:, :-1]) * (adjoint[:, 1:] - adjoint[:, :-1])
    column_products = (forward[:, :, 1:] - forward[:, :, :-1]) * (adjoint[:, :, 1:] - adjoint[:, :, :-1])
    return -0.5 * (both_sides(depth_products, 0) + both_sides(row_products, 1) + both_sides(column_products, 2))

def reference(conductivity, warm_forward, warm_adjoint, electrodes, patterns, observed):
    depth_faces = 0.5 * (conductivity[1:] + conductivity[:-1])
    row_faces = 0.5 * (conductivity[:, 1:] + conductivity[:, :-1])
    column_faces = 0.5 * (conductivity[:, :, 1:] + conductivity[:, :, :-1])
    coeffs = (depth_faces, row_faces, column_faces)
    diagonal = leakage + both_sides(depth_faces, 0) + both_sides(row_faces, 1) + both_sides(column_faces, 2)
    voxels = electrodes[patterns].astype(jnp.int32)
    cell_total = NZ * GRID * GRID
    strength = 2.0 * math.sqrt(cell_total)
    data_weight = 0.1 * strength

    def one_pattern(accumulated, pattern_number):
        start_forward = lax.dynamic_index_in_dim(warm_forward, pattern_number, 1, keepdims=False)
        start_adjoint = lax.dynamic_index_in_dim(warm_adjoint, pattern_number, 1, keepdims=False)
        chosen = lax.dynamic_index_in_dim(voxels, pattern_number, 0, keepdims=False)
        right_side = jnp.zeros((cell_total,), jnp.float32).at[chosen[0]].add(strength).at[chosen[1]].add(-strength)
        forward = solve(right_side.reshape(NZ, GRID, GRID), start_forward, coeffs, diagonal)
        flattened = forward.reshape(-1)
        voltage = flattened[chosen[2]] - flattened[chosen[3]]
        misfit = voltage - lax.dynamic_index_in_dim(observed, pattern_number, 0, keepdims=False)
        weighted = data_weight * misfit
        source = jnp.zeros((cell_total,), jnp.float32).at[chosen[2]].add(weighted).at[chosen[3]].add(-weighted)
        adjoint = solve(source.reshape(NZ, GRID, GRID), start_adjoint, coeffs, diagonal)
        return (accumulated + face_products(forward, adjoint), voltage)
    gradient, predicted = lax.scan(one_pattern, jnp.zeros((NZ, GRID, GRID), jnp.float32), jnp.arange(PATTERNS, dtype=jnp.int32))
    return (gradient, predicted)
```

```python
import functools
import math

import jax
import jax.numpy as jnp
from jax import lax
from jax.experimental import pallas as pl
from jax.experimental.pallas import tpu as pltpu
from jax.sharding import PartitionSpec as P

MESH = pl.DeviceIdType.MESH
LEAK = 0.05
N = 128
PLANE = N * N
PC = 8

ZL, ZH, XM, XP, YM, YP, DG, DI = range(8)


def up_row(x):
    return pltpu.roll(x, N - 1, 0)


def down_row(x):
    return pltpu.roll(x, 1, 0)


def up_col(x):
    return pltpu.roll(x, N - 1, 1)


def down_col(x):
    return pltpu.roll(x, 1, 1)


def total(x):
    part = jnp.sum(x.reshape(N // 8, 8, N), axis=0)
    return jnp.sum(jnp.sum(part, axis=1, keepdims=True), axis=0, keepdims=True)


def kernel(
    npat,
    layers,
    group,
    strength,
    cond,
    wf,
    wa,
    elec,
    pats,
    obs,
    grad_out,
    pred_out,
    sh,
    xh,
    dh,
    wh,
    d0,
    w0,
    dc,
    co,
    dih,
    acc,
    tile,
    red,
    kc,
    gb,
    rsb,
    agb,
    sig_s,
    sig_r,
    hs,
    hr,
    red_s,
    red_r,
    rs_s,
    rs_r,
    ag_s,
    ag_r,
):
    q = lax.axis_index("pat")
    v = lax.axis_index("vox")
    has_lo = v > 0
    has_hi = v < layers - 1
    groups = layers // group
    rank = (lax.rem(v, group), v // group)
    sizes = (group, groups)
    warm = (wf, wa)
    data_weight = 0.1 * strength
    chunk = N // npat

    def member(stage, k):
        return (v // group) * group + k if stage == 0 else k * group + lax.rem(v, group)

    barrier = pltpu.get_barrier_semaphore()

    def greet(device):
        pl.semaphore_signal(barrier, inc=1, device_id=device, device_id_type=MESH)

    @pl.when(has_lo)
    def _():
        greet((q, v - 1))

    @pl.when(has_hi)
    def _():
        greet((q, v + 1))

    for stage in range(2):
        for j in range(1, sizes[stage]):
            greet((q, member(stage, lax.rem(rank[stage] + j, sizes[stage]))))
    for j in range(1, npat):
        greet((lax.rem(q + j, npat), v))

    rows = lax.broadcasted_iota(jnp.int32, (N, N), 0)
    cols = lax.broadcasted_iota(jnp.int32, (N, N), 1)
    cell = rows * N + cols
    trow = lax.broadcasted_iota(jnp.int32, (PC, N), 0)
    tcol = lax.broadcasted_iota(jnp.int32, (PC, N), 1)

    @pl.when(jnp.logical_not(has_lo))
    def _():
        sh[0] = jnp.zeros((2, N, N), jnp.float32)

        @pl.loop(0, PC)
        def _(p):
            for s in range(2):
                for h in (xh, dh, wh):
                    h[s, 0, p] = jnp.zeros((N, N), jnp.float32)

    @pl.when(jnp.logical_not(has_hi))
    def _():
        sh[1] = jnp.zeros((2, N, N), jnp.float32)

        @pl.loop(0, PC)
        def _(p):
            for s in range(2):
                for h in (xh, dh, wh):
                    h[s, 1, p] = jnp.zeros((N, N), jnp.float32)

    tile[...] = jnp.zeros((2, PC, N), jnp.float32)
    acc[...] = jnp.zeros((7, N, N), jnp.float32)

    partners = (sizes[0] - 1) + (sizes[1] - 1) + (npat - 1)
    pl.semaphore_wait(
        barrier, partners + has_lo.astype(jnp.int32) + has_hi.astype(jnp.int32)
    )

    def sig_copy(d):
        return pltpu.make_async_remote_copy(
            cond, sh.at[d], sig_s.at[d], sig_r.at[d],
            device_id=(q, v + 1 - 2 * d), device_id_type=MESH,
        )

    def halo_copy(stage, s, d, p):
        plane = 1 - d
        if stage == 0:
            src, dst = warm[s].at[plane, p], xh.at[s, d, p]
        elif stage == 1:
            src, dst = d0.at[s, p, plane], dh.at[s, d, p]
        else:
            src, dst = w0.at[s, p, plane], wh.at[s, d, p]
        return pltpu.make_async_remote_copy(
            src, dst, hs.at[stage, s, d, p], hr.at[stage, s, d, p],
            device_id=(q, v + 1 - 2 * d), device_id_type=MESH,
        )

    def send_halo(stage, s, p):
        @pl.when(has_hi)
        def _():
            halo_copy(stage, s, 0, p).start()

        @pl.when(has_lo)
        def _():
            halo_copy(stage, s, 1, p).start()

    def await_halo(stage, s, p):
        @pl.when(has_lo)
        def _():
            halo_copy(stage, s, 0, p).wait_recv()

        @pl.when(has_hi)
        def _():
            halo_copy(stage, s, 1, p).wait_recv()

    @pl.when(has_hi)
    def _():
        sig_copy(0).start()

    @pl.when(has_lo)
    def _():
        sig_copy(1).start()

    @pl.loop(0, PC)
    def _(p):
        send_halo(0, 0, p)

    @pl.when(has_lo)
    def _():
        sig_copy(0).wait_recv()

    @pl.when(has_hi)
    def _():
        sig_copy(1).wait_recv()

    lo_open = has_lo.astype(jnp.float32)
    hi_open = has_hi.astype(jnp.float32)
    s0, s1 = cond[0], cond[1]
    slo, shi = sh[0, 1], sh[1, 0]
    z_lo = 0.5 * (s0 + slo) * lo_open
    z_mid = 0.5 * (s0 + s1)
    z_hi = 0.5 * (s1 + shi) * hi_open

    def in_plane(s):
        xp = jnp.where(rows < N - 1, 0.5 * (s + up_row(s)), 0.0)
        yp = jnp.where(cols < N - 1, 0.5 * (s + up_col(s)), 0.0)
        return xp, down_row(xp), yp, down_col(yp)

    for plane, (s, below, above) in enumerate(((s0, z_lo, z_mid), (s1, z_mid, z_hi))):
        xp, xm, yp, ym = in_plane(s)
        diag = LEAK + (below + above) + (xp + xm) + (yp + ym)
        inv = 1.0 / diag
        for k, value in ((ZL, below), (ZH, above), (XM, xm), (XP, xp), (YM, ym), (YP, yp)):
            co[k, plane] = value * inv
        co[DG, plane] = diag
        co[DI, plane] = inv
    for d, (s, near, far) in enumerate(((slo, z_lo, sh[0, 0]), (shi, z_hi, sh[1, 1]))):
        xp, xm, yp, ym = in_plane(s)
        dih[d] = 1.0 / (LEAK + (near + 0.5 * (s + far)) + (xp + xm) + (yp + ym))

    def apply(a, b, lo, hi):
        out = []
        for plane, (x, below, above) in enumerate(((a, lo, b), (b, a, hi))):
            y = co[ZL, plane] * below + co[ZH, plane] * above
            y = y + co[XM, plane] * down_row(x) + co[XP, plane] * up_row(x)
            y = y + co[YM, plane] * down_col(x) + co[YP, plane] * up_col(x)
            out.append(x - y)
        return out

    def voxel(p, which):
        return elec[pats[p, which]]

    def difference(p, first, second, plane, scale):
        here = (2 * v + plane) * PLANE
        plus = jnp.where(cell == voxel(p, first) - here, scale, 0.0)
        return plus - jnp.where(cell == voxel(p, second) - here, scale, 0.0)

    def record(r, p, values):
        now = tile[r]
        for k, value in values:
            now = jnp.where((trow == p) & (tcol == k), value, now)
        tile[r] = now

    def first(s):
        @pl.loop(0, PC)
        def _(p):
            await_halo(0, s, p)
            a, b = warm[s][0, p], warm[s][1, p]
            y0, y1 = apply(a, b, xh[s, 0, p], xh[s, 1, p])
            if s == 0:
                e0 = difference(p, 0, 1, 0, strength) * co[DI, 0] - y0
                e1 = difference(p, 0, 1, 1, strength) * co[DI, 1] - y1
            else:
                e0, e1 = -y0, -y1
            d0[s, p, 0] = e0
            d0[s, p, 1] = e1
            send_halo(1, s, p)
            if s == 0:
                send_halo(0, 1, p)
                g0 = difference(p, 2, 3, 0, 1.0)
                g1 = difference(p, 2, 3, 1, 1.0)
                record(0, p, (
                    (0, total(co[DG, 0] * e0 * e0 + co[DG, 1] * e1 * e1)),
                    (4, total(g0 * a + g1 * b)),
                    (5, total(g0 * e0 + g1 * e1)),
                ))

    def second(s):
        @pl.loop(0, PC)
        def _(p):
            await_halo(1, s, p)
            a, b, lo, hi = d0[s, p, 0], d0[s, p, 1], dh[s, 0, p], dh[s, 1, p]
            if s == 1:
                weight = kc[2, pl.ds(p, 1), :]
                a = a + weight * (difference(p, 2, 3, 0, 1.0) * co[DI, 0])
                b = b + weight * (difference(p, 2, 3, 1, 1.0) * co[DI, 1])
                lo = lo + weight * (difference(p, 2, 3, -1, 1.0) * dih[0])
                hi = hi + weight * (difference(p, 2, 3, 2, 1.0) * dih[1])
                dc[p, 0] = a
                dc[p, 1] = b
                dh[s, 0, p] = lo
                dh[s, 1, p] = hi
            y0, y1 = apply(a, b, lo, hi)
            w0[s, p, 0] = y0
            w0[s, p, 1] = y1
            send_halo(2, s, p)
            u0, u1 = co[DG, 0] * y0, co[DG, 1] * y1
            values = [(1, total(u0 * a + u1 * b)), (2, total(u0 * y0 + u1 * y1))]
            if s == 0:
                g0 = difference(p, 2, 3, 0, 1.0)
                g1 = difference(p, 2, 3, 1, 1.0)
                values.append((6, total(g0 * y0 + g1 * y1)))
            else:
                values.append((0, total(co[DG, 0] * a * a + co[DG, 1] * b * b)))
            record(s, p, values)

    def third(s):
        @pl.loop(0, PC)
        def _(p):
            await_halo(2, s, p)
            a, b = w0[s, p, 0], w0[s, p, 1]
            y0, y1 = apply(a, b, wh[s, 0, p], wh[s, 1, p])
            record(s, p, ((3, total(co[DG, 0] * a * y0 + co[DG, 1] * b * y1)),))

    def sum_copy(r, stage, k, slot):
        return pltpu.make_async_remote_copy(
            red.at[r, stage, slot], red.at[r, stage, slot],
            red_s.at[r, stage, k], red_r.at[r, stage, slot],
            device_id=(q, member(stage, k)), device_id_type=MESH,
        )

    def sum_over_vox(r):
        value = tile[r]
        for stage in range(2):
            mine, size = rank[stage], sizes[stage]
            red[r, stage, mine] = value
            for j in range(1, size):
                sum_copy(r, stage, lax.rem(mine + j, size), mine).start()
            for j in range(1, size):
                k = lax.rem(mine + j, size)
                sum_copy(r, stage, k, k).wait_recv()
            value = red[r, stage, 0]
            for k in range(1, size):
                value = value + red[r, stage, k]
        return value

    def column(value, k):
        return jnp.sum(jnp.where(tcol == k, value, 0.0), axis=1, keepdims=True)

    def steps(value):
        rho, mu, nu, xi = (column(value, k) for k in range(4))
        alpha = rho / mu
        rho1 = rho - 2.0 * alpha * mu + alpha * alpha * nu
        beta1 = 1.0 + rho1 / rho
        curve = beta1 * beta1 * mu - 2.0 * alpha * beta1 * nu + alpha * alpha * xi
        alpha1 = rho1 / curve
        return alpha + alpha1 * beta1, -alpha * alpha1

    first(0)
    second(0)
    first(1)
    third(0)
    value = sum_over_vox(0)
    c1, c2 = steps(value)
    predicted = column(value, 4) + c1 * column(value, 5) + c2 * column(value, 6)
    observed = jnp.zeros((PC, 1), jnp.float32)
    for p in range(PC):
        observed = jnp.where(trow[:, 0:1] == p, obs[p], observed)
    kc[0] = jnp.broadcast_to(c1, (PC, N))
    kc[1] = jnp.broadcast_to(c2, (PC, N))
    kc[2] = jnp.broadcast_to(data_weight * (predicted - observed), (PC, N))
    pred_out[...] = jnp.broadcast_to(predicted, (PC, N))
    second(1)
    third(1)
    value = sum_over_vox(1)
    c1, c2 = steps(value)
    kc[3] = jnp.broadcast_to(c1, (PC, N))
    kc[4] = jnp.broadcast_to(c2, (PC, N))

    @pl.loop(0, PC)
    def _(p):
        fields = []
        for s, (own_d, k1, k2) in enumerate((
            ([d0.at[0, p, 0], d0.at[0, p, 1]], 0, 1),
            ([dc.at[p, 0], dc.at[p, 1]], 3, 4),
        )):
            m1, m2 = kc[k1, pl.ds(p, 1), :], kc[k2, pl.ds(p, 1), :]
            fields.append((
                xh[s, 0, p] + m1 * dh[s, 0, p] + m2 * wh[s, 0, p],
                warm[s][0, p] + m1 * own_d[0][...] + m2 * w0[s, p, 0],
                warm[s][1, p] + m1 * own_d[1][...] + m2 * w0[s, p, 1],
                xh[s, 1, p] + m1 * dh[s, 1, p] + m2 * wh[s, 1, p],
            ))
        f, a = fields
        for k in range(3):
            acc[k] += (f[k + 1] - f[k]) * (a[k + 1] - a[k])
        for k in range(2):
            x, y = f[k + 1], a[k + 1]
            acc[3 + k] += (up_row(x) - x) * (up_row(y) - y)
            acc[5 + k] += (up_col(x) - x) * (up_col(y) - y)

    for plane in range(2):
        lo, hi = acc[plane], acc[plane + 1]
        lo = lo * lo_open if plane == 0 else lo
        hi = hi * hi_open if plane == 1 else hi
        px = jnp.where(rows < N - 1, acc[3 + plane], 0.0)
        py = jnp.where(cols < N - 1, acc[5 + plane], 0.0)
        gb[plane] = -0.5 * ((lo + hi) + (px + down_row(px)) + (py + down_col(py)))

    def part(k):
        return pl.ds(pl.multiple_of(k * chunk, chunk), chunk)

    def rs_copy(k, slot):
        return pltpu.make_async_remote_copy(
            gb.at[:, part(k), :], rsb.at[slot], rs_s.at[k], rs_r.at[slot],
            device_id=(k, v), device_id_type=MESH,
        )

    def ag_copy(k, slot):
        return pltpu.make_async_remote_copy(
            agb.at[:, part(slot), :], agb.at[:, part(slot), :], ag_s.at[k], ag_r.at[slot],
            device_id=(k, v), device_id_type=MESH,
        )

    others = [lax.rem(q + j, npat) for j in range(1, npat)]
    for k in others:
        rs_copy(k, q).start()
    rsb[q] = gb[:, part(q), :]
    for k in others:
        rs_copy(k, k).wait_recv()
    whole = rsb[0]
    for k in range(1, npat):
        whole = whole + rsb[k]
    agb[:, part(q), :] = whole
    for k in others:
        ag_copy(k, q).start()
    for k in others:
        ag_copy(k, k).wait_recv()
    grad_out[...] = agb[...]

    @pl.when(has_hi)
    def _():
        sig_copy(0).wait_send()

    @pl.when(has_lo)
    def _():
        sig_copy(1).wait_send()

    @pl.loop(0, PC)
    def _(p):
        for stage in range(3):
            for s in range(2):
                @pl.when(has_hi)
                def _():
                    halo_copy(stage, s, 0, p).wait_send()

                @pl.when(has_lo)
                def _():
                    halo_copy(stage, s, 1, p).wait_send()

    for r in range(2):
        for stage in range(2):
            for j in range(1, sizes[stage]):
                sum_copy(r, stage, lax.rem(rank[stage] + j, sizes[stage]), rank[stage]).wait_send()
    for k in others:
        rs_copy(k, q).wait_send()
        ag_copy(k, q).wait_send()


def solution(mesh):
    npat, layers = mesh.shape["pat"], mesh.shape["vox"]
    group = 8 if layers >= 64 else 2

    def per_device(conductivity, warm_forward, warm_adjoint, electrodes, patterns, observed):
        planes = conductivity.shape[0]
        strength = 2.0 * math.sqrt(layers * planes * PLANE)
        vmem = pl.BlockSpec(memory_space=pltpu.VMEM)
        smem = pl.BlockSpec(memory_space=pltpu.SMEM)
        f32 = jnp.float32
        dma = pltpu.SemaphoreType.DMA
        groups = layers // group
        widest = max(group, groups)
        gradient, predicted = pl.pallas_call(
            functools.partial(kernel, npat, layers, group, strength),
            out_shape=(
                jax.ShapeDtypeStruct((2, N, N), f32),
                jax.ShapeDtypeStruct((PC, N), f32),
            ),
            in_specs=[vmem, vmem, vmem, smem, smem, smem],
            out_specs=(vmem, vmem),
            scratch_shapes=[
                pltpu.VMEM((2, 2, N, N), f32),
                pltpu.VMEM((2, 2, PC, N, N), f32),
                pltpu.VMEM((2, 2, PC, N, N), f32),
                pltpu.VMEM((2, 2, PC, N, N), f32),
                pltpu.VMEM((2, PC, 2, N, N), f32),
                pltpu.VMEM((2, PC, 2, N, N), f32),
                pltpu.VMEM((PC, 2, N, N), f32),
                pltpu.VMEM((8, 2, N, N), f32),
                pltpu.VMEM((2, N, N), f32),
                pltpu.VMEM((7, N, N), f32),
                pltpu.VMEM((2, PC, N), f32),
                pltpu.VMEM((2, 2, widest, PC, N), f32),
                pltpu.VMEM((5, PC, N), f32),
                pltpu.VMEM((2, N, N), f32),
                pltpu.VMEM((npat, 2, N // npat, N), f32),
                pltpu.VMEM((2, N, N), f32),
                dma((2,)),
                dma((2,)),
                dma((3, 2, 2, PC)),
                dma((3, 2, 2, PC)),
                dma((2, 2, widest)),
                dma((2, 2, widest)),
                dma((npat,)),
                dma((npat,)),
                dma((npat,)),
                dma((npat,)),
            ],
            compiler_params=pltpu.CompilerParams(
                collective_id=0, has_side_effects=True, vmem_limit_bytes=48 * 2**20
            ),
            name="ert_gradient",
        )(conductivity, warm_forward, warm_adjoint, electrodes, patterns, observed)
        return gradient, predicted[:, 0]

    in_specs = (
        P("vox", None, None),
        P("vox", "pat", None, None),
        P("vox", "pat", None, None),
        P(),
        P("pat", None),
        P("pat"),
    )
    return jax.shard_map(
        per_device,
        mesh=mesh,
        in_specs=in_specs,
        out_specs=(P("vox", None, None), P("pat")),
        check_vma=False,
    )
```

```python
import functools
import math

import jax
import jax.numpy as jnp
from jax import lax
from jax.experimental import pallas as pl
from jax.experimental.pallas import tpu as pltpu
from jax.sharding import PartitionSpec as P

MESH = pl.DeviceIdType.MESH
LEAK = 0.05
N = 128
PLANE = N * N
PC = 8

ZL, ZH, XM, XP, YM, YP = range(6)
F_RHO, F_MU, F_NU, F_XI, F_X, F_D, F_W = range(7)
YY, GY, GG = 7, 11, 15


def up_row(x):
    return pltpu.roll(x, N - 1, 0)


def down_row(x):
    return pltpu.roll(x, 1, 0)


def up_col(x):
    return pltpu.roll(x, N - 1, 1)


def down_col(x):
    return pltpu.roll(x, 1, 1)


def total(x):
    part = jnp.sum(x.reshape(N // 8, 8, N), axis=0)
    return jnp.sum(jnp.sum(part, axis=1, keepdims=True), axis=0, keepdims=True)


def kernel(
    npat,
    layers,
    group,
    strength,
    cond_in,
    wf_in,
    wa_in,
    elec,
    pats,
    obs,
    grad_out,
    pred_out,
    cond,
    warm,
    sh,
    fh,
    xh,
    dh,
    wh,
    d0,
    w0,
    gd,
    gw,
    rb,
    co,
    dg,
    di,
    acc,
    tile,
    red,
    kc,
    gb,
    rsb,
    agb,
    in_s,
    sig_s,
    sig_r,
    hs,
    hr,
    rr,
    rq,
    red_s,
    red_r,
    rs_s,
    rs_r,
    ag_s,
    ag_r,
):
    q = lax.axis_index("pat")
    v = lax.axis_index("vox")
    last = layers - 1
    has_lo = v > 0
    has_hi = v < last
    groups = layers // group
    rank = (lax.rem(v, group), v // group)
    sizes = (group, groups)
    data_weight = 0.1 * strength
    chunk = N // npat
    lower, upper = layers // 2 - 1, layers // 2
    inner = (q >= npat // 2 - 1) & (q <= npat // 2) if npat > 2 else q == 0
    crossing = ((lower, upper, 0), (upper, lower, last))

    local = [
        pltpu.make_async_copy(cond_in, cond, in_s.at[0]),
        pltpu.make_async_copy(wf_in, warm.at[0], in_s.at[1]),
        pltpu.make_async_copy(wa_in, warm.at[1], in_s.at[2]),
    ]

    def member(stage, k):
        return (v // group) * group + k if stage == 0 else k * group + lax.rem(v, group)

    barrier = pltpu.get_barrier_semaphore()

    def greet(device):
        pl.semaphore_signal(barrier, inc=1, device_id=device, device_id_type=MESH)

    @pl.when(has_lo)
    def _():
        greet((q, v - 1))

    @pl.when(has_hi)
    def _():
        greet((q, v + 1))

    expected = has_lo.astype(jnp.int32) + has_hi.astype(jnp.int32)
    for source, target, via in crossing:
        on_path = inner & ((v == source) | (v == target))

        @pl.when(on_path)
        def _():
            greet((q, via))

        @pl.when(inner & (v == via))
        def _():
            greet((q, source))
            greet((q, target))

        expected = expected + on_path.astype(jnp.int32)
        expected = expected + 2 * (inner & (v == via)).astype(jnp.int32)

    for stage in range(2):
        for j in range(1, sizes[stage]):
            greet((q, member(stage, lax.rem(rank[stage] + j, sizes[stage]))))
    for j in range(1, npat):
        greet((lax.rem(q + j, npat), v))

    for copy in local:
        copy.start()

    rows = lax.broadcasted_iota(jnp.int32, (N, N), 0)
    cols = lax.broadcasted_iota(jnp.int32, (N, N), 1)
    cell = rows * N + cols
    trow = lax.broadcasted_iota(jnp.int32, (PC, N), 0)
    tcol = lax.broadcasted_iota(jnp.int32, (PC, N), 1)
    blank = jnp.zeros((N, N), jnp.float32)

    for d, outside in enumerate((jnp.logical_not(has_lo), jnp.logical_not(has_hi))):
        @pl.when(outside)
        def _():
            sh[d, 0] = blank
            sh[d, 1] = blank
            fh[d] = blank

            @pl.loop(0, PC)
            def _(p):
                for s in range(2):
                    for h in (xh, dh, wh):
                        h[s, d, p] = blank

    tile[...] = jnp.zeros((PC, N), jnp.float32)
    for k in range(7):
        acc[k] = blank

    def neighbour(d):
        return (q, v + 1 - 2 * d)

    def sig_copy(kind, d):
        plane = (1 - d, d)[kind] if kind < 2 else None
        src = di.at[2 + d] if kind == 2 else cond.at[plane]
        dst = fh.at[d] if kind == 2 else sh.at[d, plane]
        return pltpu.make_async_remote_copy(
            src, dst, sig_s.at[kind, d], sig_r.at[kind, d],
            device_id=neighbour(d), device_id_type=MESH,
        )

    def outgoing(stage, s, d, p):
        plane = 1 - d
        if stage == 0:
            return warm.at[s, plane, p]
        return (d0 if stage == 1 else w0).at[s, p, plane]

    def incoming(stage, s, d, p):
        return (xh, dh, wh)[stage].at[s, d, p]

    def halo_copy(stage, s, d, p):
        return pltpu.make_async_remote_copy(
            outgoing(stage, s, d, p), incoming(stage, s, d, p),
            hs.at[stage, s, d, p], hr.at[stage, s, d, p],
            device_id=neighbour(d), device_id_type=MESH,
        )

    def detour_in(stage, s, d, p):
        at = s * (PC // 2) + p // 2
        return pltpu.make_async_remote_copy(
            outgoing(stage, s, d, p), rb.at[stage, at],
            hs.at[stage, s, d, p], rr.at[stage, at],
            device_id=(q, crossing[d][2]), device_id_type=MESH,
        )

    def detour_out(stage, s, d, p):
        at = s * (PC // 2) + p // 2
        return pltpu.make_async_remote_copy(
            rb.at[stage, at], incoming(stage, s, d, p),
            rq.at[stage, at], hr.at[stage, s, d, p],
            device_id=(q, crossing[d][1]), device_id_type=MESH,
        )

    exists = (has_hi, has_lo)

    def both(fn):
        for d in range(2):
            @pl.when(exists[d])
            def _():
                fn(d)

    def both_in(fn):
        for d in range(2):
            @pl.when(exists[1 - d])
            def _():
                fn(d)

    def send_halo(stage, s, p):
        odd = lax.rem(p, 2) == 1
        for d in range(2):
            around = inner & (v == crossing[d][0]) & odd

            @pl.when(exists[d] & jnp.logical_not(around))
            def _():
                halo_copy(stage, s, d, p).start()

            @pl.when(around)
            def _():
                detour_in(stage, s, d, p).start()

    def pass_on(stage, s, p):
        odd = lax.rem(p, 2) == 1
        for d in range(2):
            @pl.when(inner & (v == crossing[d][2]) & odd)
            def _():
                detour_in(stage, s, d, p).wait_recv()
                detour_out(stage, s, d, p).start()

    def await_halo(stage, s, p):
        both_in(lambda d: halo_copy(stage, s, d, p).wait_recv())

    for copy in local:
        copy.wait()
    partners = (sizes[0] - 1) + (sizes[1] - 1) + (npat - 1)
    pl.semaphore_wait(barrier, partners + expected)

    both(lambda d: sig_copy(0, d).start())
    for s in range(2):
        @pl.loop(0, PC)
        def _(p):
            send_halo(0, s, p)
    both(lambda d: sig_copy(1, d).start())

    lo_open = has_lo.astype(jnp.float32)
    hi_open = has_hi.astype(jnp.float32)

    def couple(k, s, below, above):
        xp = jnp.where(rows < N - 1, 0.5 * (s + up_row(s)), 0.0)
        yp = jnp.where(cols < N - 1, 0.5 * (s + up_col(s)), 0.0)
        xm, ym = down_row(xp), down_col(yp)
        diag = LEAK + (below + above) + (xp + xm) + (yp + ym)
        inv = 1.0 / diag
        for at, value in ((ZL, below), (ZH, above), (XM, xm), (XP, xp), (YM, ym), (YP, yp)):
            co[at, k] = value * inv
        if k in (1, 2):
            dg[k - 1] = diag
        di[k + 1] = inv

    both_in(lambda d: sig_copy(0, d).wait_recv())
    couple(1, cond[0], 0.5 * (cond[0] + sh[0, 1]) * lo_open, 0.5 * (cond[0] + cond[1]))
    couple(2, cond[1], 0.5 * (cond[0] + cond[1]), 0.5 * (cond[1] + sh[1, 0]) * hi_open)
    both(lambda d: sig_copy(2, d).start())

    def apply(k, x, below, above):
        y = co[ZL, k] * below + co[ZH, k] * above
        y = y + co[XM, k] * down_row(x) + co[XP, k] * up_row(x)
        y = y + co[YM, k] * down_col(x) + co[YP, k] * up_col(x)
        return x - y

    def difference(p, first, second, plane, scale):
        here = (2 * v + plane) * PLANE
        plus = jnp.where(cell == elec[pats[first, p]] - here, scale, 0.0)
        return plus - jnp.where(cell == elec[pats[second, p]] - here, scale, 0.0)

    def probe(p, plane):
        return difference(p, 2, 3, plane, 1.0)

    def record(p, values):
        now = tile[...]
        for k, value in values:
            now = jnp.where((trow == p) & (tcol == k), value, now)
        tile[...] = now

    for s in range(2):
        @pl.loop(0, PC)
        def _(p):
            await_halo(0, s, p)
            a, b = warm[s, 0, p], warm[s, 1, p]
            e0 = -apply(1, a, xh[s, 0, p], b)
            e1 = -apply(2, b, a, xh[s, 1, p])
            if s == 0:
                e0 = e0 + difference(p, 0, 1, 0, strength) * di[2]
                e1 = e1 + difference(p, 0, 1, 1, strength) * di[3]
            d0[s, p, 0] = e0
            d0[s, p, 1] = e1
            send_halo(1, s, p)
            g0, g1 = probe(p, 0), probe(p, 1)
            rho = total(dg[0] * e0 * e0 + dg[1] * e1 * e1)
            ge = total(g0 * e0 + g1 * e1)
            if s == 0:
                record(p, ((F_RHO, rho), (F_D, ge), (F_X, total(g0 * a + g1 * b))))
            else:
                record(p, ((YY, rho), (GY, ge)))
            pass_on(0, s, p)

    both_in(lambda d: sig_copy(1, d).wait_recv())
    couple(0, sh[0, 1], 0.5 * (sh[0, 0] + sh[0, 1]), 0.5 * (cond[0] + sh[0, 1]) * lo_open)
    couple(3, sh[1, 0], 0.5 * (cond[1] + sh[1, 0]) * hi_open, 0.5 * (sh[1, 0] + sh[1, 1]))
    both_in(lambda d: sig_copy(2, d).wait_recv())
    di[0] = fh[0]
    di[5] = fh[1]

    @pl.loop(0, PC)
    def _(p):
        e = [probe(p, k - 2) * di[k] for k in range(6)]
        y = [apply(k, e[k + 1], e[k], e[k + 2]) for k in range(4)]
        for k in range(4):
            gd[p, k] = e[k + 1]
            gw[p, k] = y[k]
        z0, z1 = apply(1, y[1], y[0], y[2]), apply(2, y[2], y[1], y[3])
        g0, g1 = probe(p, 0), probe(p, 1)
        u0, u1 = dg[0] * y[1], dg[1] * y[2]
        record(p, (
            (GG, total(g0 * e[2] + g1 * e[3])),
            (GG + 1, total(g0 * y[1] + g1 * y[2])),
            (GG + 2, total(u0 * y[1] + u1 * y[2])),
            (GG + 3, total(u0 * z0 + u1 * z1)),
        ))

    for s in range(2):
        @pl.loop(0, PC)
        def _(p):
            await_halo(1, s, p)
            a, b = d0[s, p, 0], d0[s, p, 1]
            y0 = apply(1, a, dh[s, 0, p], b)
            y1 = apply(2, b, a, dh[s, 1, p])
            w0[s, p, 0] = y0
            w0[s, p, 1] = y1
            send_halo(2, s, p)
            u0, u1 = dg[0] * y0, dg[1] * y1
            mu = total(u0 * a + u1 * b)
            nu = total(u0 * y0 + u1 * y1)
            gy = total(probe(p, 0) * y0 + probe(p, 1) * y1)
            if s == 0:
                record(p, ((F_MU, mu), (F_NU, nu), (F_W, gy)))
            else:
                cross = total(u0 * gw[p, 1] + u1 * gw[p, 2])
                record(p, ((YY + 1, mu), (YY + 2, nu), (GY + 1, gy), (GY + 2, cross)))
            pass_on(1, s, p)

    for s in range(2):
        @pl.loop(0, PC)
        def _(p):
            pass_on(2, s, p)
            await_halo(2, s, p)
            a, b = w0[s, p, 0], w0[s, p, 1]
            u0 = dg[0] * apply(1, a, wh[s, 0, p], b)
            u1 = dg[1] * apply(2, b, a, wh[s, 1, p])
            xi = total(a * u0 + b * u1)
            if s == 0:
                record(p, ((F_XI, xi),))
            else:
                cross = total(u0 * gw[p, 1] + u1 * gw[p, 2])
                record(p, ((YY + 3, xi), (GY + 3, cross)))

    def sum_copy(stage, k, slot):
        return pltpu.make_async_remote_copy(
            red.at[stage, slot], red.at[stage, slot],
            red_s.at[stage, k], red_r.at[stage, slot],
            device_id=(q, member(stage, k)), device_id_type=MESH,
        )

    value = tile[...]
    for stage in range(2):
        mine, size = rank[stage], sizes[stage]
        red[stage, mine] = value
        for j in range(1, size):
            sum_copy(stage, lax.rem(mine + j, size), mine).start()
        for j in range(1, size):
            k = lax.rem(mine + j, size)
            sum_copy(stage, k, k).wait_recv()
        value = red[stage, 0]
        for k in range(1, size):
            value = value + red[stage, k]

    def column(k):
        return jnp.sum(jnp.where(tcol == k, value, 0.0), axis=1, keepdims=True)

    def steps(rho, mu, nu, xi):
        alpha = rho / mu
        rho1 = rho - 2.0 * alpha * mu + alpha * alpha * nu
        beta1 = 1.0 + rho1 / rho
        curve = beta1 * beta1 * mu - 2.0 * alpha * beta1 * nu + alpha * alpha * xi
        alpha1 = rho1 / curve
        return alpha + alpha1 * beta1, -alpha * alpha1

    c1, c2 = steps(column(F_RHO), column(F_MU), column(F_NU), column(F_XI))
    predicted = column(F_X) + c1 * column(F_D) + c2 * column(F_W)
    observed = jnp.zeros((PC, 1), jnp.float32)
    for p in range(PC):
        observed = jnp.where(trow[:, 0:1] == p, obs[p], observed)
    weight = data_weight * (predicted - observed)
    e1, e2 = steps(*(
        column(YY + k) + weight * (2.0 * column(GY + k) + weight * column(GG + k))
        for k in range(4)
    ))
    for k, factor in enumerate((c1, c2, e1, e2, e1 * weight, e2 * weight)):
        kc[k] = jnp.broadcast_to(factor, (PC, N))
    wide = jnp.where(trow == tcol, predicted, 0.0)
    pred_out[...] = jnp.sum(wide, axis=0, keepdims=True)[:, :PC]

    @pl.loop(0, PC)
    def _(p):
        m = [kc[k, pl.ds(p, 1), :] for k in range(6)]

        def field(s, k):
            if k in (0, 3):
                x, d, w = (h[s, k // 3, p] for h in (xh, dh, wh))
            else:
                x, d, w = warm[s, k - 1, p], d0[s, p, k - 1], w0[s, p, k - 1]
            out = x + m[2 * s] * d + m[2 * s + 1] * w
            if s == 1:
                out = out + m[4] * gd[p, k] + m[5] * gw[p, k]
            return out

        f = [field(0, k) for k in range(4)]
        a = [field(1, k) for k in range(4)]
        for k in range(3):
            acc[k] += (f[k + 1] - f[k]) * (a[k + 1] - a[k])
        for k in range(2):
            x, y = f[k + 1], a[k + 1]
            acc[3 + k] += (up_row(x) - x) * (up_row(y) - y)
            acc[5 + k] += (up_col(x) - x) * (up_col(y) - y)

    for plane in range(2):
        lo, hi = acc[plane], acc[plane + 1]
        lo = lo * lo_open if plane == 0 else lo
        hi = hi * hi_open if plane == 1 else hi
        px = jnp.where(rows < N - 1, acc[3 + plane], 0.0)
        py = jnp.where(cols < N - 1, acc[5 + plane], 0.0)
        gb[plane] = -0.5 * ((lo + hi) + (px + down_row(px)) + (py + down_col(py)))

    def part(k):
        return pl.ds(pl.multiple_of(k * chunk, chunk), chunk)

    def rs_copy(k, slot):
        return pltpu.make_async_remote_copy(
            gb.at[:, part(k), :], rsb.at[slot], rs_s.at[k], rs_r.at[slot],
            device_id=(k, v), device_id_type=MESH,
        )

    def ag_copy(k, slot):
        return pltpu.make_async_remote_copy(
            agb.at[:, part(slot), :], agb.at[:, part(slot), :], ag_s.at[k], ag_r.at[slot],
            device_id=(k, v), device_id_type=MESH,
        )

    others = [lax.rem(q + j, npat) for j in range(1, npat)]
    for k in others:
        rs_copy(k, q).start()
    rsb[q] = gb[:, part(q), :]
    for k in others:
        rs_copy(k, k).wait_recv()
    whole = rsb[0]
    for k in range(1, npat):
        whole = whole + rsb[k]
    agb[:, part(q), :] = whole
    for k in others:
        ag_copy(k, q).start()
    for k in others:
        ag_copy(k, k).wait_recv()
    grad_out[...] = agb[...]

    for kind in range(3):
        both(lambda d: sig_copy(kind, d).wait_send())

    @pl.loop(0, PC)
    def _(p):
        for stage in range(3):
            for s in range(2):
                both(lambda d: halo_copy(stage, s, d, p).wait_send())
                for d in range(2):
                    @pl.when(inner & (v == crossing[d][2]) & (lax.rem(p, 2) == 1))
                    def _():
                        detour_out(stage, s, d, p).wait_send()

    for stage in range(2):
        for j in range(1, sizes[stage]):
            sum_copy(stage, lax.rem(rank[stage] + j, sizes[stage]), rank[stage]).wait_send()
    for k in others:
        rs_copy(k, q).wait_send()
        ag_copy(k, q).wait_send()


def solution(mesh):
    npat, layers = mesh.shape["pat"], mesh.shape["vox"]
    group = 8 if layers >= 64 else 2

    def per_device(conductivity, warm_forward, warm_adjoint, electrodes, patterns, observed):
        planes = conductivity.shape[0]
        strength = 2.0 * math.sqrt(layers * planes * PLANE)
        vmem = pl.BlockSpec(memory_space=pltpu.VMEM)
        smem = pl.BlockSpec(memory_space=pltpu.SMEM)
        hbm = pl.BlockSpec(memory_space=pltpu.HBM)
        f32 = jnp.float32
        dma = pltpu.SemaphoreType.DMA
        groups = layers // group
        widest = max(group, groups)
        gradient, predicted = pl.pallas_call(
            functools.partial(kernel, npat, layers, group, strength),
            out_shape=(
                jax.ShapeDtypeStruct((2, N, N), f32),
                jax.ShapeDtypeStruct((1, PC), f32),
            ),
            in_specs=[hbm, hbm, hbm, smem, smem, smem],
            out_specs=(vmem, vmem),
            scratch_shapes=[
                pltpu.VMEM((2, N, N), f32),
                pltpu.VMEM((2, 2, PC, N, N), f32),
                pltpu.VMEM((2, 2, N, N), f32),
                pltpu.VMEM((2, N, N), f32),
                pltpu.VMEM((2, 2, PC, N, N), f32),
                pltpu.VMEM((2, 2, PC, N, N), f32),
                pltpu.VMEM((2, 2, PC, N, N), f32),
                pltpu.VMEM((2, PC, 2, N, N), f32),
                pltpu.VMEM((2, PC, 2, N, N), f32),
                pltpu.VMEM((PC, 4, N, N), f32),
                pltpu.VMEM((PC, 4, N, N), f32),
                pltpu.VMEM((3, PC, N, N), f32),
                pltpu.VMEM((6, 4, N, N), f32),
                pltpu.VMEM((2, N, N), f32),
                pltpu.VMEM((6, N, N), f32),
                pltpu.VMEM((7, N, N), f32),
                pltpu.VMEM((PC, N), f32),
                pltpu.VMEM((2, widest, PC, N), f32),
                pltpu.VMEM((6, PC, N), f32),
                pltpu.VMEM((2, N, N), f32),
                pltpu.VMEM((npat, 2, N // npat, N), f32),
                pltpu.VMEM((2, N, N), f32),
                dma((3,)),
                dma((3, 2)),
                dma((3, 2)),
                dma((3, 2, 2, PC)),
                dma((3, 2, 2, PC)),
                dma((3, PC)),
                dma((3, PC)),
                dma((2, widest)),
                dma((2, widest)),
                dma((npat,)),
                dma((npat,)),
                dma((npat,)),
                dma((npat,)),
            ],
            compiler_params=pltpu.CompilerParams(
                collective_id=0, has_side_effects=True, vmem_limit_bytes=58 * 2**20
            ),
            name="ert_gradient",
        )(conductivity, warm_forward, warm_adjoint, electrodes, patterns.T, observed)
        return gradient, predicted.reshape(PC)

    in_specs = (
        P("vox", None, None),
        P("vox", "pat", None, None),
        P("vox", "pat", None, None),
        P(),
        P("pat", None),
        P("pat"),
    )
    return jax.shard_map(
        per_device,
        mesh=mesh,
        in_specs=in_specs,
        out_specs=(P("vox", None, None), P("pat")),
        check_vma=False,
    )
```

```python
import functools
import math

import jax
import jax.numpy as jnp
from jax import lax
from jax.experimental import pallas as pl
from jax.experimental.pallas import tpu as pltpu
from jax.sharding import PartitionSpec as P

MESH = pl.DeviceIdType.MESH
LEAK = 0.05
N = 128
PLANE = N * N
PC = 8
PIECES = 8

ZL, ZH, XM, XP, YM, YP = range(6)
F_RHO, F_MU, F_NU, F_XI, F_X, F_D, F_W = range(7)
YY, GY, GG = 7, 11, 15


def up_row(x):
    return pltpu.roll(x, N - 1, 0)


def down_row(x):
    return pltpu.roll(x, 1, 0)


def up_col(x):
    return pltpu.roll(x, N - 1, 1)


def down_col(x):
    return pltpu.roll(x, 1, 1)


def total(x):
    part = jnp.sum(x.reshape(N // 8, 8, N), axis=0)
    return jnp.sum(jnp.sum(part, axis=1, keepdims=True), axis=0, keepdims=True)


def kernel(
    npat,
    layers,
    group,
    strength,
    cond_in,
    wf_in,
    wa_in,
    elec,
    pats,
    obs,
    grad_out,
    pred_out,
    cond,
    warm,
    sh,
    fh,
    xh,
    dh,
    wh,
    d0,
    w0,
    gd,
    gw,
    rb,
    co,
    dg,
    di,
    acc,
    tile,
    red,
    kc,
    gb,
    lb_outer,
    lb_inner,
    half,
    grad,
    in_s,
    sig_s,
    sig_r,
    hs,
    hr,
    rr,
    rq,
    red_s,
    red_r,
    ls,
    lr,
):
    lb = (lb_outer, lb_inner)
    q = lax.axis_index("pat")
    v = lax.axis_index("vox")
    last = layers - 1
    has_lo = v > 0
    has_hi = v < last
    groups = layers // group
    rank = (lax.rem(v, group), v // group)
    sizes = (group, groups)
    data_weight = 0.1 * strength
    lower, upper = layers // 2 - 1, layers // 2
    middle = npat // 2
    inner = (q >= middle - 1) & (q <= middle) if npat > 2 else q == 0
    crossing = (
        (lower, upper, 0, inner),
        (upper, lower, last, jnp.logical_not(inner)),
    )

    local = [
        pltpu.make_async_copy(cond_in, cond, in_s.at[0]),
        pltpu.make_async_copy(wf_in, warm.at[0], in_s.at[1]),
        pltpu.make_async_copy(wa_in, warm.at[1], in_s.at[2]),
    ]

    def member(stage, k):
        return (v // group) * group + k if stage == 0 else k * group + lax.rem(v, group)

    barrier = pltpu.get_barrier_semaphore()

    def greet(device):
        pl.semaphore_signal(barrier, inc=1, device_id=device, device_id_type=MESH)

    @pl.when(has_lo)
    def _():
        greet((q, v - 1))

    @pl.when(has_hi)
    def _():
        greet((q, v + 1))

    expected = has_lo.astype(jnp.int32) + has_hi.astype(jnp.int32)
    for source, target, via, taken in crossing:
        on_path = taken & ((v == source) | (v == target))

        @pl.when(on_path)
        def _():
            greet((q, via))

        @pl.when(taken & (v == via))
        def _():
            greet((q, source))
            greet((q, target))

        expected = expected + on_path.astype(jnp.int32)
        expected = expected + 2 * (taken & (v == via)).astype(jnp.int32)

    for stage in range(2):
        for j in range(1, sizes[stage]):
            greet((q, member(stage, lax.rem(rank[stage] + j, sizes[stage]))))
    below, above = q > 0, q < npat - 1

    @pl.when(below)
    def _():
        greet((q - 1, v))

    @pl.when(above)
    def _():
        greet((q + 1, v))

    expected = expected + below.astype(jnp.int32) + above.astype(jnp.int32)
    for copy in local:
        copy.start()

    rows = lax.broadcasted_iota(jnp.int32, (N, N), 0)
    cols = lax.broadcasted_iota(jnp.int32, (N, N), 1)
    cell = rows * N + cols
    trow = lax.broadcasted_iota(jnp.int32, (PC, N), 0)
    tcol = lax.broadcasted_iota(jnp.int32, (PC, N), 1)
    blank = jnp.zeros((N, N), jnp.float32)

    for d, outside in enumerate((jnp.logical_not(has_lo), jnp.logical_not(has_hi))):
        @pl.when(outside)
        def _():
            sh[d, 0] = blank
            sh[d, 1] = blank
            fh[d] = blank

            @pl.loop(0, PC)
            def _(p):
                for s in range(2):
                    for h in (xh, dh, wh):
                        h[s, d, p] = blank

    tile[...] = jnp.zeros((PC, N), jnp.float32)
    for k in range(7):
        acc[k] = blank

    def neighbour(d):
        return (q, v + 1 - 2 * d)

    def sig_copy(kind, d):
        plane = (1 - d, d)[kind] if kind < 2 else None
        src = di.at[2 + d] if kind == 2 else cond.at[plane]
        dst = fh.at[d] if kind == 2 else sh.at[d, plane]
        return pltpu.make_async_remote_copy(
            src, dst, sig_s.at[kind, d], sig_r.at[kind, d],
            device_id=neighbour(d), device_id_type=MESH,
        )

    def outgoing(stage, s, d, p):
        plane = 1 - d
        if stage == 0:
            return warm.at[s, plane, p]
        return (d0 if stage == 1 else w0).at[s, p, plane]

    def incoming(stage, s, d, p):
        return (xh, dh, wh)[stage].at[s, d, p]

    def halo_copy(stage, s, d, p):
        return pltpu.make_async_remote_copy(
            outgoing(stage, s, d, p), incoming(stage, s, d, p),
            hs.at[stage, s, d, p], hr.at[stage, s, d, p],
            device_id=neighbour(d), device_id_type=MESH,
        )

    def detour_in(stage, s, d, p):
        at = s * PC + p
        return pltpu.make_async_remote_copy(
            outgoing(stage, s, d, p), rb.at[stage, at],
            hs.at[stage, s, d, p], rr.at[stage, at],
            device_id=(q, crossing[d][2]), device_id_type=MESH,
        )

    def detour_out(stage, s, d, p):
        at = s * PC + p
        return pltpu.make_async_remote_copy(
            rb.at[stage, at], incoming(stage, s, d, p),
            rq.at[stage, at], hr.at[stage, s, d, p],
            device_id=(q, crossing[d][1]), device_id_type=MESH,
        )

    exists = (has_hi, has_lo)

    def both(fn):
        for d in range(2):
            @pl.when(exists[d])
            def _():
                fn(d)

    def both_in(fn):
        for d in range(2):
            @pl.when(exists[1 - d])
            def _():
                fn(d)

    def send_halo(stage, s, p):
        for d in range(2):
            around = crossing[d][3] & (v == crossing[d][0])

            @pl.when(exists[d] & jnp.logical_not(around))
            def _():
                halo_copy(stage, s, d, p).start()

            @pl.when(around)
            def _():
                detour_in(stage, s, d, p).start()

    def pass_on(stage, s, p):
        for d in range(2):
            @pl.when(crossing[d][3] & (v == crossing[d][2]))
            def _():
                detour_in(stage, s, d, p).wait_recv()
                detour_out(stage, s, d, p).start()

    def await_halo(stage, s, p):
        both_in(lambda d: halo_copy(stage, s, d, p).wait_recv())

    for copy in local:
        copy.wait()
    partners = (sizes[0] - 1) + (sizes[1] - 1)
    pl.semaphore_wait(barrier, partners + expected)

    both(lambda d: sig_copy(0, d).start())
    for s in range(2):
        @pl.loop(0, PC)
        def _(p):
            send_halo(0, s, p)
    both(lambda d: sig_copy(1, d).start())

    lo_open = has_lo.astype(jnp.float32)
    hi_open = has_hi.astype(jnp.float32)

    def couple(k, s, below, above):
        xp = jnp.where(rows < N - 1, 0.5 * (s + up_row(s)), 0.0)
        yp = jnp.where(cols < N - 1, 0.5 * (s + up_col(s)), 0.0)
        xm, ym = down_row(xp), down_col(yp)
        diag = LEAK + (below + above) + (xp + xm) + (yp + ym)
        inv = 1.0 / diag
        for at, value in ((ZL, below), (ZH, above), (XM, xm), (XP, xp), (YM, ym), (YP, yp)):
            co[at, k] = value * inv
        if k in (1, 2):
            dg[k - 1] = diag
        di[k + 1] = inv

    both_in(lambda d: sig_copy(0, d).wait_recv())
    couple(1, cond[0], 0.5 * (cond[0] + sh[0, 1]) * lo_open, 0.5 * (cond[0] + cond[1]))
    couple(2, cond[1], 0.5 * (cond[0] + cond[1]), 0.5 * (cond[1] + sh[1, 0]) * hi_open)
    both(lambda d: sig_copy(2, d).start())

    def apply(k, x, below, above):
        y = co[ZL, k] * below + co[ZH, k] * above
        y = y + co[XM, k] * down_row(x) + co[XP, k] * up_row(x)
        y = y + co[YM, k] * down_col(x) + co[YP, k] * up_col(x)
        return x - y

    def difference(p, first, second, plane, scale):
        here = (2 * v + plane) * PLANE
        plus = jnp.where(cell == elec[pats[first, p]] - here, scale, 0.0)
        return plus - jnp.where(cell == elec[pats[second, p]] - here, scale, 0.0)

    def probe(p, plane):
        return difference(p, 2, 3, plane, 1.0)

    def record(p, values):
        now = tile[...]
        for k, value in values:
            now = jnp.where((trow == p) & (tcol == k), value, now)
        tile[...] = now

    for s in range(2):
        @pl.loop(0, PC)
        def _(p):
            await_halo(0, s, p)
            a, b = warm[s, 0, p], warm[s, 1, p]
            e0 = -apply(1, a, xh[s, 0, p], b)
            e1 = -apply(2, b, a, xh[s, 1, p])
            if s == 0:
                e0 = e0 + difference(p, 0, 1, 0, strength) * di[2]
                e1 = e1 + difference(p, 0, 1, 1, strength) * di[3]
            d0[s, p, 0] = e0
            d0[s, p, 1] = e1
            send_halo(1, s, p)
            g0, g1 = probe(p, 0), probe(p, 1)
            rho = total(dg[0] * e0 * e0 + dg[1] * e1 * e1)
            ge = total(g0 * e0 + g1 * e1)
            if s == 0:
                record(p, ((F_RHO, rho), (F_D, ge), (F_X, total(g0 * a + g1 * b))))
            else:
                record(p, ((YY, rho), (GY, ge)))
            pass_on(0, s, p)

    both_in(lambda d: sig_copy(1, d).wait_recv())
    couple(0, sh[0, 1], 0.5 * (sh[0, 0] + sh[0, 1]), 0.5 * (cond[0] + sh[0, 1]) * lo_open)
    couple(3, sh[1, 0], 0.5 * (cond[1] + sh[1, 0]) * hi_open, 0.5 * (sh[1, 0] + sh[1, 1]))
    both_in(lambda d: sig_copy(2, d).wait_recv())
    di[0] = fh[0]
    di[5] = fh[1]

    @pl.loop(0, PC)
    def _(p):
        e = [probe(p, k - 2) * di[k] for k in range(6)]
        y = [apply(k, e[k + 1], e[k], e[k + 2]) for k in range(4)]
        for k in range(4):
            gd[p, k] = e[k + 1]
            gw[p, k] = y[k]
        z0, z1 = apply(1, y[1], y[0], y[2]), apply(2, y[2], y[1], y[3])
        g0, g1 = probe(p, 0), probe(p, 1)
        u0, u1 = dg[0] * y[1], dg[1] * y[2]
        record(p, (
            (GG, total(g0 * e[2] + g1 * e[3])),
            (GG + 1, total(g0 * y[1] + g1 * y[2])),
            (GG + 2, total(u0 * y[1] + u1 * y[2])),
            (GG + 3, total(u0 * z0 + u1 * z1)),
        ))

    for s in range(2):
        @pl.loop(0, PC)
        def _(p):
            await_halo(1, s, p)
            a, b = d0[s, p, 0], d0[s, p, 1]
            y0 = apply(1, a, dh[s, 0, p], b)
            y1 = apply(2, b, a, dh[s, 1, p])
            w0[s, p, 0] = y0
            w0[s, p, 1] = y1
            send_halo(2, s, p)
            u0, u1 = dg[0] * y0, dg[1] * y1
            mu = total(u0 * a + u1 * b)
            nu = total(u0 * y0 + u1 * y1)
            gy = total(probe(p, 0) * y0 + probe(p, 1) * y1)
            if s == 0:
                record(p, ((F_MU, mu), (F_NU, nu), (F_W, gy)))
            else:
                cross = total(u0 * gw[p, 1] + u1 * gw[p, 2])
                record(p, ((YY + 1, mu), (YY + 2, nu), (GY + 1, gy), (GY + 2, cross)))
            pass_on(1, s, p)

    for s in range(2):
        @pl.loop(0, PC)
        def _(p):
            pass_on(2, s, p)
            await_halo(2, s, p)
            a, b = w0[s, p, 0], w0[s, p, 1]
            u0 = dg[0] * apply(1, a, wh[s, 0, p], b)
            u1 = dg[1] * apply(2, b, a, wh[s, 1, p])
            xi = total(a * u0 + b * u1)
            if s == 0:
                record(p, ((F_XI, xi),))
            else:
                cross = total(u0 * gw[p, 1] + u1 * gw[p, 2])
                record(p, ((YY + 3, xi), (GY + 3, cross)))

    def sum_copy(stage, k, slot):
        return pltpu.make_async_remote_copy(
            red.at[stage, slot], red.at[stage, slot],
            red_s.at[stage, k], red_r.at[stage, slot],
            device_id=(q, member(stage, k)), device_id_type=MESH,
        )

    value = tile[...]
    for stage in range(2):
        mine, size = rank[stage], sizes[stage]
        red[stage, mine] = value
        for j in range(1, size):
            sum_copy(stage, lax.rem(mine + j, size), mine).start()
        for j in range(1, size):
            k = lax.rem(mine + j, size)
            sum_copy(stage, k, k).wait_recv()
        value = red[stage, 0]
        for k in range(1, size):
            value = value + red[stage, k]

    def column(k):
        return jnp.sum(jnp.where(tcol == k, value, 0.0), axis=1, keepdims=True)

    def steps(rho, mu, nu, xi):
        alpha = rho / mu
        rho1 = rho - 2.0 * alpha * mu + alpha * alpha * nu
        beta1 = 1.0 + rho1 / rho
        curve = beta1 * beta1 * mu - 2.0 * alpha * beta1 * nu + alpha * alpha * xi
        alpha1 = rho1 / curve
        return alpha + alpha1 * beta1, -alpha * alpha1

    c1, c2 = steps(column(F_RHO), column(F_MU), column(F_NU), column(F_XI))
    predicted = column(F_X) + c1 * column(F_D) + c2 * column(F_W)
    observed = jnp.zeros((PC, 1), jnp.float32)
    for p in range(PC):
        observed = jnp.where(trow[:, 0:1] == p, obs[p], observed)
    weight = data_weight * (predicted - observed)
    e1, e2 = steps(*(
        column(YY + k) + weight * (2.0 * column(GY + k) + weight * column(GG + k))
        for k in range(4)
    ))
    for k, factor in enumerate((c1, c2, e1, e2, e1 * weight, e2 * weight)):
        kc[k] = jnp.broadcast_to(factor, (PC, N))
    wide = jnp.where(trow == tcol, predicted, 0.0)
    pred_out[...] = jnp.sum(wide, axis=0, keepdims=True)[:, :PC]

    @pl.loop(0, PC)
    def _(p):
        m = [kc[k, pl.ds(p, 1), :] for k in range(6)]

        def field(s, k):
            if k in (0, 3):
                x, d, w = (h[s, k // 3, p] for h in (xh, dh, wh))
            else:
                x, d, w = warm[s, k - 1, p], d0[s, p, k - 1], w0[s, p, k - 1]
            out = x + m[2 * s] * d + m[2 * s + 1] * w
            if s == 1:
                out = out + m[4] * gd[p, k] + m[5] * gw[p, k]
            return out

        f = [field(0, k) for k in range(4)]
        a = [field(1, k) for k in range(4)]
        for k in range(3):
            acc[k] += (f[k + 1] - f[k]) * (a[k + 1] - a[k])
        for k in range(2):
            x, y = f[k + 1], a[k + 1]
            acc[3 + k] += (up_row(x) - x) * (up_row(y) - y)
            acc[5 + k] += (up_col(x) - x) * (up_col(y) - y)

    for plane in range(2):
        lo, hi = acc[plane], acc[plane + 1]
        lo = lo * lo_open if plane == 0 else lo
        hi = hi * hi_open if plane == 1 else hi
        px = jnp.where(rows < N - 1, acc[3 + plane], 0.0)
        py = jnp.where(cols < N - 1, acc[5 + plane], 0.0)
        gb[plane] = -0.5 * ((lo + hi) + (px + down_row(px)) + (py + down_col(py)))

    is_outer = (q == 0) | (q == npat - 1) if npat > 2 else q < 0
    is_inner = jnp.logical_not(is_outer)
    outward = jnp.where(q < middle, q - 1, q + 1)
    inward = jnp.where(q < middle, q + 1, q - 1)
    height = N // (PIECES // 2)

    def line_copy(leg, j):
        at = (j // (PIECES // 2), pl.ds(j % (PIECES // 2) * height, height))
        src = (gb, half, grad)[leg].at[at]
        dst = (lb[0], lb[1], grad)[leg].at[at]
        return pltpu.make_async_remote_copy(
            src, dst, ls.at[leg, j], lr.at[leg, j],
            device_id=(outward if leg == 2 else inward, v), device_id_type=MESH,
        )

    def piece(j):
        return j // (PIECES // 2), slice(j % (PIECES // 2) * height, (j % (PIECES // 2) + 1) * height)

    @pl.when(is_outer)
    def _():
        for j in range(PIECES):
            line_copy(0, j).start()
        for j in range(PIECES):
            line_copy(2, j).wait_recv()
        for j in range(PIECES):
            line_copy(0, j).wait_send()

    @pl.when(is_inner)
    def _():
        for j in range(PIECES):
            at = piece(j)
            if npat > 2:
                line_copy(0, j).wait_recv()
                half[at] = gb[at] + lb[0][at]
            else:
                half[at] = gb[at]
            line_copy(1, j).start()
        for j in range(PIECES):
            at = piece(j)
            line_copy(1, j).wait_recv()
            grad[at] = half[at] + lb[1][at]
            if npat > 2:
                line_copy(2, j).start()
        for j in range(PIECES):
            line_copy(1, j).wait_send()
            if npat > 2:
                line_copy(2, j).wait_send()

    grad_out[...] = grad[...]

    for kind in range(3):
        both(lambda d: sig_copy(kind, d).wait_send())

    @pl.loop(0, PC)
    def _(p):
        for stage in range(3):
            for s in range(2):
                both(lambda d: halo_copy(stage, s, d, p).wait_send())
                for d in range(2):
                    @pl.when(crossing[d][3] & (v == crossing[d][2]))
                    def _():
                        detour_out(stage, s, d, p).wait_send()

    for stage in range(2):
        for j in range(1, sizes[stage]):
            sum_copy(stage, lax.rem(rank[stage] + j, sizes[stage]), rank[stage]).wait_send()


def solution(mesh):
    npat, layers = mesh.shape["pat"], mesh.shape["vox"]
    group = 8 if layers >= 64 else 2

    def per_device(conductivity, warm_forward, warm_adjoint, electrodes, patterns, observed):
        planes = conductivity.shape[0]
        strength = 2.0 * math.sqrt(layers * planes * PLANE)
        vmem = pl.BlockSpec(memory_space=pltpu.VMEM)
        smem = pl.BlockSpec(memory_space=pltpu.SMEM)
        hbm = pl.BlockSpec(memory_space=pltpu.HBM)
        f32 = jnp.float32
        dma = pltpu.SemaphoreType.DMA
        groups = layers // group
        widest = max(group, groups)
        gradient, predicted = pl.pallas_call(
            functools.partial(kernel, npat, layers, group, strength),
            out_shape=(
                jax.ShapeDtypeStruct((2, N, N), f32),
                jax.ShapeDtypeStruct((1, PC), f32),
            ),
            in_specs=[hbm, hbm, hbm, smem, smem, smem],
            out_specs=(vmem, vmem),
            scratch_shapes=[
                pltpu.VMEM((2, N, N), f32),
                pltpu.VMEM((2, 2, PC, N, N), f32),
                pltpu.VMEM((2, 2, N, N), f32),
                pltpu.VMEM((2, N, N), f32),
                pltpu.VMEM((2, 2, PC, N, N), f32),
                pltpu.VMEM((2, 2, PC, N, N), f32),
                pltpu.VMEM((2, 2, PC, N, N), f32),
                pltpu.VMEM((2, PC, 2, N, N), f32),
                pltpu.VMEM((2, PC, 2, N, N), f32),
                pltpu.VMEM((PC, 4, N, N), f32),
                pltpu.VMEM((PC, 4, N, N), f32),
                pltpu.VMEM((3, 2 * PC, N, N), f32),
                pltpu.VMEM((6, 4, N, N), f32),
                pltpu.VMEM((2, N, N), f32),
                pltpu.VMEM((6, N, N), f32),
                pltpu.VMEM((7, N, N), f32),
                pltpu.VMEM((PC, N), f32),
                pltpu.VMEM((2, widest, PC, N), f32),
                pltpu.VMEM((6, PC, N), f32),
                pltpu.VMEM((2, N, N), f32),
                pltpu.VMEM((2, N, N), f32),
                pltpu.VMEM((2, N, N), f32),
                pltpu.VMEM((2, N, N), f32),
                pltpu.VMEM((2, N, N), f32),
                dma((3,)),
                dma((3, 2)),
                dma((3, 2)),
                dma((3, 2, 2, PC)),
                dma((3, 2, 2, PC)),
                dma((3, 2 * PC)),
                dma((3, 2 * PC)),
                dma((2, widest)),
                dma((2, widest)),
                dma((3, PIECES)),
                dma((3, PIECES)),
            ],
            compiler_params=pltpu.CompilerParams(
                collective_id=0, has_side_effects=True, vmem_limit_bytes=58 * 2**20
            ),
            name="ert_gradient",
        )(conductivity, warm_forward, warm_adjoint, electrodes, patterns.T, observed)
        return gradient, predicted.reshape(PC)

    in_specs = (
        P("vox", None, None),
        P("vox", "pat", None, None),
        P("vox", "pat", None, None),
        P(),
        P("pat", None),
        P("pat"),
    )
    return jax.shard_map(
        per_device,
        mesh=mesh,
        in_specs=in_specs,
        out_specs=(P("vox", None, None), P("pat")),
        check_vma=False,
    )
```

```python
import functools
import math

import jax
import jax.numpy as jnp
from jax import lax
from jax.experimental import pallas as pl
from jax.experimental.pallas import tpu as pltpu
from jax.sharding import PartitionSpec as P

MESH = pl.DeviceIdType.MESH
LEAK = 0.05
N = 128
PLANE = N * N
PC = 8
PIECES = 8

ZL, ZH, XM, XP, YM, YP = range(6)
F_RHO, F_MU, F_NU, F_XI, F_X, F_D, F_W = range(7)
YY, GY, GG = 7, 11, 15


def up_row(x):
    return pltpu.roll(x, N - 1, 0)


def down_row(x):
    return pltpu.roll(x, 1, 0)


def up_col(x):
    return pltpu.roll(x, N - 1, 1)


def down_col(x):
    return pltpu.roll(x, 1, 1)


def total(x):
    part = jnp.sum(x.reshape(N // 8, 8, N), axis=0)
    return jnp.sum(jnp.sum(part, axis=1, keepdims=True), axis=0, keepdims=True)


def kernel(
    npat,
    layers,
    group,
    strength,
    cond_in,
    wf_in,
    wa_in,
    elec,
    pats,
    obs,
    grad_out,
    pred_out,
    cond,
    warm,
    sh,
    fh,
    xh,
    dh,
    wh,
    d0,
    w0,
    gd,
    gw,
    rb,
    sb,
    co,
    dg,
    di,
    acc,
    tile,
    red,
    kc,
    gb,
    lb_outer,
    lb_inner,
    half,
    grad,
    in_s,
    sig_s,
    sig_r,
    sig_rr,
    sig_rq,
    hs,
    hr,
    rr,
    rq,
    red_s,
    red_r,
    ls,
    lr,
):
    lb = (lb_outer, lb_inner)
    q = lax.axis_index("pat")
    v = lax.axis_index("vox")
    last = layers - 1
    has_lo = v > 0
    has_hi = v < last
    groups = layers // group
    rank = (lax.rem(v, group), v // group)
    sizes = (group, groups)
    data_weight = 0.1 * strength
    lower, upper = layers // 2 - 1, layers // 2
    middle = npat // 2
    inner = (q >= middle - 1) & (q <= middle) if npat > 2 else q == 0
    crossing = (
        (lower, upper, 0, inner),
        (upper, lower, last, jnp.logical_not(inner)),
    )

    local = [
        pltpu.make_async_copy(cond_in, cond, in_s.at[0]),
        pltpu.make_async_copy(wf_in, warm.at[0], in_s.at[1]),
        pltpu.make_async_copy(wa_in, warm.at[1], in_s.at[2]),
    ]

    def member(stage, k):
        return (v // group) * group + k if stage == 0 else k * group + lax.rem(v, group)

    barrier = pltpu.get_barrier_semaphore()

    def greet(device):
        pl.semaphore_signal(barrier, inc=1, device_id=device, device_id_type=MESH)

    @pl.when(has_lo)
    def _():
        greet((q, v - 1))

    @pl.when(has_hi)
    def _():
        greet((q, v + 1))

    expected = has_lo.astype(jnp.int32) + has_hi.astype(jnp.int32)
    for source, target, via, taken in crossing:
        on_path = taken & ((v == source) | (v == target))

        @pl.when(on_path)
        def _():
            greet((q, via))

        @pl.when(taken & (v == via))
        def _():
            greet((q, source))
            greet((q, target))

        expected = expected + on_path.astype(jnp.int32)
        expected = expected + 2 * (taken & (v == via)).astype(jnp.int32)

    for stage in range(2):
        for j in range(1, sizes[stage]):
            greet((q, member(stage, lax.rem(rank[stage] + j, sizes[stage]))))
    below, above = q > 0, q < npat - 1

    @pl.when(below)
    def _():
        greet((q - 1, v))

    @pl.when(above)
    def _():
        greet((q + 1, v))

    expected = expected + below.astype(jnp.int32) + above.astype(jnp.int32)
    for copy in local:
        copy.start()

    rows = lax.broadcasted_iota(jnp.int32, (N, N), 0)
    cols = lax.broadcasted_iota(jnp.int32, (N, N), 1)
    cell = rows * N + cols
    trow = lax.broadcasted_iota(jnp.int32, (PC, N), 0)
    tcol = lax.broadcasted_iota(jnp.int32, (PC, N), 1)
    blank = jnp.zeros((N, N), jnp.float32)

    for d, outside in enumerate((jnp.logical_not(has_lo), jnp.logical_not(has_hi))):
        @pl.when(outside)
        def _():
            sh[d, 0] = blank
            sh[d, 1] = blank
            fh[d] = blank

            @pl.loop(0, PC)
            def _(p):
                for s in range(2):
                    for h in (xh, dh, wh):
                        h[s, d, p] = blank

    tile[...] = jnp.zeros((PC, N), jnp.float32)
    for k in range(7):
        acc[k] = blank

    def neighbour(d):
        return (q, v + 1 - 2 * d)

    def sig_ends(kind, d):
        if kind == 2:
            return di.at[2 + d], fh.at[d]
        plane = (1 - d, d)[kind]
        return cond.at[plane], sh.at[d, plane]

    def sig_copy(kind, d):
        src, dst = sig_ends(kind, d)
        return pltpu.make_async_remote_copy(
            src, dst, sig_s.at[kind, d], sig_r.at[kind, d],
            device_id=neighbour(d), device_id_type=MESH,
        )

    def sig_in(kind, d):
        return pltpu.make_async_remote_copy(
            sig_ends(kind, d)[0], sb.at[kind], sig_s.at[kind, d], sig_rr.at[kind],
            device_id=(q, crossing[d][2]), device_id_type=MESH,
        )

    def sig_out(kind, d):
        return pltpu.make_async_remote_copy(
            sb.at[kind], sig_ends(kind, d)[1], sig_rq.at[kind], sig_r.at[kind, d],
            device_id=(q, crossing[d][1]), device_id_type=MESH,
        )

    def outgoing(stage, s, d, p):
        plane = 1 - d
        if stage == 0:
            return warm.at[s, plane, p]
        return (d0 if stage == 1 else w0).at[s, p, plane]

    def incoming(stage, s, d, p):
        return (xh, dh, wh)[stage].at[s, d, p]

    def halo_copy(stage, s, d, p):
        return pltpu.make_async_remote_copy(
            outgoing(stage, s, d, p), incoming(stage, s, d, p),
            hs.at[stage, s, d, p], hr.at[stage, s, d, p],
            device_id=neighbour(d), device_id_type=MESH,
        )

    def detour_in(stage, s, d, p):
        at = s * PC + p
        return pltpu.make_async_remote_copy(
            outgoing(stage, s, d, p), rb.at[stage, at],
            hs.at[stage, s, d, p], rr.at[stage, at],
            device_id=(q, crossing[d][2]), device_id_type=MESH,
        )

    def detour_out(stage, s, d, p):
        at = s * PC + p
        return pltpu.make_async_remote_copy(
            rb.at[stage, at], incoming(stage, s, d, p),
            rq.at[stage, at], hr.at[stage, s, d, p],
            device_id=(q, crossing[d][1]), device_id_type=MESH,
        )

    exists = (has_hi, has_lo)

    def both(fn):
        for d in range(2):
            @pl.when(exists[d])
            def _():
                fn(d)

    def both_in(fn):
        for d in range(2):
            @pl.when(exists[1 - d])
            def _():
                fn(d)

    def send_sig(kind):
        for d in range(2):
            around = crossing[d][3] & (v == crossing[d][0])

            @pl.when(exists[d] & jnp.logical_not(around))
            def _():
                sig_copy(kind, d).start()

            @pl.when(around)
            def _():
                sig_in(kind, d).start()

    def pass_sig(kind):
        for d in range(2):
            @pl.when(crossing[d][3] & (v == crossing[d][2]))
            def _():
                sig_in(kind, d).wait_recv()
                sig_out(kind, d).start()

    def send_halo(stage, s, p):
        for d in range(2):
            around = crossing[d][3] & (v == crossing[d][0])

            @pl.when(exists[d] & jnp.logical_not(around))
            def _():
                halo_copy(stage, s, d, p).start()

            @pl.when(around)
            def _():
                detour_in(stage, s, d, p).start()

    def pass_on(stage, s, p):
        for d in range(2):
            @pl.when(crossing[d][3] & (v == crossing[d][2]))
            def _():
                detour_in(stage, s, d, p).wait_recv()
                detour_out(stage, s, d, p).start()

    def await_halo(stage, s, p):
        both_in(lambda d: halo_copy(stage, s, d, p).wait_recv())

    for copy in local:
        copy.wait()
    partners = (sizes[0] - 1) + (sizes[1] - 1)
    pl.semaphore_wait(barrier, partners + expected)

    send_sig(0)
    for s in range(2):
        @pl.loop(0, PC)
        def _(p):
            send_halo(0, s, p)
    pass_sig(0)

    lo_open = has_lo.astype(jnp.float32)
    hi_open = has_hi.astype(jnp.float32)

    def couple(k, s, below, above):
        xp = jnp.where(rows < N - 1, 0.5 * (s + up_row(s)), 0.0)
        yp = jnp.where(cols < N - 1, 0.5 * (s + up_col(s)), 0.0)
        xm, ym = down_row(xp), down_col(yp)
        diag = LEAK + (below + above) + (xp + xm) + (yp + ym)
        inv = 1.0 / diag
        for at, value in ((ZL, below), (ZH, above), (XM, xm), (XP, xp), (YM, ym), (YP, yp)):
            co[at, k] = value * inv
        if k in (1, 2):
            dg[k - 1] = diag
        di[k + 1] = inv

    both_in(lambda d: sig_copy(0, d).wait_recv())
    couple(1, cond[0], 0.5 * (cond[0] + sh[0, 1]) * lo_open, 0.5 * (cond[0] + cond[1]))
    couple(2, cond[1], 0.5 * (cond[0] + cond[1]), 0.5 * (cond[1] + sh[1, 0]) * hi_open)

    def apply(k, x, below, above):
        y = co[ZL, k] * below + co[ZH, k] * above
        y = y + co[XM, k] * down_row(x) + co[XP, k] * up_row(x)
        y = y + co[YM, k] * down_col(x) + co[YP, k] * up_col(x)
        return x - y

    def difference(p, first, second, plane, scale):
        here = (2 * v + plane) * PLANE
        plus = jnp.where(cell == elec[pats[first, p]] - here, scale, 0.0)
        return plus - jnp.where(cell == elec[pats[second, p]] - here, scale, 0.0)

    def probe(p, plane):
        return difference(p, 2, 3, plane, 1.0)

    def record(p, values):
        now = tile[...]
        for k, value in values:
            now = jnp.where((trow == p) & (tcol == k), value, now)
        tile[...] = now

    for s in range(2):
        @pl.loop(0, PC)
        def _(p):
            await_halo(0, s, p)
            a, b = warm[s, 0, p], warm[s, 1, p]
            e0 = -apply(1, a, xh[s, 0, p], b)
            e1 = -apply(2, b, a, xh[s, 1, p])
            if s == 0:
                e0 = e0 + difference(p, 0, 1, 0, strength) * di[2]
                e1 = e1 + difference(p, 0, 1, 1, strength) * di[3]
            d0[s, p, 0] = e0
            d0[s, p, 1] = e1
            send_halo(1, s, p)
            g0, g1 = probe(p, 0), probe(p, 1)
            rho = total(dg[0] * e0 * e0 + dg[1] * e1 * e1)
            ge = total(g0 * e0 + g1 * e1)
            if s == 0:
                record(p, ((F_RHO, rho), (F_D, ge), (F_X, total(g0 * a + g1 * b))))
            else:
                record(p, ((YY, rho), (GY, ge)))
            pass_on(0, s, p)

    send_sig(1)
    send_sig(2)

    for s in range(2):
        @pl.loop(0, PC)
        def _(p):
            await_halo(1, s, p)
            a, b = d0[s, p, 0], d0[s, p, 1]
            y0 = apply(1, a, dh[s, 0, p], b)
            y1 = apply(2, b, a, dh[s, 1, p])
            w0[s, p, 0] = y0
            w0[s, p, 1] = y1
            send_halo(2, s, p)
            u0, u1 = dg[0] * y0, dg[1] * y1
            mu = total(u0 * a + u1 * b)
            nu = total(u0 * y0 + u1 * y1)
            gy = total(probe(p, 0) * y0 + probe(p, 1) * y1)
            if s == 0:
                record(p, ((F_MU, mu), (F_NU, nu), (F_W, gy)))
            else:
                record(p, ((YY + 1, mu), (YY + 2, nu), (GY + 1, gy)))
            pass_on(1, s, p)

    pass_sig(1)
    pass_sig(2)
    both_in(lambda d: sig_copy(1, d).wait_recv())
    couple(0, sh[0, 1], 0.5 * (sh[0, 0] + sh[0, 1]), 0.5 * (cond[0] + sh[0, 1]) * lo_open)
    couple(3, sh[1, 0], 0.5 * (cond[1] + sh[1, 0]) * hi_open, 0.5 * (sh[1, 0] + sh[1, 1]))
    both_in(lambda d: sig_copy(2, d).wait_recv())
    di[0] = fh[0]
    di[5] = fh[1]

    @pl.loop(0, PC)
    def _(p):
        e = [probe(p, k - 2) * di[k] for k in range(6)]
        y = [apply(k, e[k + 1], e[k], e[k + 2]) for k in range(4)]
        for k in range(4):
            gd[p, k] = e[k + 1]
            gw[p, k] = y[k]
        z0, z1 = apply(1, y[1], y[0], y[2]), apply(2, y[2], y[1], y[3])
        g0, g1 = probe(p, 0), probe(p, 1)
        u0, u1 = dg[0] * y[1], dg[1] * y[2]
        record(p, (
            (GG, total(g0 * e[2] + g1 * e[3])),
            (GG + 1, total(g0 * y[1] + g1 * y[2])),
            (GG + 2, total(u0 * y[1] + u1 * y[2])),
            (GG + 3, total(u0 * z0 + u1 * z1)),
        ))

    for s in range(2):
        @pl.loop(0, PC)
        def _(p):
            pass_on(2, s, p)
            await_halo(2, s, p)
            a, b = w0[s, p, 0], w0[s, p, 1]
            u0 = dg[0] * apply(1, a, wh[s, 0, p], b)
            u1 = dg[1] * apply(2, b, a, wh[s, 1, p])
            xi = total(a * u0 + b * u1)
            if s == 0:
                record(p, ((F_XI, xi),))
            else:
                k0, k1 = gw[p, 1], gw[p, 2]
                near = total(dg[0] * a * k0 + dg[1] * b * k1)
                record(p, ((YY + 3, xi), (GY + 2, near), (GY + 3, total(u0 * k0 + u1 * k1))))

    def sum_copy(stage, k, slot):
        return pltpu.make_async_remote_copy(
            red.at[stage, slot], red.at[stage, slot],
            red_s.at[stage, k], red_r.at[stage, slot],
            device_id=(q, member(stage, k)), device_id_type=MESH,
        )

    value = tile[...]
    for stage in range(2):
        mine, size = rank[stage], sizes[stage]
        red[stage, mine] = value
        for j in range(1, size):
            sum_copy(stage, lax.rem(mine + j, size), mine).start()
        for j in range(1, size):
            k = lax.rem(mine + j, size)
            sum_copy(stage, k, k).wait_recv()
        value = red[stage, 0]
        for k in range(1, size):
            value = value + red[stage, k]

    def column(k):
        return jnp.sum(jnp.where(tcol == k, value, 0.0), axis=1, keepdims=True)

    def steps(rho, mu, nu, xi):
        alpha = rho / mu
        rho1 = rho - 2.0 * alpha * mu + alpha * alpha * nu
        beta1 = 1.0 + rho1 / rho
        curve = beta1 * beta1 * mu - 2.0 * alpha * beta1 * nu + alpha * alpha * xi
        alpha1 = rho1 / curve
        return alpha + alpha1 * beta1, -alpha * alpha1

    c1, c2 = steps(column(F_RHO), column(F_MU), column(F_NU), column(F_XI))
    predicted = column(F_X) + c1 * column(F_D) + c2 * column(F_W)
    observed = jnp.zeros((PC, 1), jnp.float32)
    for p in range(PC):
        observed = jnp.where(trow[:, 0:1] == p, obs[p], observed)
    weight = data_weight * (predicted - observed)
    e1, e2 = steps(*(
        column(YY + k) + weight * (2.0 * column(GY + k) + weight * column(GG + k))
        for k in range(4)
    ))
    for k, factor in enumerate((c1, c2, e1, e2, e1 * weight, e2 * weight)):
        kc[k] = jnp.broadcast_to(factor, (PC, N))
    wide = jnp.where(trow == tcol, predicted, 0.0)
    pred_out[...] = jnp.sum(wide, axis=0, keepdims=True)[:, :PC]

    @pl.loop(0, PC)
    def _(p):
        m = [kc[k, pl.ds(p, 1), :] for k in range(6)]

        def field(s, k):
            if k in (0, 3):
                x, d, w = (h[s, k // 3, p] for h in (xh, dh, wh))
            else:
                x, d, w = warm[s, k - 1, p], d0[s, p, k - 1], w0[s, p, k - 1]
            out = x + m[2 * s] * d + m[2 * s + 1] * w
            if s == 1:
                out = out + m[4] * gd[p, k] + m[5] * gw[p, k]
            return out

        f = [field(0, k) for k in range(4)]
        a = [field(1, k) for k in range(4)]
        for k in range(3):
            acc[k] += (f[k + 1] - f[k]) * (a[k + 1] - a[k])
        for k in range(2):
            x, y = f[k + 1], a[k + 1]
            acc[3 + k] += (up_row(x) - x) * (up_row(y) - y)
            acc[5 + k] += (up_col(x) - x) * (up_col(y) - y)

    for plane in range(2):
        lo, hi = acc[plane], acc[plane + 1]
        lo = lo * lo_open if plane == 0 else lo
        hi = hi * hi_open if plane == 1 else hi
        px = jnp.where(rows < N - 1, acc[3 + plane], 0.0)
        py = jnp.where(cols < N - 1, acc[5 + plane], 0.0)
        gb[plane] = -0.5 * ((lo + hi) + (px + down_row(px)) + (py + down_col(py)))

    is_outer = (q == 0) | (q == npat - 1) if npat > 2 else q < 0
    is_inner = jnp.logical_not(is_outer)
    outward = jnp.where(q < middle, q - 1, q + 1)
    inward = jnp.where(q < middle, q + 1, q - 1)
    height = N // (PIECES // 2)

    def line_copy(leg, j):
        at = (j // (PIECES // 2), pl.ds(j % (PIECES // 2) * height, height))
        src = (gb, half, grad)[leg].at[at]
        dst = (lb[0], lb[1], grad)[leg].at[at]
        return pltpu.make_async_remote_copy(
            src, dst, ls.at[leg, j], lr.at[leg, j],
            device_id=(outward if leg == 2 else inward, v), device_id_type=MESH,
        )

    def piece(j):
        return j // (PIECES // 2), slice(j % (PIECES // 2) * height, (j % (PIECES // 2) + 1) * height)

    @pl.when(is_outer)
    def _():
        for j in range(PIECES):
            line_copy(0, j).start()
        for j in range(PIECES):
            line_copy(2, j).wait_recv()
        for j in range(PIECES):
            line_copy(0, j).wait_send()

    @pl.when(is_inner)
    def _():
        for j in range(PIECES):
            at = piece(j)
            if npat > 2:
                line_copy(0, j).wait_recv()
                half[at] = gb[at] + lb[0][at]
            else:
                half[at] = gb[at]
            line_copy(1, j).start()
        for j in range(PIECES):
            at = piece(j)
            line_copy(1, j).wait_recv()
            grad[at] = half[at] + lb[1][at]
            if npat > 2:
                line_copy(2, j).start()
        for j in range(PIECES):
            line_copy(1, j).wait_send()
            if npat > 2:
                line_copy(2, j).wait_send()

    grad_out[...] = grad[...]

    for kind in range(3):
        both(lambda d: sig_copy(kind, d).wait_send())
        for d in range(2):
            @pl.when(crossing[d][3] & (v == crossing[d][2]))
            def _():
                sig_out(kind, d).wait_send()

    @pl.loop(0, PC)
    def _(p):
        for stage in range(3):
            for s in range(2):
                both(lambda d: halo_copy(stage, s, d, p).wait_send())
                for d in range(2):
                    @pl.when(crossing[d][3] & (v == crossing[d][2]))
                    def _():
                        detour_out(stage, s, d, p).wait_send()

    for stage in range(2):
        for j in range(1, sizes[stage]):
            sum_copy(stage, lax.rem(rank[stage] + j, sizes[stage]), rank[stage]).wait_send()


def solution(mesh):
    npat, layers = mesh.shape["pat"], mesh.shape["vox"]
    group = 8 if layers >= 64 else 2

    def per_device(conductivity, warm_forward, warm_adjoint, electrodes, patterns, observed):
        planes = conductivity.shape[0]
        strength = 2.0 * math.sqrt(layers * planes * PLANE)
        vmem = pl.BlockSpec(memory_space=pltpu.VMEM)
        smem = pl.BlockSpec(memory_space=pltpu.SMEM)
        hbm = pl.BlockSpec(memory_space=pltpu.HBM)
        f32 = jnp.float32
        dma = pltpu.SemaphoreType.DMA
        groups = layers // group
        widest = max(group, groups)
        gradient, predicted = pl.pallas_call(
            functools.partial(kernel, npat, layers, group, strength),
            out_shape=(
                jax.ShapeDtypeStruct((2, N, N), f32),
                jax.ShapeDtypeStruct((1, PC), f32),
            ),
            in_specs=[hbm, hbm, hbm, smem, smem, smem],
            out_specs=(vmem, vmem),
            scratch_shapes=[
                pltpu.VMEM((2, N, N), f32),
                pltpu.VMEM((2, 2, PC, N, N), f32),
                pltpu.VMEM((2, 2, N, N), f32),
                pltpu.VMEM((2, N, N), f32),
                pltpu.VMEM((2, 2, PC, N, N), f32),
                pltpu.VMEM((2, 2, PC, N, N), f32),
                pltpu.VMEM((2, 2, PC, N, N), f32),
                pltpu.VMEM((2, PC, 2, N, N), f32),
                pltpu.VMEM((2, PC, 2, N, N), f32),
                pltpu.VMEM((PC, 4, N, N), f32),
                pltpu.VMEM((PC, 4, N, N), f32),
                pltpu.VMEM((3, 2 * PC, N, N), f32),
                pltpu.VMEM((3, N, N), f32),
                pltpu.VMEM((6, 4, N, N), f32),
                pltpu.VMEM((2, N, N), f32),
                pltpu.VMEM((6, N, N), f32),
                pltpu.VMEM((7, N, N), f32),
                pltpu.VMEM((PC, N), f32),
                pltpu.VMEM((2, widest, PC, N), f32),
                pltpu.VMEM((6, PC, N), f32),
                pltpu.VMEM((2, N, N), f32),
                pltpu.VMEM((2, N, N), f32),
                pltpu.VMEM((2, N, N), f32),
                pltpu.VMEM((2, N, N), f32),
                pltpu.VMEM((2, N, N), f32),
                dma((3,)),
                dma((3, 2)),
                dma((3, 2)),
                dma((3,)),
                dma((3,)),
                dma((3, 2, 2, PC)),
                dma((3, 2, 2, PC)),
                dma((3, 2 * PC)),
                dma((3, 2 * PC)),
                dma((2, widest)),
                dma((2, widest)),
                dma((3, PIECES)),
                dma((3, PIECES)),
            ],
            compiler_params=pltpu.CompilerParams(
                collective_id=0, has_side_effects=True, vmem_limit_bytes=58 * 2**20
            ),
            name="ert_gradient",
        )(conductivity, warm_forward, warm_adjoint, electrodes, patterns.T, observed)
        return gradient, predicted.reshape(PC)

    in_specs = (
        P("vox", None, None),
        P("vox", "pat", None, None),
        P("vox", "pat", None, None),
        P(),
        P("pat", None),
        P("pat"),
    )
    return jax.shard_map(
        per_device,
        mesh=mesh,
        in_specs=in_specs,
        out_specs=(P("vox", None, None), P("pat")),
        check_vma=False,
    )
```

```python
import functools
import math

import jax
import jax.numpy as jnp
from jax import lax
from jax.experimental import pallas as pl
from jax.experimental.pallas import tpu as pltpu
from jax.sharding import PartitionSpec as P

MESH = pl.DeviceIdType.MESH
LEAK = 0.05
N = 128
PLANE = N * N
PC = 8
PIECES = 8

ZL, ZH, XM, XP, YM, YP = range(6)
F_RHO, F_MU, F_NU, F_XI, F_X, F_D, F_W = range(7)
YY, GY, GG = 7, 11, 15


def up_row(x):
    return pltpu.roll(x, N - 1, 0)


def down_row(x):
    return pltpu.roll(x, 1, 0)


def up_col(x):
    return pltpu.roll(x, N - 1, 1)


def down_col(x):
    return pltpu.roll(x, 1, 1)


def total(x):
    part = jnp.sum(x.reshape(N // 8, 8, N), axis=0)
    return jnp.sum(jnp.sum(part, axis=1, keepdims=True), axis=0, keepdims=True)


def kernel(
    npat,
    layers,
    group,
    strength,
    cond_in,
    wf_in,
    wa_in,
    elec,
    pats,
    obs,
    grad_out,
    pred_out,
    cond,
    warm,
    sh,
    fh,
    xh,
    dh,
    wh,
    d0,
    w0,
    gd,
    gw,
    rb,
    sb,
    co,
    dg,
    di,
    acc,
    top,
    tile,
    red,
    kc,
    gb,
    lb_outer,
    lb_inner,
    half,
    grad,
    in_s,
    sig_s,
    sig_r,
    sig_rr,
    sig_rq,
    hs,
    hr,
    rr,
    rq,
    red_s,
    red_r,
    ls,
    lr,
):
    lb = (lb_outer, lb_inner)
    q = lax.axis_index("pat")
    v = lax.axis_index("vox")
    last = layers - 1
    has_lo = v > 0
    has_hi = v < last
    groups = layers // group
    rank = (lax.rem(v, group), v // group)
    sizes = (group, groups)
    data_weight = 0.1 * strength
    lower, upper = layers // 2 - 1, layers // 2
    middle = npat // 2
    inner = (q >= middle - 1) & (q <= middle) if npat > 2 else q == 0
    crossing = (
        (lower, upper, 0, inner),
        (upper, lower, last, jnp.logical_not(inner)),
    )

    local = [
        pltpu.make_async_copy(cond_in, cond, in_s.at[0]),
        pltpu.make_async_copy(wf_in, warm.at[0], in_s.at[1]),
        pltpu.make_async_copy(wa_in, warm.at[1], in_s.at[2]),
    ]

    def member(stage, k):
        return (v // group) * group + k if stage == 0 else k * group + lax.rem(v, group)

    barrier = pltpu.get_barrier_semaphore()

    def greet(device):
        pl.semaphore_signal(barrier, inc=1, device_id=device, device_id_type=MESH)

    @pl.when(has_lo)
    def _():
        greet((q, v - 1))

    @pl.when(has_hi)
    def _():
        greet((q, v + 1))

    expected = has_lo.astype(jnp.int32) + has_hi.astype(jnp.int32)
    for source, target, via, taken in crossing:
        on_path = taken & ((v == source) | (v == target))

        @pl.when(on_path)
        def _():
            greet((q, via))

        @pl.when(taken & (v == via))
        def _():
            greet((q, source))
            greet((q, target))

        expected = expected + on_path.astype(jnp.int32)
        expected = expected + 2 * (taken & (v == via)).astype(jnp.int32)

    for stage in range(2):
        for j in range(1, sizes[stage]):
            greet((q, member(stage, lax.rem(rank[stage] + j, sizes[stage]))))
    below, above = q > 0, q < npat - 1

    @pl.when(below)
    def _():
        greet((q - 1, v))

    @pl.when(above)
    def _():
        greet((q + 1, v))

    expected = expected + below.astype(jnp.int32) + above.astype(jnp.int32)
    for copy in local:
        copy.start()

    rows = lax.broadcasted_iota(jnp.int32, (N, N), 0)
    cols = lax.broadcasted_iota(jnp.int32, (N, N), 1)
    cell = rows * N + cols
    trow = lax.broadcasted_iota(jnp.int32, (PC, N), 0)
    tcol = lax.broadcasted_iota(jnp.int32, (PC, N), 1)
    blank = jnp.zeros((N, N), jnp.float32)

    for d, outside in enumerate((jnp.logical_not(has_lo), jnp.logical_not(has_hi))):
        @pl.when(outside)
        def _():
            sh[d, 0] = blank
            sh[d, 1] = blank
            fh[d] = blank

            @pl.loop(0, PC)
            def _(p):
                for s in range(2):
                    for h in (xh, dh, wh):
                        h[s, d, p] = blank

    tile[...] = jnp.zeros((PC, N), jnp.float32)
    for k in range(7):
        acc[k] = blank

    def neighbour(d):
        return (q, v + 1 - 2 * d)

    def sig_ends(kind, d):
        if kind == 2:
            return di.at[2 + d], fh.at[d]
        plane = (1 - d, d)[kind]
        return cond.at[plane], sh.at[d, plane]

    def sig_copy(kind, d):
        src, dst = sig_ends(kind, d)
        return pltpu.make_async_remote_copy(
            src, dst, sig_s.at[kind, d], sig_r.at[kind, d],
            device_id=neighbour(d), device_id_type=MESH,
        )

    def sig_in(kind, d):
        return pltpu.make_async_remote_copy(
            sig_ends(kind, d)[0], sb.at[kind], sig_s.at[kind, d], sig_rr.at[kind],
            device_id=(q, crossing[d][2]), device_id_type=MESH,
        )

    def sig_out(kind, d):
        return pltpu.make_async_remote_copy(
            sb.at[kind], sig_ends(kind, d)[1], sig_rq.at[kind], sig_r.at[kind, d],
            device_id=(q, crossing[d][1]), device_id_type=MESH,
        )

    def outgoing(stage, s, d, p):
        plane = 1 - d
        if stage == 0:
            return warm.at[s, plane, p]
        return (d0 if stage == 1 else w0).at[s, p, plane]

    def incoming(stage, s, d, p):
        return (xh, dh, wh)[stage].at[s, d, p]

    def halo_copy(stage, s, d, p):
        return pltpu.make_async_remote_copy(
            outgoing(stage, s, d, p), incoming(stage, s, d, p),
            hs.at[stage, s, d, p], hr.at[stage, s, d, p],
            device_id=neighbour(d), device_id_type=MESH,
        )

    def detour_in(stage, s, d, p):
        at = s * PC + p
        return pltpu.make_async_remote_copy(
            outgoing(stage, s, d, p), rb.at[stage, at],
            hs.at[stage, s, d, p], rr.at[stage, at],
            device_id=(q, crossing[d][2]), device_id_type=MESH,
        )

    def detour_out(stage, s, d, p):
        at = s * PC + p
        return pltpu.make_async_remote_copy(
            rb.at[stage, at], incoming(stage, s, d, p),
            rq.at[stage, at], hr.at[stage, s, d, p],
            device_id=(q, crossing[d][1]), device_id_type=MESH,
        )

    exists = (has_hi, has_lo)

    def both(fn):
        for d in range(2):
            @pl.when(exists[d])
            def _():
                fn(d)

    def both_in(fn):
        for d in range(2):
            @pl.when(exists[1 - d])
            def _():
                fn(d)

    def send_sig(kind):
        for d in range(2):
            around = crossing[d][3] & (v == crossing[d][0])

            @pl.when(exists[d] & jnp.logical_not(around))
            def _():
                sig_copy(kind, d).start()

            @pl.when(around)
            def _():
                sig_in(kind, d).start()

    def pass_sig(kind):
        for d in range(2):
            @pl.when(crossing[d][3] & (v == crossing[d][2]))
            def _():
                sig_in(kind, d).wait_recv()
                sig_out(kind, d).start()

    def send_halo(stage, s, p):
        for d in range(2):
            around = crossing[d][3] & (v == crossing[d][0])

            @pl.when(exists[d] & jnp.logical_not(around))
            def _():
                halo_copy(stage, s, d, p).start()

            @pl.when(around)
            def _():
                detour_in(stage, s, d, p).start()

    def pass_on(stage, s, p):
        for d in range(2):
            @pl.when(crossing[d][3] & (v == crossing[d][2]))
            def _():
                detour_in(stage, s, d, p).wait_recv()
                detour_out(stage, s, d, p).start()

    def await_halo(stage, s, p):
        both_in(lambda d: halo_copy(stage, s, d, p).wait_recv())

    for copy in local:
        copy.wait()
    partners = (sizes[0] - 1) + (sizes[1] - 1)
    pl.semaphore_wait(barrier, partners + expected)

    send_sig(0)
    for s in range(2):
        @pl.loop(0, PC)
        def _(p):
            send_halo(0, s, p)
    pass_sig(0)

    lo_open = has_lo.astype(jnp.float32)
    hi_open = has_hi.astype(jnp.float32)

    def couple(k, s, below, above):
        xp = jnp.where(rows < N - 1, 0.5 * (s + up_row(s)), 0.0)
        yp = jnp.where(cols < N - 1, 0.5 * (s + up_col(s)), 0.0)
        xm, ym = down_row(xp), down_col(yp)
        diag = LEAK + (below + above) + (xp + xm) + (yp + ym)
        inv = 1.0 / diag
        for at, value in ((ZL, below), (ZH, above), (XM, xm), (XP, xp), (YM, ym), (YP, yp)):
            co[at, k] = value * inv
        if k in (1, 2):
            dg[k - 1] = diag
        di[k + 1] = inv

    both_in(lambda d: sig_copy(0, d).wait_recv())
    couple(1, cond[0], 0.5 * (cond[0] + sh[0, 1]) * lo_open, 0.5 * (cond[0] + cond[1]))
    couple(2, cond[1], 0.5 * (cond[0] + cond[1]), 0.5 * (cond[1] + sh[1, 0]) * hi_open)

    def apply(k, x, below, above):
        y = co[ZL, k] * below + co[ZH, k] * above
        y = y + co[XM, k] * down_row(x) + co[XP, k] * up_row(x)
        y = y + co[YM, k] * down_col(x) + co[YP, k] * up_col(x)
        return x - y

    def difference(p, first, second, plane, scale):
        here = (2 * v + plane) * PLANE
        plus = jnp.where(cell == elec[pats[first, p]] - here, scale, 0.0)
        return plus - jnp.where(cell == elec[pats[second, p]] - here, scale, 0.0)

    def probe(p, plane):
        return difference(p, 2, 3, plane, 1.0)

    def record(p, values):
        now = tile[...]
        for k, value in values:
            now = jnp.where((trow == p) & (tcol == k), value, now)
        tile[...] = now

    for s in range(2):
        @pl.loop(0, PC)
        def _(p):
            await_halo(0, s, p)
            a, b = warm[s, 0, p], warm[s, 1, p]
            e0 = -apply(1, a, xh[s, 0, p], b)
            e1 = -apply(2, b, a, xh[s, 1, p])
            if s == 0:
                e0 = e0 + difference(p, 0, 1, 0, strength) * di[2]
                e1 = e1 + difference(p, 0, 1, 1, strength) * di[3]
            d0[s, p, 0] = e0
            d0[s, p, 1] = e1
            send_halo(1, s, p)
            g0, g1 = probe(p, 0), probe(p, 1)
            rho = total(dg[0] * e0 * e0 + dg[1] * e1 * e1)
            ge = total(g0 * e0 + g1 * e1)
            if s == 0:
                record(p, ((F_RHO, rho), (F_D, ge), (F_X, total(g0 * a + g1 * b))))
            else:
                record(p, ((YY, rho), (GY, ge)))
            pass_on(0, s, p)

    send_sig(1)
    send_sig(2)

    for s in range(2):
        @pl.loop(0, PC)
        def _(p):
            await_halo(1, s, p)
            a, b = d0[s, p, 0], d0[s, p, 1]
            y0 = apply(1, a, dh[s, 0, p], b)
            y1 = apply(2, b, a, dh[s, 1, p])
            w0[s, p, 0] = y0
            w0[s, p, 1] = y1
            send_halo(2, s, p)
            u0, u1 = dg[0] * y0, dg[1] * y1
            mu = total(u0 * a + u1 * b)
            nu = total(u0 * y0 + u1 * y1)
            gy = total(probe(p, 0) * y0 + probe(p, 1) * y1)
            if s == 0:
                record(p, ((F_MU, mu), (F_NU, nu), (F_W, gy)))
            else:
                record(p, ((YY + 1, mu), (YY + 2, nu), (GY + 1, gy)))
            pass_on(1, s, p)

    pass_sig(1)
    pass_sig(2)
    both_in(lambda d: sig_copy(1, d).wait_recv())
    couple(0, sh[0, 1], 0.5 * (sh[0, 0] + sh[0, 1]), 0.5 * (cond[0] + sh[0, 1]) * lo_open)
    couple(3, sh[1, 0], 0.5 * (cond[1] + sh[1, 0]) * hi_open, 0.5 * (sh[1, 0] + sh[1, 1]))
    both_in(lambda d: sig_copy(2, d).wait_recv())
    di[0] = fh[0]
    di[5] = fh[1]

    @pl.loop(0, PC)
    def _(p):
        pass_on(2, 0, p)
        e = [probe(p, k - 2) * di[k] for k in range(6)]
        y = [apply(k, e[k + 1], e[k], e[k + 2]) for k in range(4)]
        for k in range(4):
            gd[p, k] = e[k + 1]
            gw[p, k] = y[k]
        z0, z1 = apply(1, y[1], y[0], y[2]), apply(2, y[2], y[1], y[3])
        g0, g1 = probe(p, 0), probe(p, 1)
        u0, u1 = dg[0] * y[1], dg[1] * y[2]
        record(p, (
            (GG, total(g0 * e[2] + g1 * e[3])),
            (GG + 1, total(g0 * y[1] + g1 * y[2])),
            (GG + 2, total(u0 * y[1] + u1 * y[2])),
            (GG + 3, total(u0 * z0 + u1 * z1)),
        ))

    for s in range(2):
        @pl.loop(0, PC)
        def _(p):
            if s == 0:
                pass_on(2, 1, p)
            await_halo(2, s, p)
            a, b = w0[s, p, 0], w0[s, p, 1]
            u0 = dg[0] * apply(1, a, wh[s, 0, p], b)
            u1 = dg[1] * apply(2, b, a, wh[s, 1, p])
            xi = total(a * u0 + b * u1)
            if s == 0:
                record(p, ((F_XI, xi),))
            else:
                k0, k1 = gw[p, 1], gw[p, 2]
                near = total(dg[0] * a * k0 + dg[1] * b * k1)
                record(p, ((YY + 3, xi), (GY + 2, near), (GY + 3, total(u0 * k0 + u1 * k1))))

    def sum_copy(stage, k, slot):
        return pltpu.make_async_remote_copy(
            red.at[stage, slot], red.at[stage, slot],
            red_s.at[stage, k], red_r.at[stage, slot],
            device_id=(q, member(stage, k)), device_id_type=MESH,
        )

    value = tile[...]
    for stage in range(2):
        mine, size = rank[stage], sizes[stage]
        red[stage, mine] = value
        for j in range(1, size):
            sum_copy(stage, lax.rem(mine + j, size), mine).start()
        for j in range(1, size):
            k = lax.rem(mine + j, size)
            sum_copy(stage, k, k).wait_recv()
        value = red[stage, 0]
        for k in range(1, size):
            value = value + red[stage, k]

    def column(k):
        return jnp.sum(jnp.where(tcol == k, value, 0.0), axis=1, keepdims=True)

    def steps(rho, mu, nu, xi):
        alpha = rho / mu
        rho1 = rho - 2.0 * alpha * mu + alpha * alpha * nu
        beta1 = 1.0 + rho1 / rho
        curve = beta1 * beta1 * mu - 2.0 * alpha * beta1 * nu + alpha * alpha * xi
        alpha1 = rho1 / curve
        return alpha + alpha1 * beta1, -alpha * alpha1

    c1, c2 = steps(column(F_RHO), column(F_MU), column(F_NU), column(F_XI))
    predicted = column(F_X) + c1 * column(F_D) + c2 * column(F_W)
    observed = jnp.zeros((PC, 1), jnp.float32)
    for p in range(PC):
        observed = jnp.where(trow[:, 0:1] == p, obs[p], observed)
    weight = data_weight * (predicted - observed)
    e1, e2 = steps(*(
        column(YY + k) + weight * (2.0 * column(GY + k) + weight * column(GG + k))
        for k in range(4)
    ))
    for k, factor in enumerate((c1, c2, e1, e2, e1 * weight, e2 * weight)):
        kc[k] = jnp.broadcast_to(factor, (PC, N))
    wide = jnp.where(trow == tcol, predicted, 0.0)
    pred_out[...] = jnp.sum(wide, axis=0, keepdims=True)[:, :PC]

    is_outer = (q == 0) | (q == npat - 1) if npat > 2 else q < 0
    is_inner = jnp.logical_not(is_outer)
    outward = jnp.where(q < middle, q - 1, q + 1)
    inward = jnp.where(q < middle, q + 1, q - 1)
    height = N // (PIECES // 2)

    def line_copy(leg, j):
        at = (j // (PIECES // 2), pl.ds(j % (PIECES // 2) * height, height))
        src = (gb, half, grad)[leg].at[at]
        dst = (lb[0], lb[1], grad)[leg].at[at]
        return pltpu.make_async_remote_copy(
            src, dst, ls.at[leg, j], lr.at[leg, j],
            device_id=(outward if leg == 2 else inward, v), device_id_type=MESH,
        )

    def piece(j):
        return j // (PIECES // 2), slice(j % (PIECES // 2) * height, (j % (PIECES // 2) + 1) * height)

    def field(p, s, k):
        if k in (0, 3):
            x, d, w = (h[s, k // 3, p] for h in (xh, dh, wh))
        else:
            x, d, w = warm[s, k - 1, p], d0[s, p, k - 1], w0[s, p, k - 1]
        out = x + kc[2 * s, pl.ds(p, 1), :] * d + kc[2 * s + 1, pl.ds(p, 1), :] * w
        if s == 1:
            out = out + kc[4, pl.ds(p, 1), :] * gd[p, k] + kc[5, pl.ds(p, 1), :] * gw[p, k]
        return out

    def within(plane, x, y):
        acc[3 + plane] += (up_row(x) - x) * (up_row(y) - y)
        acc[5 + plane] += (up_col(x) - x) * (up_col(y) - y)

    def finish(plane):
        lo, hi = acc[plane], acc[plane + 1]
        lo = lo * lo_open if plane == 0 else lo
        hi = hi * hi_open if plane == 1 else hi
        px = jnp.where(rows < N - 1, acc[3 + plane], 0.0)
        py = jnp.where(cols < N - 1, acc[5 + plane], 0.0)
        gb[plane] = -0.5 * ((lo + hi) + (px + down_row(px)) + (py + down_col(py)))

        @pl.when(is_outer)
        def _():
            for j in range(plane * PIECES // 2, (plane + 1) * PIECES // 2):
                line_copy(0, j).start()

    @pl.loop(0, PC)
    def _(p):
        f = [field(p, 0, k) for k in range(3)]
        a = [field(p, 1, k) for k in range(3)]
        top[0, p] = f[2]
        top[1, p] = a[2]
        for k in range(2):
            acc[k] += (f[k + 1] - f[k]) * (a[k + 1] - a[k])
        within(0, f[1], a[1])

    finish(0)

    @pl.loop(0, PC)
    def _(p):
        x, y = top[0, p], top[1, p]
        acc[2] += (field(p, 0, 3) - x) * (field(p, 1, 3) - y)
        within(1, x, y)

    finish(1)

    @pl.when(is_outer)
    def _():
        for j in range(PIECES):
            line_copy(2, j).wait_recv()
        for j in range(PIECES):
            line_copy(0, j).wait_send()

    @pl.when(is_inner)
    def _():
        for j in range(PIECES):
            at = piece(j)
            if npat > 2:
                line_copy(0, j).wait_recv()
                half[at] = gb[at] + lb[0][at]
            else:
                half[at] = gb[at]
            line_copy(1, j).start()
        for j in range(PIECES):
            at = piece(j)
            line_copy(1, j).wait_recv()
            grad[at] = half[at] + lb[1][at]
            if npat > 2:
                line_copy(2, j).start()
        for j in range(PIECES):
            line_copy(1, j).wait_send()
            if npat > 2:
                line_copy(2, j).wait_send()

    grad_out[...] = grad[...]

    for kind in range(3):
        both(lambda d: sig_copy(kind, d).wait_send())
        for d in range(2):
            @pl.when(crossing[d][3] & (v == crossing[d][2]))
            def _():
                sig_out(kind, d).wait_send()

    @pl.loop(0, PC)
    def _(p):
        for stage in range(3):
            for s in range(2):
                both(lambda d: halo_copy(stage, s, d, p).wait_send())
                for d in range(2):
                    @pl.when(crossing[d][3] & (v == crossing[d][2]))
                    def _():
                        detour_out(stage, s, d, p).wait_send()

    for stage in range(2):
        for j in range(1, sizes[stage]):
            sum_copy(stage, lax.rem(rank[stage] + j, sizes[stage]), rank[stage]).wait_send()


def solution(mesh):
    npat, layers = mesh.shape["pat"], mesh.shape["vox"]
    group = 8 if layers >= 64 else 2

    def per_device(conductivity, warm_forward, warm_adjoint, electrodes, patterns, observed):
        planes = conductivity.shape[0]
        strength = 2.0 * math.sqrt(layers * planes * PLANE)
        vmem = pl.BlockSpec(memory_space=pltpu.VMEM)
        smem = pl.BlockSpec(memory_space=pltpu.SMEM)
        hbm = pl.BlockSpec(memory_space=pltpu.HBM)
        f32 = jnp.float32
        dma = pltpu.SemaphoreType.DMA
        groups = layers // group
        widest = max(group, groups)
        gradient, predicted = pl.pallas_call(
            functools.partial(kernel, npat, layers, group, strength),
            out_shape=(
                jax.ShapeDtypeStruct((2, N, N), f32),
                jax.ShapeDtypeStruct((1, PC), f32),
            ),
            in_specs=[hbm, hbm, hbm, smem, smem, smem],
            out_specs=(vmem, vmem),
            scratch_shapes=[
                pltpu.VMEM((2, N, N), f32),
                pltpu.VMEM((2, 2, PC, N, N), f32),
                pltpu.VMEM((2, 2, N, N), f32),
                pltpu.VMEM((2, N, N), f32),
                pltpu.VMEM((2, 2, PC, N, N), f32),
                pltpu.VMEM((2, 2, PC, N, N), f32),
                pltpu.VMEM((2, 2, PC, N, N), f32),
                pltpu.VMEM((2, PC, 2, N, N), f32),
                pltpu.VMEM((2, PC, 2, N, N), f32),
                pltpu.VMEM((PC, 4, N, N), f32),
                pltpu.VMEM((PC, 4, N, N), f32),
                pltpu.VMEM((3, 2 * PC, N, N), f32),
                pltpu.VMEM((3, N, N), f32),
                pltpu.VMEM((6, 4, N, N), f32),
                pltpu.VMEM((2, N, N), f32),
                pltpu.VMEM((6, N, N), f32),
                pltpu.VMEM((7, N, N), f32),
                pltpu.VMEM((2, PC, N, N), f32),
                pltpu.VMEM((PC, N), f32),
                pltpu.VMEM((2, widest, PC, N), f32),
                pltpu.VMEM((6, PC, N), f32),
                pltpu.VMEM((2, N, N), f32),
                pltpu.VMEM((2, N, N), f32),
                pltpu.VMEM((2, N, N), f32),
                pltpu.VMEM((2, N, N), f32),
                pltpu.VMEM((2, N, N), f32),
                dma((3,)),
                dma((3, 2)),
                dma((3, 2)),
                dma((3,)),
                dma((3,)),
                dma((3, 2, 2, PC)),
                dma((3, 2, 2, PC)),
                dma((3, 2 * PC)),
                dma((3, 2 * PC)),
                dma((2, widest)),
                dma((2, widest)),
                dma((3, PIECES)),
                dma((3, PIECES)),
            ],
            compiler_params=pltpu.CompilerParams(
                collective_id=0, has_side_effects=True, vmem_limit_bytes=int(53.7 * 2**20)
            ),
            name="ert_gradient",
        )(conductivity, warm_forward, warm_adjoint, electrodes, patterns.T, observed)
        return gradient, predicted.reshape(PC)

    in_specs = (
        P("vox", None, None),
        P("vox", "pat", None, None),
        P("vox", "pat", None, None),
        P(),
        P("pat", None),
        P("pat"),
    )
    return jax.shard_map(
        per_device,
        mesh=mesh,
        in_specs=in_specs,
        out_specs=(P("vox", None, None), P("pat")),
        check_vma=False,
    )
```

```python
import functools
import math

import jax
import jax.numpy as jnp
from jax import lax
from jax.experimental import pallas as pl
from jax.experimental.pallas import tpu as pltpu
from jax.sharding import PartitionSpec as P

MESH = pl.DeviceIdType.MESH
LEAK = 0.05
N = 128
PLANE = N * N
PC = 8
PIECES = 8

ZL, ZH, XM, XP, YM, YP = range(6)
F_RHO, F_MU, F_NU, F_XI, F_X, F_D, F_W = range(7)
YY, GY, GG = 7, 11, 15


def up_row(x):
    return pltpu.roll(x, N - 1, 0)


def down_row(x):
    return pltpu.roll(x, 1, 0)


def up_col(x):
    return pltpu.roll(x, N - 1, 1)


def down_col(x):
    return pltpu.roll(x, 1, 1)


def total(x):
    part = jnp.sum(x.reshape(N // 8, 8, N), axis=0)
    return jnp.sum(jnp.sum(part, axis=1, keepdims=True), axis=0, keepdims=True)


def kernel(
    npat,
    layers,
    group,
    strength,
    cond_in,
    wf_in,
    wa_in,
    elec_in,
    pats_in,
    obs_in,
    grad_out,
    pred_out,
    cond,
    warm,
    elec,
    pats,
    obs,
    sh,
    fh,
    xh,
    dh,
    wh,
    d0,
    w0,
    gd,
    gw,
    rb,
    sb,
    co,
    dg,
    di,
    acc,
    top,
    tile,
    red,
    kc,
    gb,
    lb_outer,
    lb_inner,
    half,
    grad,
    in_s,
    sig_s,
    sig_r,
    sig_rr,
    sig_rq,
    hs,
    hr,
    rr,
    rq,
    red_s,
    red_r,
    ls,
    lr,
):
    lb = (lb_outer, lb_inner)
    q = lax.axis_index("pat")
    v = lax.axis_index("vox")
    last = layers - 1
    has_lo = v > 0
    has_hi = v < last
    groups = layers // group
    rank = (lax.rem(v, group), v // group)
    sizes = (group, groups)
    data_weight = 0.1 * strength
    lower, upper = layers // 2 - 1, layers // 2
    middle = npat // 2
    inner = (q >= middle - 1) & (q <= middle) if npat > 2 else q == 0
    crossing = (
        (lower, upper, 0, inner),
        (upper, lower, last, jnp.logical_not(inner)),
    )

    local = [
        pltpu.make_async_copy(cond_in, cond, in_s.at[0]),
        pltpu.make_async_copy(wf_in, warm.at[0], in_s.at[1]),
        pltpu.make_async_copy(wa_in, warm.at[1], in_s.at[2]),
        pltpu.make_async_copy(elec_in, elec, in_s.at[3]),
        pltpu.make_async_copy(pats_in, pats, in_s.at[4]),
        pltpu.make_async_copy(obs_in, obs, in_s.at[5]),
    ]

    def member(stage, k):
        return (v // group) * group + k if stage == 0 else k * group + lax.rem(v, group)

    barrier = pltpu.get_barrier_semaphore()

    def greet(device):
        pl.semaphore_signal(barrier, inc=1, device_id=device, device_id_type=MESH)

    @pl.when(has_lo)
    def _():
        greet((q, v - 1))

    @pl.when(has_hi)
    def _():
        greet((q, v + 1))

    expected = has_lo.astype(jnp.int32) + has_hi.astype(jnp.int32)
    for source, target, via, taken in crossing:
        on_path = taken & ((v == source) | (v == target))

        @pl.when(on_path)
        def _():
            greet((q, via))

        @pl.when(taken & (v == via))
        def _():
            greet((q, source))
            greet((q, target))

        expected = expected + on_path.astype(jnp.int32)
        expected = expected + 2 * (taken & (v == via)).astype(jnp.int32)

    for stage in range(2):
        for j in range(1, sizes[stage]):
            greet((q, member(stage, lax.rem(rank[stage] + j, sizes[stage]))))
    below, above = q > 0, q < npat - 1

    @pl.when(below)
    def _():
        greet((q - 1, v))

    @pl.when(above)
    def _():
        greet((q + 1, v))

    expected = expected + below.astype(jnp.int32) + above.astype(jnp.int32)
    for copy in local:
        copy.start()

    rows = lax.broadcasted_iota(jnp.int32, (N, N), 0)
    cols = lax.broadcasted_iota(jnp.int32, (N, N), 1)
    cell = rows * N + cols
    trow = lax.broadcasted_iota(jnp.int32, (PC, N), 0)
    tcol = lax.broadcasted_iota(jnp.int32, (PC, N), 1)
    blank = jnp.zeros((N, N), jnp.float32)

    for d, outside in enumerate((jnp.logical_not(has_lo), jnp.logical_not(has_hi))):
        @pl.when(outside)
        def _():
            sh[d, 0] = blank
            sh[d, 1] = blank
            fh[d] = blank

            @pl.loop(0, PC)
            def _(p):
                for s in range(2):
                    for h in (xh, dh, wh):
                        h[s, d, p] = blank

    tile[...] = jnp.zeros((PC, N), jnp.float32)
    for k in range(7):
        acc[k] = blank

    def neighbour(d):
        return (q, v + 1 - 2 * d)

    def sig_ends(kind, d):
        if kind == 2:
            return di.at[2 + d], fh.at[d]
        plane = (1 - d, d)[kind]
        return cond.at[plane], sh.at[d, plane]

    def sig_copy(kind, d):
        src, dst = sig_ends(kind, d)
        return pltpu.make_async_remote_copy(
            src, dst, sig_s.at[kind, d], sig_r.at[kind, d],
            device_id=neighbour(d), device_id_type=MESH,
        )

    def sig_in(kind, d):
        return pltpu.make_async_remote_copy(
            sig_ends(kind, d)[0], sb.at[kind], sig_s.at[kind, d], sig_rr.at[kind],
            device_id=(q, crossing[d][2]), device_id_type=MESH,
        )

    def sig_out(kind, d):
        return pltpu.make_async_remote_copy(
            sb.at[kind], sig_ends(kind, d)[1], sig_rq.at[kind], sig_r.at[kind, d],
            device_id=(q, crossing[d][1]), device_id_type=MESH,
        )

    def outgoing(stage, s, d, p):
        plane = 1 - d
        if stage == 0:
            return warm.at[s, plane, p]
        return (d0 if stage == 1 else w0).at[s, p, plane]

    def incoming(stage, s, d, p):
        return (xh, dh, wh)[stage].at[s, d, p]

    def halo_copy(stage, s, d, p):
        return pltpu.make_async_remote_copy(
            outgoing(stage, s, d, p), incoming(stage, s, d, p),
            hs.at[stage, s, d, p], hr.at[stage, s, d, p],
            device_id=neighbour(d), device_id_type=MESH,
        )

    def detour_in(stage, s, d, p):
        at = s * PC + p
        return pltpu.make_async_remote_copy(
            outgoing(stage, s, d, p), rb.at[stage, at],
            hs.at[stage, s, d, p], rr.at[stage, at],
            device_id=(q, crossing[d][2]), device_id_type=MESH,
        )

    def detour_out(stage, s, d, p):
        at = s * PC + p
        return pltpu.make_async_remote_copy(
            rb.at[stage, at], incoming(stage, s, d, p),
            rq.at[stage, at], hr.at[stage, s, d, p],
            device_id=(q, crossing[d][1]), device_id_type=MESH,
        )

    exists = (has_hi, has_lo)

    def both(fn):
        for d in range(2):
            @pl.when(exists[d])
            def _():
                fn(d)

    def both_in(fn):
        for d in range(2):
            @pl.when(exists[1 - d])
            def _():
                fn(d)

    def send_sig(kind):
        for d in range(2):
            around = crossing[d][3] & (v == crossing[d][0])

            @pl.when(exists[d] & jnp.logical_not(around))
            def _():
                sig_copy(kind, d).start()

            @pl.when(around)
            def _():
                sig_in(kind, d).start()

    def pass_sig(kind):
        for d in range(2):
            @pl.when(crossing[d][3] & (v == crossing[d][2]))
            def _():
                sig_in(kind, d).wait_recv()
                sig_out(kind, d).start()

    def send_halo(stage, s, p):
        for d in range(2):
            around = crossing[d][3] & (v == crossing[d][0])

            @pl.when(exists[d] & jnp.logical_not(around))
            def _():
                halo_copy(stage, s, d, p).start()

            @pl.when(around)
            def _():
                detour_in(stage, s, d, p).start()

    def pass_on(stage, s, p):
        for d in range(2):
            @pl.when(crossing[d][3] & (v == crossing[d][2]))
            def _():
                detour_in(stage, s, d, p).wait_recv()
                detour_out(stage, s, d, p).start()

    def await_halo(stage, s, p):
        both_in(lambda d: halo_copy(stage, s, d, p).wait_recv())

    for copy in local:
        copy.wait()
    partners = (sizes[0] - 1) + (sizes[1] - 1)
    pl.semaphore_wait(barrier, partners + expected)

    send_sig(0)
    for s in range(2):
        @pl.loop(0, PC)
        def _(p):
            send_halo(0, s, p)
    pass_sig(0)

    lo_open = has_lo.astype(jnp.float32)
    hi_open = has_hi.astype(jnp.float32)

    def couple(k, s, below, above):
        xp = jnp.where(rows < N - 1, 0.5 * (s + up_row(s)), 0.0)
        yp = jnp.where(cols < N - 1, 0.5 * (s + up_col(s)), 0.0)
        xm, ym = down_row(xp), down_col(yp)
        diag = LEAK + (below + above) + (xp + xm) + (yp + ym)
        inv = 1.0 / diag
        for at, value in ((ZL, below), (ZH, above), (XM, xm), (XP, xp), (YM, ym), (YP, yp)):
            co[at, k] = value * inv
        if k in (1, 2):
            dg[k - 1] = diag
        di[k + 1] = inv

    both_in(lambda d: sig_copy(0, d).wait_recv())
    couple(1, cond[0], 0.5 * (cond[0] + sh[0, 1]) * lo_open, 0.5 * (cond[0] + cond[1]))
    couple(2, cond[1], 0.5 * (cond[0] + cond[1]), 0.5 * (cond[1] + sh[1, 0]) * hi_open)

    def apply(k, x, below, above):
        y = co[ZL, k] * below + co[ZH, k] * above
        y = y + co[XM, k] * down_row(x) + co[XP, k] * up_row(x)
        y = y + co[YM, k] * down_col(x) + co[YP, k] * up_col(x)
        return x - y

    def difference(p, first, second, plane, scale):
        here = (2 * v + plane) * PLANE
        plus = jnp.where(cell == elec[pats[first, p]] - here, scale, 0.0)
        return plus - jnp.where(cell == elec[pats[second, p]] - here, scale, 0.0)

    def probe(p, plane):
        return difference(p, 2, 3, plane, 1.0)

    def record(p, values):
        now = tile[...]
        for k, value in values:
            now = jnp.where((trow == p) & (tcol == k), value, now)
        tile[...] = now

    for s in range(2):
        @pl.loop(0, PC)
        def _(p):
            await_halo(0, s, p)
            a, b = warm[s, 0, p], warm[s, 1, p]
            e0 = -apply(1, a, xh[s, 0, p], b)
            e1 = -apply(2, b, a, xh[s, 1, p])
            if s == 0:
                e0 = e0 + difference(p, 0, 1, 0, strength) * di[2]
                e1 = e1 + difference(p, 0, 1, 1, strength) * di[3]
            d0[s, p, 0] = e0
            d0[s, p, 1] = e1
            send_halo(1, s, p)
            g0, g1 = probe(p, 0), probe(p, 1)
            rho = total(dg[0] * e0 * e0 + dg[1] * e1 * e1)
            ge = total(g0 * e0 + g1 * e1)
            if s == 0:
                record(p, ((F_RHO, rho), (F_D, ge), (F_X, total(g0 * a + g1 * b))))
            else:
                record(p, ((YY, rho), (GY, ge)))
            pass_on(0, s, p)

    send_sig(1)
    send_sig(2)

    for s in range(2):
        @pl.loop(0, PC)
        def _(p):
            await_halo(1, s, p)
            a, b = d0[s, p, 0], d0[s, p, 1]
            y0 = apply(1, a, dh[s, 0, p], b)
            y1 = apply(2, b, a, dh[s, 1, p])
            w0[s, p, 0] = y0
            w0[s, p, 1] = y1
            send_halo(2, s, p)
            u0, u1 = dg[0] * y0, dg[1] * y1
            mu = total(u0 * a + u1 * b)
            nu = total(u0 * y0 + u1 * y1)
            gy = total(probe(p, 0) * y0 + probe(p, 1) * y1)
            if s == 0:
                record(p, ((F_MU, mu), (F_NU, nu), (F_W, gy)))
            else:
                record(p, ((YY + 1, mu), (YY + 2, nu), (GY + 1, gy)))
            pass_on(1, s, p)

    pass_sig(1)
    pass_sig(2)
    both_in(lambda d: sig_copy(1, d).wait_recv())
    couple(0, sh[0, 1], 0.5 * (sh[0, 0] + sh[0, 1]), 0.5 * (cond[0] + sh[0, 1]) * lo_open)
    couple(3, sh[1, 0], 0.5 * (cond[1] + sh[1, 0]) * hi_open, 0.5 * (sh[1, 0] + sh[1, 1]))
    both_in(lambda d: sig_copy(2, d).wait_recv())
    di[0] = fh[0]
    di[5] = fh[1]

    @pl.loop(0, PC)
    def _(p):
        pass_on(2, 0, p)
        e = [probe(p, k - 2) * di[k] for k in range(6)]
        y = [apply(k, e[k + 1], e[k], e[k + 2]) for k in range(4)]
        for k in range(4):
            gd[p, k] = e[k + 1]
            gw[p, k] = y[k]
        z0, z1 = apply(1, y[1], y[0], y[2]), apply(2, y[2], y[1], y[3])
        g0, g1 = probe(p, 0), probe(p, 1)
        u0, u1 = dg[0] * y[1], dg[1] * y[2]
        record(p, (
            (GG, total(g0 * e[2] + g1 * e[3])),
            (GG + 1, total(g0 * y[1] + g1 * y[2])),
            (GG + 2, total(u0 * y[1] + u1 * y[2])),
            (GG + 3, total(u0 * z0 + u1 * z1)),
        ))

    for s in range(2):
        @pl.loop(0, PC)
        def _(p):
            if s == 0:
                pass_on(2, 1, p)
            await_halo(2, s, p)
            a, b = w0[s, p, 0], w0[s, p, 1]
            u0 = dg[0] * apply(1, a, wh[s, 0, p], b)
            u1 = dg[1] * apply(2, b, a, wh[s, 1, p])
            xi = total(a * u0 + b * u1)
            if s == 0:
                record(p, ((F_XI, xi),))
            else:
                k0, k1 = gw[p, 1], gw[p, 2]
                near = total(dg[0] * a * k0 + dg[1] * b * k1)
                record(p, ((YY + 3, xi), (GY + 2, near), (GY + 3, total(u0 * k0 + u1 * k1))))

    def sum_copy(stage, k, slot):
        return pltpu.make_async_remote_copy(
            red.at[stage, slot], red.at[stage, slot],
            red_s.at[stage, k], red_r.at[stage, slot],
            device_id=(q, member(stage, k)), device_id_type=MESH,
        )

    def halos_have_left():
        for kind in range(3):
            both(lambda d: sig_copy(kind, d).wait_send())
            for d in range(2):
                @pl.when(crossing[d][3] & (v == crossing[d][2]))
                def _():
                    sig_out(kind, d).wait_send()

        @pl.loop(0, PC)
        def _(p):
            for stage in range(3):
                for s in range(2):
                    both(lambda d: halo_copy(stage, s, d, p).wait_send())
                    for d in range(2):
                        @pl.when(crossing[d][3] & (v == crossing[d][2]))
                        def _():
                            detour_out(stage, s, d, p).wait_send()

    value = tile[...]
    for stage in range(2):
        mine, size = rank[stage], sizes[stage]
        red[stage, mine] = value
        for j in range(1, size):
            sum_copy(stage, lax.rem(mine + j, size), mine).start()
        if stage == 1:
            halos_have_left()
        for j in range(1, size):
            k = lax.rem(mine + j, size)
            sum_copy(stage, k, k).wait_recv()
        value = red[stage, 0]
        for k in range(1, size):
            value = value + red[stage, k]

    def column(k):
        return jnp.sum(jnp.where(tcol == k, value, 0.0), axis=1, keepdims=True)

    def steps(rho, mu, nu, xi):
        alpha = rho / mu
        rho1 = rho - 2.0 * alpha * mu + alpha * alpha * nu
        beta1 = 1.0 + rho1 / rho
        curve = beta1 * beta1 * mu - 2.0 * alpha * beta1 * nu + alpha * alpha * xi
        alpha1 = rho1 / curve
        return alpha + alpha1 * beta1, -alpha * alpha1

    c1, c2 = steps(column(F_RHO), column(F_MU), column(F_NU), column(F_XI))
    predicted = column(F_X) + c1 * column(F_D) + c2 * column(F_W)
    observed = jnp.zeros((PC, 1), jnp.float32)
    for p in range(PC):
        observed = jnp.where(trow[:, 0:1] == p, obs[p], observed)
    weight = data_weight * (predicted - observed)
    e1, e2 = steps(*(
        column(YY + k) + weight * (2.0 * column(GY + k) + weight * column(GG + k))
        for k in range(4)
    ))
    for k, factor in enumerate((c1, c2, e1, e2, e1 * weight, e2 * weight)):
        kc[k] = jnp.broadcast_to(factor, (PC, N))
    wide = jnp.where(trow == tcol, predicted, 0.0)
    pred_out[...] = jnp.sum(wide, axis=0, keepdims=True)[:, :PC]

    is_outer = (q == 0) | (q == npat - 1) if npat > 2 else q < 0
    is_inner = jnp.logical_not(is_outer)
    outward = jnp.where(q < middle, q - 1, q + 1)
    inward = jnp.where(q < middle, q + 1, q - 1)
    height = N // (PIECES // 2)

    def line_copy(leg, j):
        at = (j // (PIECES // 2), pl.ds(j % (PIECES // 2) * height, height))
        src = (gb, half, grad)[leg].at[at]
        dst = (lb[0], lb[1], grad)[leg].at[at]
        return pltpu.make_async_remote_copy(
            src, dst, ls.at[leg, j], lr.at[leg, j],
            device_id=(outward if leg == 2 else inward, v), device_id_type=MESH,
        )

    def piece(j):
        return j // (PIECES // 2), slice(j % (PIECES // 2) * height, (j % (PIECES // 2) + 1) * height)

    def field(p, s, k):
        if k in (0, 3):
            x, d, w = (h[s, k // 3, p] for h in (xh, dh, wh))
        else:
            x, d, w = warm[s, k - 1, p], d0[s, p, k - 1], w0[s, p, k - 1]
        out = x + kc[2 * s, pl.ds(p, 1), :] * d + kc[2 * s + 1, pl.ds(p, 1), :] * w
        if s == 1:
            out = out + kc[4, pl.ds(p, 1), :] * gd[p, k] + kc[5, pl.ds(p, 1), :] * gw[p, k]
        return out

    def within(plane, x, y):
        acc[3 + plane] += (up_row(x) - x) * (up_row(y) - y)
        acc[5 + plane] += (up_col(x) - x) * (up_col(y) - y)

    def finish(plane):
        lo, hi = acc[plane], acc[plane + 1]
        lo = lo * lo_open if plane == 0 else lo
        hi = hi * hi_open if plane == 1 else hi
        px = jnp.where(rows < N - 1, acc[3 + plane], 0.0)
        py = jnp.where(cols < N - 1, acc[5 + plane], 0.0)
        gb[plane] = -0.5 * ((lo + hi) + (px + down_row(px)) + (py + down_col(py)))

        @pl.when(is_outer)
        def _():
            for j in range(plane * PIECES // 2, (plane + 1) * PIECES // 2):
                line_copy(0, j).start()

    @pl.loop(0, PC)
    def _(p):
        f = [field(p, 0, k) for k in range(3)]
        a = [field(p, 1, k) for k in range(3)]
        top[0, p] = f[2]
        top[1, p] = a[2]
        for k in range(2):
            acc[k] += (f[k + 1] - f[k]) * (a[k + 1] - a[k])
        within(0, f[1], a[1])

    finish(0)

    @pl.loop(0, PC)
    def _(p):
        x, y = top[0, p], top[1, p]
        acc[2] += (field(p, 0, 3) - x) * (field(p, 1, 3) - y)
        within(1, x, y)

    finish(1)

    @pl.when(is_outer)
    def _():
        for j in range(PIECES):
            line_copy(2, j).wait_recv()
        for j in range(PIECES):
            line_copy(0, j).wait_send()

    @pl.when(is_inner)
    def _():
        for j in range(PIECES):
            at = piece(j)
            if npat > 2:
                line_copy(0, j).wait_recv()
                half[at] = gb[at] + lb[0][at]
            else:
                half[at] = gb[at]
            line_copy(1, j).start()
        for j in range(PIECES):
            at = piece(j)
            line_copy(1, j).wait_recv()
            grad[at] = half[at] + lb[1][at]
            if npat > 2:
                line_copy(2, j).start()
        for j in range(PIECES):
            line_copy(1, j).wait_send()
            if npat > 2:
                line_copy(2, j).wait_send()

    grad_out[...] = grad[...]

    for stage in range(2):
        for j in range(1, sizes[stage]):
            sum_copy(stage, lax.rem(rank[stage] + j, sizes[stage]), rank[stage]).wait_send()


def solution(mesh):
    npat, layers = mesh.shape["pat"], mesh.shape["vox"]
    group = 8 if layers >= 64 else 2

    def per_device(conductivity, warm_forward, warm_adjoint, electrodes, patterns, observed):
        planes = conductivity.shape[0]
        strength = 2.0 * math.sqrt(layers * planes * PLANE)
        vmem = pl.BlockSpec(memory_space=pltpu.VMEM)
        hbm = pl.BlockSpec(memory_space=pltpu.HBM)
        f32 = jnp.float32
        dma = pltpu.SemaphoreType.DMA
        groups = layers // group
        widest = max(group, groups)
        gradient, predicted = pl.pallas_call(
            functools.partial(kernel, npat, layers, group, strength),
            out_shape=(
                jax.ShapeDtypeStruct((2, N, N), f32),
                jax.ShapeDtypeStruct((1, PC), f32),
            ),
            in_specs=[hbm] * 6,
            out_specs=(vmem, vmem),
            scratch_shapes=[
                pltpu.VMEM((2, N, N), f32),
                pltpu.VMEM((2, 2, PC, N, N), f32),
                pltpu.SMEM(electrodes.shape, jnp.int32),
                pltpu.SMEM((4, PC), jnp.int32),
                pltpu.SMEM((PC,), f32),
                pltpu.VMEM((2, 2, N, N), f32),
                pltpu.VMEM((2, N, N), f32),
                pltpu.VMEM((2, 2, PC, N, N), f32),
                pltpu.VMEM((2, 2, PC, N, N), f32),
                pltpu.VMEM((2, 2, PC, N, N), f32),
                pltpu.VMEM((2, PC, 2, N, N), f32),
                pltpu.VMEM((2, PC, 2, N, N), f32),
                pltpu.VMEM((PC, 4, N, N), f32),
                pltpu.VMEM((PC, 4, N, N), f32),
                pltpu.VMEM((3, 2 * PC, N, N), f32),
                pltpu.VMEM((3, N, N), f32),
                pltpu.VMEM((6, 4, N, N), f32),
                pltpu.VMEM((2, N, N), f32),
                pltpu.VMEM((6, N, N), f32),
                pltpu.VMEM((7, N, N), f32),
                pltpu.VMEM((2, PC, N, N), f32),
                pltpu.VMEM((PC, N), f32),
                pltpu.VMEM((2, widest, PC, N), f32),
                pltpu.VMEM((6, PC, N), f32),
                pltpu.VMEM((2, N, N), f32),
                pltpu.VMEM((2, N, N), f32),
                pltpu.VMEM((2, N, N), f32),
                pltpu.VMEM((2, N, N), f32),
                pltpu.VMEM((2, N, N), f32),
                dma((6,)),
                dma((3, 2)),
                dma((3, 2)),
                dma((3,)),
                dma((3,)),
                dma((3, 2, 2, PC)),
                dma((3, 2, 2, PC)),
                dma((3, 2 * PC)),
                dma((3, 2 * PC)),
                dma((2, widest)),
                dma((2, widest)),
                dma((3, PIECES)),
                dma((3, PIECES)),
            ],
            compiler_params=pltpu.CompilerParams(
                collective_id=0, has_side_effects=True, vmem_limit_bytes=48 * 2**20
            ),
            name="ert_gradient",
        )(*(
            pltpu.with_memory_space_constraint(x, pltpu.HBM)
            for x in (conductivity, warm_forward, warm_adjoint, electrodes, patterns.T, observed)
        ))
        return gradient, predicted.reshape(PC)

    in_specs = (
        P("vox", None, None),
        P("vox", "pat", None, None),
        P("vox", "pat", None, None),
        P(),
        P("pat", None),
        P("pat"),
    )
    return jax.shard_map(
        per_device,
        mesh=mesh,
        in_specs=in_specs,
        out_specs=(P("vox", None, None), P("pat")),
        check_vma=False,
    )
```

```python
import functools
import math

import jax
import jax.numpy as jnp
from jax import lax
from jax.experimental import pallas as pl
from jax.experimental.pallas import tpu as pltpu
from jax.sharding import PartitionSpec as P

MESH = pl.DeviceIdType.MESH
LEAK = 0.05
N = 128
PLANE = N * N
PC = 8
PIECES = 8

ZL, ZH, XM, XP, YM, YP = range(6)
F_RHO, F_MU, F_NU, F_XI, F_X, F_D, F_W = range(7)
YY, GY, GG = 7, 11, 15


def up_row(x):
    return pltpu.roll(x, N - 1, 0)


def down_row(x):
    return pltpu.roll(x, 1, 0)


def up_col(x):
    return pltpu.roll(x, N - 1, 1)


def down_col(x):
    return pltpu.roll(x, 1, 1)


def total(x):
    part = jnp.sum(x.reshape(N // 8, 8, N), axis=0)
    return jnp.sum(jnp.sum(part, axis=1, keepdims=True), axis=0, keepdims=True)


def kernel(
    npat,
    layers,
    group,
    strength,
    cond_in,
    wf_in,
    wa_in,
    elec_in,
    pats_in,
    obs_in,
    grad_out,
    pred_out,
    cond,
    warm,
    elec,
    pats,
    obs,
    sh,
    fh,
    xh,
    dh,
    wh,
    d0,
    w0,
    gd,
    gw,
    rb,
    sb,
    co,
    dg,
    di,
    acc,
    top,
    tile,
    red,
    kc,
    gb,
    lb_outer,
    lb_inner,
    half,
    grad,
    in_s,
    sig_s,
    sig_r,
    sig_rr,
    sig_rq,
    hs,
    hr,
    rr,
    rq,
    red_s,
    red_r,
    ls,
    lr,
):
    lb = (lb_outer, lb_inner)
    q = lax.axis_index("pat")
    v = lax.axis_index("vox")
    last = layers - 1
    has_lo = v > 0
    has_hi = v < last
    groups = layers // group
    rank = (lax.rem(v, group), v // group)
    sizes = (group, groups)
    data_weight = 0.1 * strength
    lower, upper = layers // 2 - 1, layers // 2
    middle = npat // 2
    inner = (q >= middle - 1) & (q <= middle) if npat > 2 else q == 0
    crossing = (
        (lower, upper, 0, inner),
        (upper, lower, last, jnp.logical_not(inner)),
    )
    aside = jnp.where(inner, 6, 24) if layers == 64 else 0
    beside = (aside, upper + aside if layers == 64 else last)

    local = [
        pltpu.make_async_copy(cond_in, cond, in_s.at[0]),
        pltpu.make_async_copy(wf_in, warm.at[0], in_s.at[1]),
        pltpu.make_async_copy(wa_in, warm.at[1], in_s.at[2]),
        pltpu.make_async_copy(elec_in, elec, in_s.at[3]),
        pltpu.make_async_copy(pats_in, pats, in_s.at[4]),
        pltpu.make_async_copy(obs_in, obs, in_s.at[5]),
    ]

    def member(stage, k):
        return (v // group) * group + k if stage == 0 else k * group + lax.rem(v, group)

    barrier = pltpu.get_barrier_semaphore()

    def greet(device):
        pl.semaphore_signal(barrier, inc=1, device_id=device, device_id_type=MESH)

    @pl.when(has_lo)
    def _():
        greet((q, v - 1))

    @pl.when(has_hi)
    def _():
        greet((q, v + 1))

    expected = has_lo.astype(jnp.int32) + has_hi.astype(jnp.int32)
    for source, target, via, taken in crossing:
        on_path = taken & ((v == source) | (v == target))

        @pl.when(on_path)
        def _():
            greet((q, via))

        @pl.when(taken & (v == via))
        def _():
            greet((q, source))
            greet((q, target))

        expected = expected + on_path.astype(jnp.int32)
        expected = expected + 2 * (taken & (v == via)).astype(jnp.int32)

    for d in range(2):
        source, target = crossing[d][:2]
        at_end, at_via = (v == source) | (v == target), v == beside[d]

        @pl.when(at_end)
        def _():
            greet((q, beside[d]))

        @pl.when(at_via)
        def _():
            greet((q, source))
            greet((q, target))

        expected = expected + at_end.astype(jnp.int32) + 2 * at_via.astype(jnp.int32)

    for stage in range(2):
        for j in range(1, sizes[stage]):
            greet((q, member(stage, lax.rem(rank[stage] + j, sizes[stage]))))
    below, above = q > 0, q < npat - 1

    @pl.when(below)
    def _():
        greet((q - 1, v))

    @pl.when(above)
    def _():
        greet((q + 1, v))

    expected = expected + below.astype(jnp.int32) + above.astype(jnp.int32)
    for copy in local:
        copy.start()

    rows = lax.broadcasted_iota(jnp.int32, (N, N), 0)
    cols = lax.broadcasted_iota(jnp.int32, (N, N), 1)
    cell = rows * N + cols
    trow = lax.broadcasted_iota(jnp.int32, (PC, N), 0)
    tcol = lax.broadcasted_iota(jnp.int32, (PC, N), 1)
    blank = jnp.zeros((N, N), jnp.float32)

    for d, outside in enumerate((jnp.logical_not(has_lo), jnp.logical_not(has_hi))):
        @pl.when(outside)
        def _():
            sh[d, 0] = blank
            sh[d, 1] = blank
            fh[d] = blank

            @pl.loop(0, PC)
            def _(p):
                for s in range(2):
                    for h in (xh, dh, wh):
                        h[s, d, p] = blank

    tile[...] = jnp.zeros((PC, N), jnp.float32)
    for k in range(7):
        acc[k] = blank

    def neighbour(d):
        return (q, v + 1 - 2 * d)

    def sig_ends(kind, d):
        if kind == 2:
            return di.at[2 + d], fh.at[d]
        plane = (1 - d, d)[kind]
        return cond.at[plane], sh.at[d, plane]

    def sig_copy(kind, d):
        src, dst = sig_ends(kind, d)
        return pltpu.make_async_remote_copy(
            src, dst, sig_s.at[kind, d], sig_r.at[kind, d],
            device_id=neighbour(d), device_id_type=MESH,
        )

    def sig_via(kind, d):
        return beside[d] if kind else crossing[d][2]

    def sig_detour(kind, d, at):
        return v == at if kind else crossing[d][3] & (v == at)

    def sig_in(kind, d):
        return pltpu.make_async_remote_copy(
            sig_ends(kind, d)[0], sb.at[kind], sig_s.at[kind, d], sig_rr.at[kind],
            device_id=(q, sig_via(kind, d)), device_id_type=MESH,
        )

    def sig_out(kind, d):
        return pltpu.make_async_remote_copy(
            sb.at[kind], sig_ends(kind, d)[1], sig_rq.at[kind], sig_r.at[kind, d],
            device_id=(q, crossing[d][1]), device_id_type=MESH,
        )

    def outgoing(stage, s, d, p):
        plane = 1 - d
        if stage == 0:
            return warm.at[s, plane, p]
        return (d0 if stage == 1 else w0).at[s, p, plane]

    def incoming(stage, s, d, p):
        return (xh, dh, wh)[stage].at[s, d, p]

    def halo_copy(stage, s, d, p):
        return pltpu.make_async_remote_copy(
            outgoing(stage, s, d, p), incoming(stage, s, d, p),
            hs.at[stage, s, d, p], hr.at[stage, s, d, p],
            device_id=neighbour(d), device_id_type=MESH,
        )

    def detour_in(stage, s, d, p):
        at = s * PC + p
        return pltpu.make_async_remote_copy(
            outgoing(stage, s, d, p), rb.at[stage, at],
            hs.at[stage, s, d, p], rr.at[stage, at],
            device_id=(q, crossing[d][2]), device_id_type=MESH,
        )

    def detour_out(stage, s, d, p):
        at = s * PC + p
        return pltpu.make_async_remote_copy(
            rb.at[stage, at], incoming(stage, s, d, p),
            rq.at[stage, at], hr.at[stage, s, d, p],
            device_id=(q, crossing[d][1]), device_id_type=MESH,
        )

    exists = (has_hi, has_lo)

    def both(fn):
        for d in range(2):
            @pl.when(exists[d])
            def _():
                fn(d)

    def both_in(fn):
        for d in range(2):
            @pl.when(exists[1 - d])
            def _():
                fn(d)

    def send_sig(kind):
        for d in range(2):
            around = sig_detour(kind, d, crossing[d][0])

            @pl.when(exists[d] & jnp.logical_not(around))
            def _():
                sig_copy(kind, d).start()

            @pl.when(around)
            def _():
                sig_in(kind, d).start()

    def pass_sig(kind):
        for d in range(2):
            @pl.when(sig_detour(kind, d, sig_via(kind, d)))
            def _():
                sig_in(kind, d).wait_recv()
                sig_out(kind, d).start()

    def send_halo(stage, s, p):
        for d in range(2):
            around = crossing[d][3] & (v == crossing[d][0])

            @pl.when(exists[d] & jnp.logical_not(around))
            def _():
                halo_copy(stage, s, d, p).start()

            @pl.when(around)
            def _():
                detour_in(stage, s, d, p).start()

    def pass_on(stage, s, p):
        for d in range(2):
            @pl.when(crossing[d][3] & (v == crossing[d][2]))
            def _():
                detour_in(stage, s, d, p).wait_recv()
                detour_out(stage, s, d, p).start()

    def await_halo(stage, s, p):
        both_in(lambda d: halo_copy(stage, s, d, p).wait_recv())

    for copy in local:
        copy.wait()
    partners = (sizes[0] - 1) + (sizes[1] - 1)
    pl.semaphore_wait(barrier, partners + expected)

    send_sig(0)
    for s in range(2):
        @pl.loop(0, PC)
        def _(p):
            send_halo(0, s, p)
    pass_sig(0)

    lo_open = has_lo.astype(jnp.float32)
    hi_open = has_hi.astype(jnp.float32)

    def couple(k, s, below, above):
        xp = jnp.where(rows < N - 1, 0.5 * (s + up_row(s)), 0.0)
        yp = jnp.where(cols < N - 1, 0.5 * (s + up_col(s)), 0.0)
        xm, ym = down_row(xp), down_col(yp)
        diag = LEAK + (below + above) + (xp + xm) + (yp + ym)
        inv = 1.0 / diag
        for at, value in ((ZL, below), (ZH, above), (XM, xm), (XP, xp), (YM, ym), (YP, yp)):
            co[at, k] = value * inv
        if k in (1, 2):
            dg[k - 1] = diag
        di[k + 1] = inv

    both_in(lambda d: sig_copy(0, d).wait_recv())
    couple(1, cond[0], 0.5 * (cond[0] + sh[0, 1]) * lo_open, 0.5 * (cond[0] + cond[1]))
    couple(2, cond[1], 0.5 * (cond[0] + cond[1]), 0.5 * (cond[1] + sh[1, 0]) * hi_open)
    send_sig(1)
    send_sig(2)

    def apply(k, x, below, above):
        y = co[ZL, k] * below + co[ZH, k] * above
        y = y + co[XM, k] * down_row(x) + co[XP, k] * up_row(x)
        y = y + co[YM, k] * down_col(x) + co[YP, k] * up_col(x)
        return x - y

    def difference(p, first, second, plane, scale):
        here = (2 * v + plane) * PLANE
        plus = jnp.where(cell == elec[pats[first, p]] - here, scale, 0.0)
        return plus - jnp.where(cell == elec[pats[second, p]] - here, scale, 0.0)

    def probe(p, plane):
        return difference(p, 2, 3, plane, 1.0)

    def record(p, values):
        now = tile[...]
        for k, value in values:
            now = jnp.where((trow == p) & (tcol == k), value, now)
        tile[...] = now

    for s in range(2):
        @pl.loop(0, PC)
        def _(p):
            await_halo(0, s, p)
            a, b = warm[s, 0, p], warm[s, 1, p]
            e0 = -apply(1, a, xh[s, 0, p], b)
            e1 = -apply(2, b, a, xh[s, 1, p])
            if s == 0:
                e0 = e0 + difference(p, 0, 1, 0, strength) * di[2]
                e1 = e1 + difference(p, 0, 1, 1, strength) * di[3]
            d0[s, p, 0] = e0
            d0[s, p, 1] = e1
            send_halo(1, s, p)
            g0, g1 = probe(p, 0), probe(p, 1)
            rho = total(dg[0] * e0 * e0 + dg[1] * e1 * e1)
            ge = total(g0 * e0 + g1 * e1)
            if s == 0:
                record(p, ((F_RHO, rho), (F_D, ge), (F_X, total(g0 * a + g1 * b))))
            else:
                record(p, ((YY, rho), (GY, ge)))
            pass_on(0, s, p)

    pass_sig(1)
    pass_sig(2)
    both_in(lambda d: sig_copy(1, d).wait_recv())
    couple(0, sh[0, 1], 0.5 * (sh[0, 0] + sh[0, 1]), 0.5 * (cond[0] + sh[0, 1]) * lo_open)
    couple(3, sh[1, 0], 0.5 * (cond[1] + sh[1, 0]) * hi_open, 0.5 * (sh[1, 0] + sh[1, 1]))
    both_in(lambda d: sig_copy(2, d).wait_recv())
    di[0] = fh[0]
    di[5] = fh[1]

    @pl.loop(0, PC)
    def _(p):
        pass_on(1, 0, p)
        e = [probe(p, k - 2) * di[k] for k in range(6)]
        y = [apply(k, e[k + 1], e[k], e[k + 2]) for k in range(4)]
        for k in range(4):
            gd[p, k] = e[k + 1]
            gw[p, k] = y[k]
        z0, z1 = apply(1, y[1], y[0], y[2]), apply(2, y[2], y[1], y[3])
        g0, g1 = probe(p, 0), probe(p, 1)
        u0, u1 = dg[0] * y[1], dg[1] * y[2]
        record(p, (
            (GG, total(g0 * e[2] + g1 * e[3])),
            (GG + 1, total(g0 * y[1] + g1 * y[2])),
            (GG + 2, total(u0 * y[1] + u1 * y[2])),
            (GG + 3, total(u0 * z0 + u1 * z1)),
        ))

    for s in range(2):
        @pl.loop(0, PC)
        def _(p):
            await_halo(1, s, p)
            a, b = d0[s, p, 0], d0[s, p, 1]
            y0 = apply(1, a, dh[s, 0, p], b)
            y1 = apply(2, b, a, dh[s, 1, p])
            w0[s, p, 0] = y0
            w0[s, p, 1] = y1
            send_halo(2, s, p)
            u0, u1 = dg[0] * y0, dg[1] * y1
            mu = total(u0 * a + u1 * b)
            nu = total(u0 * y0 + u1 * y1)
            gy = total(probe(p, 0) * y0 + probe(p, 1) * y1)
            if s == 0:
                record(p, ((F_MU, mu), (F_NU, nu), (F_W, gy)))
            else:
                record(p, ((YY + 1, mu), (YY + 2, nu), (GY + 1, gy)))
            pass_on(1 + s, 1 - s, p)

    for s in range(2):
        @pl.loop(0, PC)
        def _(p):
            if s == 0:
                pass_on(2, 1, p)
            await_halo(2, s, p)
            a, b = w0[s, p, 0], w0[s, p, 1]
            u0 = dg[0] * apply(1, a, wh[s, 0, p], b)
            u1 = dg[1] * apply(2, b, a, wh[s, 1, p])
            xi = total(a * u0 + b * u1)
            if s == 0:
                record(p, ((F_XI, xi),))
            else:
                k0, k1 = gw[p, 1], gw[p, 2]
                near = total(dg[0] * a * k0 + dg[1] * b * k1)
                record(p, ((YY + 3, xi), (GY + 2, near), (GY + 3, total(u0 * k0 + u1 * k1))))

    def sum_copy(stage, k, slot):
        return pltpu.make_async_remote_copy(
            red.at[stage, slot], red.at[stage, slot],
            red_s.at[stage, k], red_r.at[stage, slot],
            device_id=(q, member(stage, k)), device_id_type=MESH,
        )

    def halos_have_left():
        for kind in range(3):
            both(lambda d: sig_copy(kind, d).wait_send())
            for d in range(2):
                @pl.when(sig_detour(kind, d, sig_via(kind, d)))
                def _():
                    sig_out(kind, d).wait_send()

        @pl.loop(0, PC)
        def _(p):
            for stage in range(3):
                for s in range(2):
                    both(lambda d: halo_copy(stage, s, d, p).wait_send())
                    for d in range(2):
                        @pl.when(crossing[d][3] & (v == crossing[d][2]))
                        def _():
                            detour_out(stage, s, d, p).wait_send()

    value = tile[...]
    for stage in range(2):
        mine, size = rank[stage], sizes[stage]
        red[stage, mine] = value
        for j in range(1, size):
            sum_copy(stage, lax.rem(mine + j, size), mine).start()
        if stage == 1:
            halos_have_left()
        for j in range(1, size):
            k = lax.rem(mine + j, size)
            sum_copy(stage, k, k).wait_recv()
        value = red[stage, 0]
        for k in range(1, size):
            value = value + red[stage, k]

    def column(k):
        return jnp.sum(jnp.where(tcol == k, value, 0.0), axis=1, keepdims=True)

    def steps(rho, mu, nu, xi):
        alpha = rho / mu
        rho1 = rho - 2.0 * alpha * mu + alpha * alpha * nu
        beta1 = 1.0 + rho1 / rho
        curve = beta1 * beta1 * mu - 2.0 * alpha * beta1 * nu + alpha * alpha * xi
        alpha1 = rho1 / curve
        return alpha + alpha1 * beta1, -alpha * alpha1

    c1, c2 = steps(column(F_RHO), column(F_MU), column(F_NU), column(F_XI))
    predicted = column(F_X) + c1 * column(F_D) + c2 * column(F_W)
    observed = jnp.zeros((PC, 1), jnp.float32)
    for p in range(PC):
        observed = jnp.where(trow[:, 0:1] == p, obs[p], observed)
    weight = data_weight * (predicted - observed)
    e1, e2 = steps(*(
        column(YY + k) + weight * (2.0 * column(GY + k) + weight * column(GG + k))
        for k in range(4)
    ))
    for k, factor in enumerate((c1, c2, e1, e2, e1 * weight, e2 * weight)):
        kc[k] = jnp.broadcast_to(factor, (PC, N))
    wide = jnp.where(trow == tcol, predicted, 0.0)
    pred_out[...] = jnp.sum(wide, axis=0, keepdims=True)[:, :PC]

    is_outer = (q == 0) | (q == npat - 1) if npat > 2 else q < 0
    is_inner = jnp.logical_not(is_outer)
    outward = jnp.where(q < middle, q - 1, q + 1)
    inward = jnp.where(q < middle, q + 1, q - 1)
    height = N // (PIECES // 2)

    def line_copy(leg, j):
        at = (j // (PIECES // 2), pl.ds(j % (PIECES // 2) * height, height))
        src = (gb, half, grad)[leg].at[at]
        dst = (lb[0], lb[1], grad)[leg].at[at]
        return pltpu.make_async_remote_copy(
            src, dst, ls.at[leg, j], lr.at[leg, j],
            device_id=(outward if leg == 2 else inward, v), device_id_type=MESH,
        )

    def piece(j):
        return j // (PIECES // 2), slice(j % (PIECES // 2) * height, (j % (PIECES // 2) + 1) * height)

    def field(p, s, k):
        if k in (0, 3):
            x, d, w = (h[s, k // 3, p] for h in (xh, dh, wh))
        else:
            x, d, w = warm[s, k - 1, p], d0[s, p, k - 1], w0[s, p, k - 1]
        out = x + kc[2 * s, pl.ds(p, 1), :] * d + kc[2 * s + 1, pl.ds(p, 1), :] * w
        if s == 1:
            out = out + kc[4, pl.ds(p, 1), :] * gd[p, k] + kc[5, pl.ds(p, 1), :] * gw[p, k]
        return out

    def within(plane, x, y):
        acc[3 + plane] += (up_row(x) - x) * (up_row(y) - y)
        acc[5 + plane] += (up_col(x) - x) * (up_col(y) - y)

    def finish(plane):
        lo, hi = acc[plane], acc[plane + 1]
        lo = lo * lo_open if plane == 0 else lo
        hi = hi * hi_open if plane == 1 else hi
        px = jnp.where(rows < N - 1, acc[3 + plane], 0.0)
        py = jnp.where(cols < N - 1, acc[5 + plane], 0.0)
        gb[plane] = -0.5 * ((lo + hi) + (px + down_row(px)) + (py + down_col(py)))

        @pl.when(is_outer)
        def _():
            for j in range(plane * PIECES // 2, (plane + 1) * PIECES // 2):
                line_copy(0, j).start()

    @pl.loop(0, PC)
    def _(p):
        f = [field(p, 0, k) for k in range(3)]
        a = [field(p, 1, k) for k in range(3)]
        top[0, p] = f[2]
        top[1, p] = a[2]
        for k in range(2):
            acc[k] += (f[k + 1] - f[k]) * (a[k + 1] - a[k])
        within(0, f[1], a[1])

    finish(0)

    @pl.loop(0, PC)
    def _(p):
        x, y = top[0, p], top[1, p]
        acc[2] += (field(p, 0, 3) - x) * (field(p, 1, 3) - y)
        within(1, x, y)

    finish(1)

    @pl.when(is_outer)
    def _():
        for j in range(PIECES):
            line_copy(2, j).wait_recv()
        for j in range(PIECES):
            line_copy(0, j).wait_send()

    @pl.when(is_inner)
    def _():
        for j in range(PIECES):
            at = piece(j)
            if npat > 2:
                line_copy(0, j).wait_recv()
                half[at] = gb[at] + lb[0][at]
            else:
                half[at] = gb[at]
            line_copy(1, j).start()
        for j in range(PIECES):
            at = piece(j)
            line_copy(1, j).wait_recv()
            grad[at] = half[at] + lb[1][at]
            if npat > 2:
                line_copy(2, j).start()
        for j in range(PIECES):
            line_copy(1, j).wait_send()
            if npat > 2:
                line_copy(2, j).wait_send()

    grad_out[...] = grad[...]

    for stage in range(2):
        for j in range(1, sizes[stage]):
            sum_copy(stage, lax.rem(rank[stage] + j, sizes[stage]), rank[stage]).wait_send()


def solution(mesh):
    npat, layers = mesh.shape["pat"], mesh.shape["vox"]
    group = 8 if layers >= 64 else 2

    def per_device(conductivity, warm_forward, warm_adjoint, electrodes, patterns, observed):
        planes = conductivity.shape[0]
        strength = 2.0 * math.sqrt(layers * planes * PLANE)
        vmem = pl.BlockSpec(memory_space=pltpu.VMEM)
        hbm = pl.BlockSpec(memory_space=pltpu.HBM)
        f32 = jnp.float32
        dma = pltpu.SemaphoreType.DMA
        groups = layers // group
        widest = max(group, groups)
        gradient, predicted = pl.pallas_call(
            functools.partial(kernel, npat, layers, group, strength),
            out_shape=(
                jax.ShapeDtypeStruct((2, N, N), f32),
                jax.ShapeDtypeStruct((1, PC), f32),
            ),
            in_specs=[hbm] * 6,
            out_specs=(vmem, vmem),
            scratch_shapes=[
                pltpu.VMEM((2, N, N), f32),
                pltpu.VMEM((2, 2, PC, N, N), f32),
                pltpu.SMEM(electrodes.shape, jnp.int32),
                pltpu.SMEM((4, PC), jnp.int32),
                pltpu.SMEM((PC,), f32),
                pltpu.VMEM((2, 2, N, N), f32),
                pltpu.VMEM((2, N, N), f32),
                pltpu.VMEM((2, 2, PC, N, N), f32),
                pltpu.VMEM((2, 2, PC, N, N), f32),
                pltpu.VMEM((2, 2, PC, N, N), f32),
                pltpu.VMEM((2, PC, 2, N, N), f32),
                pltpu.VMEM((2, PC, 2, N, N), f32),
                pltpu.VMEM((PC, 4, N, N), f32),
                pltpu.VMEM((PC, 4, N, N), f32),
                pltpu.VMEM((3, 2 * PC, N, N), f32),
                pltpu.VMEM((3, N, N), f32),
                pltpu.VMEM((6, 4, N, N), f32),
                pltpu.VMEM((2, N, N), f32),
                pltpu.VMEM((6, N, N), f32),
                pltpu.VMEM((7, N, N), f32),
                pltpu.VMEM((2, PC, N, N), f32),
                pltpu.VMEM((PC, N), f32),
                pltpu.VMEM((2, widest, PC, N), f32),
                pltpu.VMEM((6, PC, N), f32),
                pltpu.VMEM((2, N, N), f32),
                pltpu.VMEM((2, N, N), f32),
                pltpu.VMEM((2, N, N), f32),
                pltpu.VMEM((2, N, N), f32),
                pltpu.VMEM((2, N, N), f32),
                dma((6,)),
                dma((3, 2)),
                dma((3, 2)),
                dma((3,)),
                dma((3,)),
                dma((3, 2, 2, PC)),
                dma((3, 2, 2, PC)),
                dma((3, 2 * PC)),
                dma((3, 2 * PC)),
                dma((2, widest)),
                dma((2, widest)),
                dma((3, PIECES)),
                dma((3, PIECES)),
            ],
            compiler_params=pltpu.CompilerParams(
                collective_id=0, has_side_effects=True, vmem_limit_bytes=48 * 2**20
            ),
            name="ert_gradient",
        )(*(
            pltpu.with_memory_space_constraint(x, pltpu.HBM)
            for x in (conductivity, warm_forward, warm_adjoint, electrodes, patterns.T, observed)
        ))
        return gradient, predicted.reshape(PC)

    in_specs = (
        P("vox", None, None),
        P("vox", "pat", None, None),
        P("vox", "pat", None, None),
        P(),
        P("pat", None),
        P("pat"),
    )
    return jax.shard_map(
        per_device,
        mesh=mesh,
        in_specs=in_specs,
        out_specs=(P("vox", None, None), P("pat")),
        check_vma=False,
    )
```

```python
import functools
import math

import jax
import jax.numpy as jnp
from jax import lax
from jax.experimental import pallas as pl
from jax.experimental.pallas import tpu as pltpu
from jax.sharding import PartitionSpec as P

MESH = pl.DeviceIdType.MESH
LEAK = 0.05
N = 128
PLANE = N * N
PC = 8
PIECES = 8

ZL, ZH, XM, XP, YM, YP = range(6)
F_RHO, F_MU, F_NU, F_XI, F_X, F_D, F_W = range(7)
YY, GY, GG = 7, 11, 15


def up_row(x):
    return pltpu.roll(x, N - 1, 0)


def down_row(x):
    return pltpu.roll(x, 1, 0)


def up_col(x):
    return pltpu.roll(x, N - 1, 1)


def down_col(x):
    return pltpu.roll(x, 1, 1)


def total(x):
    part = jnp.sum(x.reshape(N // 8, 8, N), axis=0)
    return jnp.sum(jnp.sum(part, axis=1, keepdims=True), axis=0, keepdims=True)


def kernel(
    npat,
    layers,
    group,
    strength,
    cond_in,
    wf_in,
    wa_in,
    elec_in,
    pats_in,
    obs_in,
    grad_out,
    pred_out,
    cond,
    warm,
    elec,
    pats,
    obs,
    sh,
    fh,
    xh,
    dh,
    wh,
    d0,
    w0,
    gd,
    gw,
    rb,
    sb,
    co,
    dg,
    di,
    acc,
    top,
    tile,
    red,
    kc,
    gb,
    lb_outer,
    lb_inner,
    half,
    grad,
    in_s,
    sig_s,
    sig_r,
    sig_rr,
    sig_rq,
    hs,
    hr,
    rr,
    rq,
    red_s,
    red_r,
    ls,
    lr,
):
    lb = (lb_outer, lb_inner)
    q = lax.axis_index("pat")
    v = lax.axis_index("vox")
    last = layers - 1
    has_lo = v > 0
    has_hi = v < last
    groups = layers // group
    rank = (lax.rem(v, group), v // group)
    sizes = (group, groups)
    data_weight = 0.1 * strength
    lower, upper = layers // 2 - 1, layers // 2
    middle = npat // 2
    inner = (q >= middle - 1) & (q <= middle) if npat > 2 else q == 0
    crossing = (
        (lower, upper, 0, inner),
        (upper, lower, last, jnp.logical_not(inner)),
    )

    local = [
        pltpu.make_async_copy(cond_in, cond, in_s.at[0]),
        pltpu.make_async_copy(wf_in, warm.at[0], in_s.at[1]),
        pltpu.make_async_copy(wa_in, warm.at[1], in_s.at[2]),
        pltpu.make_async_copy(elec_in, elec, in_s.at[3]),
        pltpu.make_async_copy(pats_in, pats, in_s.at[4]),
        pltpu.make_async_copy(obs_in, obs, in_s.at[5]),
    ]

    def member(stage, k):
        return (v // group) * group + k if stage == 0 else k * group + lax.rem(v, group)

    barrier = pltpu.get_barrier_semaphore()

    def greet(device):
        pl.semaphore_signal(barrier, inc=1, device_id=device, device_id_type=MESH)

    @pl.when(has_lo)
    def _():
        greet((q, v - 1))

    @pl.when(has_hi)
    def _():
        greet((q, v + 1))

    expected = has_lo.astype(jnp.int32) + has_hi.astype(jnp.int32)
    for source, target, via, taken in crossing:
        on_path = taken & ((v == source) | (v == target))

        @pl.when(on_path)
        def _():
            greet((q, via))

        @pl.when(taken & (v == via))
        def _():
            greet((q, source))
            greet((q, target))

        expected = expected + on_path.astype(jnp.int32)
        expected = expected + 2 * (taken & (v == via)).astype(jnp.int32)

    for stage in range(2):
        for j in range(1, sizes[stage]):
            greet((q, member(stage, lax.rem(rank[stage] + j, sizes[stage]))))
    below, above = q > 0, q < npat - 1

    @pl.when(below)
    def _():
        greet((q - 1, v))

    @pl.when(above)
    def _():
        greet((q + 1, v))

    expected = expected + below.astype(jnp.int32) + above.astype(jnp.int32)
    for copy in local:
        copy.start()

    rows = lax.broadcasted_iota(jnp.int32, (N, N), 0)
    cols = lax.broadcasted_iota(jnp.int32, (N, N), 1)
    cell = rows * N + cols
    trow = lax.broadcasted_iota(jnp.int32, (PC, N), 0)
    tcol = lax.broadcasted_iota(jnp.int32, (PC, N), 1)
    blank = jnp.zeros((N, N), jnp.float32)

    for d, outside in enumerate((jnp.logical_not(has_lo), jnp.logical_not(has_hi))):
        @pl.when(outside)
        def _():
            sh[d, 0] = blank
            sh[d, 1] = blank
            fh[d] = blank

            @pl.loop(0, PC)
            def _(p):
                for s in range(2):
                    for h in (xh, dh, wh):
                        h[s, d, p] = blank

    tile[...] = jnp.zeros((PC, N), jnp.float32)
    for k in range(7):
        acc[k] = blank

    def neighbour(d):
        return (q, v + 1 - 2 * d)

    def sig_ends(kind, d):
        if kind == 2:
            return di.at[2 + d], fh.at[d]
        plane = (1 - d, d)[kind]
        return cond.at[plane], sh.at[d, plane]

    def sig_copy(kind, d):
        src, dst = sig_ends(kind, d)
        return pltpu.make_async_remote_copy(
            src, dst, sig_s.at[kind, d], sig_r.at[kind, d],
            device_id=neighbour(d), device_id_type=MESH,
        )

    def sig_in(kind, d):
        return pltpu.make_async_remote_copy(
            sig_ends(kind, d)[0], sb.at[kind], sig_s.at[kind, d], sig_rr.at[kind],
            device_id=(q, crossing[d][2]), device_id_type=MESH,
        )

    def sig_out(kind, d):
        return pltpu.make_async_remote_copy(
            sb.at[kind], sig_ends(kind, d)[1], sig_rq.at[kind], sig_r.at[kind, d],
            device_id=(q, crossing[d][1]), device_id_type=MESH,
        )

    def outgoing(stage, s, d, p):
        plane = 1 - d
        if stage == 0:
            return warm.at[s, plane, p]
        return (d0 if stage == 1 else w0).at[s, p, plane]

    def incoming(stage, s, d, p):
        return (xh, dh, wh)[stage].at[s, d, p]

    def halo_copy(stage, s, d, p):
        return pltpu.make_async_remote_copy(
            outgoing(stage, s, d, p), incoming(stage, s, d, p),
            hs.at[stage, s, d, p], hr.at[stage, s, d, p],
            device_id=neighbour(d), device_id_type=MESH,
        )

    def detour_in(stage, s, d, p):
        at = s * PC + p
        return pltpu.make_async_remote_copy(
            outgoing(stage, s, d, p), rb.at[stage, at],
            hs.at[stage, s, d, p], rr.at[stage, at],
            device_id=(q, crossing[d][2]), device_id_type=MESH,
        )

    def detour_out(stage, s, d, p):
        at = s * PC + p
        return pltpu.make_async_remote_copy(
            rb.at[stage, at], incoming(stage, s, d, p),
            rq.at[stage, at], hr.at[stage, s, d, p],
            device_id=(q, crossing[d][1]), device_id_type=MESH,
        )

    exists = (has_hi, has_lo)

    def both(fn):
        for d in range(2):
            @pl.when(exists[d])
            def _():
                fn(d)

    def both_in(fn):
        for d in range(2):
            @pl.when(exists[1 - d])
            def _():
                fn(d)

    def send_sig(kind):
        for d in range(2):
            around = crossing[d][3] & (v == crossing[d][0])

            @pl.when(exists[d] & jnp.logical_not(around))
            def _():
                sig_copy(kind, d).start()

            @pl.when(around)
            def _():
                sig_in(kind, d).start()

    def pass_sig(kind):
        for d in range(2):
            @pl.when(crossing[d][3] & (v == crossing[d][2]))
            def _():
                sig_in(kind, d).wait_recv()
                sig_out(kind, d).start()

    def send_halo(stage, s, p):
        for d in range(2):
            around = crossing[d][3] & (v == crossing[d][0])

            @pl.when(exists[d] & jnp.logical_not(around))
            def _():
                halo_copy(stage, s, d, p).start()

            @pl.when(around)
            def _():
                detour_in(stage, s, d, p).start()

    def pass_on(stage, s, p):
        for d in range(2):
            @pl.when(crossing[d][3] & (v == crossing[d][2]))
            def _():
                detour_in(stage, s, d, p).wait_recv()
                detour_out(stage, s, d, p).start()

    def await_halo(stage, s, p):
        both_in(lambda d: halo_copy(stage, s, d, p).wait_recv())

    for copy in local:
        copy.wait()
    partners = (sizes[0] - 1) + (sizes[1] - 1)
    pl.semaphore_wait(barrier, partners + expected)

    send_sig(0)
    for s in range(2):
        @pl.loop(0, PC)
        def _(p):
            send_halo(0, s, p)
    pass_sig(0)

    lo_open = has_lo.astype(jnp.float32)
    hi_open = has_hi.astype(jnp.float32)

    def couple(k, s, below, above):
        xp = jnp.where(rows < N - 1, 0.5 * (s + up_row(s)), 0.0)
        yp = jnp.where(cols < N - 1, 0.5 * (s + up_col(s)), 0.0)
        xm, ym = down_row(xp), down_col(yp)
        diag = LEAK + (below + above) + (xp + xm) + (yp + ym)
        inv = 1.0 / diag
        for at, value in ((ZL, below), (ZH, above), (XM, xm), (XP, xp), (YM, ym), (YP, yp)):
            co[at, k] = value * inv
        if k in (1, 2):
            dg[k - 1] = diag
        di[k + 1] = inv

    both_in(lambda d: sig_copy(0, d).wait_recv())
    couple(1, cond[0], 0.5 * (cond[0] + sh[0, 1]) * lo_open, 0.5 * (cond[0] + cond[1]))
    couple(2, cond[1], 0.5 * (cond[0] + cond[1]), 0.5 * (cond[1] + sh[1, 0]) * hi_open)
    send_sig(1)
    send_sig(2)

    def apply(k, x, below, above):
        y = co[ZL, k] * below + co[ZH, k] * above
        y = y + co[XM, k] * down_row(x) + co[XP, k] * up_row(x)
        y = y + co[YM, k] * down_col(x) + co[YP, k] * up_col(x)
        return x - y

    def difference(p, first, second, plane, scale):
        here = (2 * v + plane) * PLANE
        plus = jnp.where(cell == elec[pats[first, p]] - here, scale, 0.0)
        return plus - jnp.where(cell == elec[pats[second, p]] - here, scale, 0.0)

    def probe(p, plane):
        return difference(p, 2, 3, plane, 1.0)

    def record(p, values):
        now = tile[...]
        for k, value in values:
            now = jnp.where((trow == p) & (tcol == k), value, now)
        tile[...] = now

    for s in range(2):
        @pl.loop(0, PC)
        def _(p):
            await_halo(0, s, p)
            a, b = warm[s, 0, p], warm[s, 1, p]
            e0 = -apply(1, a, xh[s, 0, p], b)
            e1 = -apply(2, b, a, xh[s, 1, p])
            if s == 0:
                e0 = e0 + difference(p, 0, 1, 0, strength) * di[2]
                e1 = e1 + difference(p, 0, 1, 1, strength) * di[3]
            d0[s, p, 0] = e0
            d0[s, p, 1] = e1
            send_halo(1, s, p)
            g0, g1 = probe(p, 0), probe(p, 1)
            rho = total(dg[0] * e0 * e0 + dg[1] * e1 * e1)
            ge = total(g0 * e0 + g1 * e1)
            if s == 0:
                record(p, ((F_RHO, rho), (F_D, ge), (F_X, total(g0 * a + g1 * b))))
            else:
                record(p, ((YY, rho), (GY, ge)))
            pass_on(0, s, p)

    pass_sig(1)
    pass_sig(2)
    both_in(lambda d: sig_copy(1, d).wait_recv())
    couple(0, sh[0, 1], 0.5 * (sh[0, 0] + sh[0, 1]), 0.5 * (cond[0] + sh[0, 1]) * lo_open)
    couple(3, sh[1, 0], 0.5 * (cond[1] + sh[1, 0]) * hi_open, 0.5 * (sh[1, 0] + sh[1, 1]))
    both_in(lambda d: sig_copy(2, d).wait_recv())
    di[0] = fh[0]
    di[5] = fh[1]

    @pl.loop(0, PC)
    def _(p):
        pass_on(1, 0, p)
        e = [probe(p, k - 2) * di[k] for k in range(6)]
        y = [apply(k, e[k + 1], e[k], e[k + 2]) for k in range(4)]
        for k in range(4):
            gd[p, k] = e[k + 1]
            gw[p, k] = y[k]
        z0, z1 = apply(1, y[1], y[0], y[2]), apply(2, y[2], y[1], y[3])
        g0, g1 = probe(p, 0), probe(p, 1)
        u0, u1 = dg[0] * y[1], dg[1] * y[2]
        record(p, (
            (GG, total(g0 * e[2] + g1 * e[3])),
            (GG + 1, total(g0 * y[1] + g1 * y[2])),
            (GG + 2, total(u0 * y[1] + u1 * y[2])),
            (GG + 3, total(u0 * z0 + u1 * z1)),
        ))

    for s in range(2):
        @pl.loop(0, PC)
        def _(p):
            await_halo(1, s, p)
            a, b = d0[s, p, 0], d0[s, p, 1]
            y0 = apply(1, a, dh[s, 0, p], b)
            y1 = apply(2, b, a, dh[s, 1, p])
            w0[s, p, 0] = y0
            w0[s, p, 1] = y1
            send_halo(2, s, p)
            u0, u1 = dg[0] * y0, dg[1] * y1
            mu = total(u0 * a + u1 * b)
            nu = total(u0 * y0 + u1 * y1)
            gy = total(probe(p, 0) * y0 + probe(p, 1) * y1)
            if s == 0:
                record(p, ((F_MU, mu), (F_NU, nu), (F_W, gy)))
            else:
                record(p, ((YY + 1, mu), (YY + 2, nu), (GY + 1, gy)))
            pass_on(1 + s, 1 - s, p)

    for s in range(2):
        @pl.loop(0, PC)
        def _(p):
            if s == 0:
                pass_on(2, 1, p)
            await_halo(2, s, p)
            a, b = w0[s, p, 0], w0[s, p, 1]
            u0 = dg[0] * apply(1, a, wh[s, 0, p], b)
            u1 = dg[1] * apply(2, b, a, wh[s, 1, p])
            xi = total(a * u0 + b * u1)
            if s == 0:
                record(p, ((F_XI, xi),))
            else:
                k0, k1 = gw[p, 1], gw[p, 2]
                near = total(dg[0] * a * k0 + dg[1] * b * k1)
                record(p, ((YY + 3, xi), (GY + 2, near), (GY + 3, total(u0 * k0 + u1 * k1))))

    def sum_copy(stage, k, slot):
        return pltpu.make_async_remote_copy(
            red.at[stage, slot], red.at[stage, slot],
            red_s.at[stage, k], red_r.at[stage, slot],
            device_id=(q, member(stage, k)), device_id_type=MESH,
        )

    def halos_have_left():
        for kind in range(3):
            both(lambda d: sig_copy(kind, d).wait_send())
            for d in range(2):
                @pl.when(crossing[d][3] & (v == crossing[d][2]))
                def _():
                    sig_out(kind, d).wait_send()

        @pl.loop(0, PC)
        def _(p):
            for stage in range(3):
                for s in range(2):
                    both(lambda d: halo_copy(stage, s, d, p).wait_send())
                    for d in range(2):
                        @pl.when(crossing[d][3] & (v == crossing[d][2]))
                        def _():
                            detour_out(stage, s, d, p).wait_send()

    value = tile[...]
    for stage in range(2):
        mine, size = rank[stage], sizes[stage]
        red[stage, mine] = value
        for j in range(1, size):
            sum_copy(stage, lax.rem(mine + j, size), mine).start()
        if stage == 1:
            halos_have_left()
        for j in range(1, size):
            k = lax.rem(mine + j, size)
            sum_copy(stage, k, k).wait_recv()
        value = red[stage, 0]
        for k in range(1, size):
            value = value + red[stage, k]

    def column(k):
        return jnp.sum(jnp.where(tcol == k, value, 0.0), axis=1, keepdims=True)

    def steps(rho, mu, nu, xi):
        alpha = rho / mu
        rho1 = rho - 2.0 * alpha * mu + alpha * alpha * nu
        beta1 = 1.0 + rho1 / rho
        curve = beta1 * beta1 * mu - 2.0 * alpha * beta1 * nu + alpha * alpha * xi
        alpha1 = rho1 / curve
        return alpha + alpha1 * beta1, -alpha * alpha1

    c1, c2 = steps(column(F_RHO), column(F_MU), column(F_NU), column(F_XI))
    predicted = column(F_X) + c1 * column(F_D) + c2 * column(F_W)
    observed = jnp.zeros((PC, 1), jnp.float32)
    for p in range(PC):
        observed = jnp.where(trow[:, 0:1] == p, obs[p], observed)
    weight = data_weight * (predicted - observed)
    e1, e2 = steps(*(
        column(YY + k) + weight * (2.0 * column(GY + k) + weight * column(GG + k))
        for k in range(4)
    ))
    for k, factor in enumerate((c1, c2, e1, e2, e1 * weight, e2 * weight)):
        kc[k] = jnp.broadcast_to(factor, (PC, N))
    wide = jnp.where(trow == tcol, predicted, 0.0)
    pred_out[...] = jnp.sum(wide, axis=0, keepdims=True)[:, :PC]

    is_outer = (q == 0) | (q == npat - 1) if npat > 2 else q < 0
    is_inner = jnp.logical_not(is_outer)
    outward = jnp.where(q < middle, q - 1, q + 1)
    inward = jnp.where(q < middle, q + 1, q - 1)
    height = N // (PIECES // 2)

    def line_copy(leg, j):
        at = (j // (PIECES // 2), pl.ds(j % (PIECES // 2) * height, height))
        src = (gb, half, grad)[leg].at[at]
        dst = (lb[0], lb[1], grad)[leg].at[at]
        return pltpu.make_async_remote_copy(
            src, dst, ls.at[leg, j], lr.at[leg, j],
            device_id=(outward if leg == 2 else inward, v), device_id_type=MESH,
        )

    def piece(j):
        return j // (PIECES // 2), slice(j % (PIECES // 2) * height, (j % (PIECES // 2) + 1) * height)

    def field(p, s, k):
        if k in (0, 3):
            x, d, w = (h[s, k // 3, p] for h in (xh, dh, wh))
        else:
            x, d, w = warm[s, k - 1, p], d0[s, p, k - 1], w0[s, p, k - 1]
        out = x + kc[2 * s, pl.ds(p, 1), :] * d + kc[2 * s + 1, pl.ds(p, 1), :] * w
        if s == 1:
            out = out + kc[4, pl.ds(p, 1), :] * gd[p, k] + kc[5, pl.ds(p, 1), :] * gw[p, k]
        return out

    def within(plane, x, y):
        acc[3 + plane] += (up_row(x) - x) * (up_row(y) - y)
        acc[5 + plane] += (up_col(x) - x) * (up_col(y) - y)

    def finish(plane):
        lo, hi = acc[plane], acc[plane + 1]
        lo = lo * lo_open if plane == 0 else lo
        hi = hi * hi_open if plane == 1 else hi
        px = jnp.where(rows < N - 1, acc[3 + plane], 0.0)
        py = jnp.where(cols < N - 1, acc[5 + plane], 0.0)
        gb[plane] = -0.5 * ((lo + hi) + (px + down_row(px)) + (py + down_col(py)))

        @pl.when(is_outer)
        def _():
            for j in range(plane * PIECES // 2, (plane + 1) * PIECES // 2):
                line_copy(0, j).start()

    @pl.loop(0, PC)
    def _(p):
        f = [field(p, 0, k) for k in range(3)]
        a = [field(p, 1, k) for k in range(3)]
        top[0, p] = f[2]
        top[1, p] = a[2]
        for k in range(2):
            acc[k] += (f[k + 1] - f[k]) * (a[k + 1] - a[k])
        within(0, f[1], a[1])

    finish(0)

    @pl.loop(0, PC)
    def _(p):
        x, y = top[0, p], top[1, p]
        acc[2] += (field(p, 0, 3) - x) * (field(p, 1, 3) - y)
        within(1, x, y)

    finish(1)

    @pl.when(is_outer)
    def _():
        for j in range(PIECES):
            line_copy(2, j).wait_recv()
        for j in range(PIECES):
            line_copy(0, j).wait_send()

    @pl.when(is_inner)
    def _():
        for j in range(PIECES):
            at = piece(j)
            if npat > 2:
                line_copy(0, j).wait_recv()
                half[at] = gb[at] + lb[0][at]
            else:
                half[at] = gb[at]
            line_copy(1, j).start()
        for j in range(PIECES):
            at = piece(j)
            line_copy(1, j).wait_recv()
            grad[at] = half[at] + lb[1][at]
            if npat > 2:
                line_copy(2, j).start()
        for j in range(PIECES):
            line_copy(1, j).wait_send()
            if npat > 2:
                line_copy(2, j).wait_send()

    grad_out[...] = grad[...]

    for stage in range(2):
        for j in range(1, sizes[stage]):
            sum_copy(stage, lax.rem(rank[stage] + j, sizes[stage]), rank[stage]).wait_send()


def solution(mesh):
    npat, layers = mesh.shape["pat"], mesh.shape["vox"]
    group = 8 if layers >= 64 else 2

    def per_device(conductivity, warm_forward, warm_adjoint, electrodes, patterns, observed):
        planes = conductivity.shape[0]
        strength = 2.0 * math.sqrt(layers * planes * PLANE)
        vmem = pl.BlockSpec(memory_space=pltpu.VMEM)
        hbm = pl.BlockSpec(memory_space=pltpu.HBM)
        f32 = jnp.float32
        dma = pltpu.SemaphoreType.DMA
        groups = layers // group
        widest = max(group, groups)
        gradient, predicted = pl.pallas_call(
            functools.partial(kernel, npat, layers, group, strength),
            out_shape=(
                jax.ShapeDtypeStruct((2, N, N), f32),
                jax.ShapeDtypeStruct((1, PC), f32),
            ),
            in_specs=[hbm] * 6,
            out_specs=(vmem, vmem),
            scratch_shapes=[
                pltpu.VMEM((2, N, N), f32),
                pltpu.VMEM((2, 2, PC, N, N), f32),
                pltpu.SMEM(electrodes.shape, jnp.int32),
                pltpu.SMEM((4, PC), jnp.int32),
                pltpu.SMEM((PC,), f32),
                pltpu.VMEM((2, 2, N, N), f32),
                pltpu.VMEM((2, N, N), f32),
                pltpu.VMEM((2, 2, PC, N, N), f32),
                pltpu.VMEM((2, 2, PC, N, N), f32),
                pltpu.VMEM((2, 2, PC, N, N), f32),
                pltpu.VMEM((2, PC, 2, N, N), f32),
                pltpu.VMEM((2, PC, 2, N, N), f32),
                pltpu.VMEM((PC, 4, N, N), f32),
                pltpu.VMEM((PC, 4, N, N), f32),
                pltpu.VMEM((3, 2 * PC, N, N), f32),
                pltpu.VMEM((3, N, N), f32),
                pltpu.VMEM((6, 4, N, N), f32),
                pltpu.VMEM((2, N, N), f32),
                pltpu.VMEM((6, N, N), f32),
                pltpu.VMEM((7, N, N), f32),
                pltpu.VMEM((2, PC, N, N), f32),
                pltpu.VMEM((PC, N), f32),
                pltpu.VMEM((2, widest, PC, N), f32),
                pltpu.VMEM((6, PC, N), f32),
                pltpu.VMEM((2, N, N), f32),
                pltpu.VMEM((2, N, N), f32),
                pltpu.VMEM((2, N, N), f32),
                pltpu.VMEM((2, N, N), f32),
                pltpu.VMEM((2, N, N), f32),
                dma((6,)),
                dma((3, 2)),
                dma((3, 2)),
                dma((3,)),
                dma((3,)),
                dma((3, 2, 2, PC)),
                dma((3, 2, 2, PC)),
                dma((3, 2 * PC)),
                dma((3, 2 * PC)),
                dma((2, widest)),
                dma((2, widest)),
                dma((3, PIECES)),
                dma((3, PIECES)),
            ],
            compiler_params=pltpu.CompilerParams(
                collective_id=0, has_side_effects=True, vmem_limit_bytes=48 * 2**20
            ),
            name="ert_gradient",
        )(*(
            pltpu.with_memory_space_constraint(x, pltpu.HBM)
            for x in (conductivity, warm_forward, warm_adjoint, electrodes, patterns.T, observed)
        ))
        return gradient, predicted.reshape(PC)

    in_specs = (
        P("vox", None, None),
        P("vox", "pat", None, None),
        P("vox", "pat", None, None),
        P(),
        P("pat", None),
        P("pat"),
    )
    return jax.shard_map(
        per_device,
        mesh=mesh,
        in_specs=in_specs,
        out_specs=(P("vox", None, None), P("pat")),
        check_vma=False,
    )
```

```python
import functools
import math

import jax
import jax.numpy as jnp
from jax import lax
from jax.experimental import pallas as pl
from jax.experimental.pallas import tpu as pltpu
from jax.sharding import PartitionSpec as P

MESH = pl.DeviceIdType.MESH
LEAK = 0.05
N = 128
PLANE = N * N
PC = 8
PIECES = 8

ZL, ZH, XM, XP, YM, YP = range(6)
F_RHO, F_MU, F_NU, F_XI, F_X, F_D, F_W = range(7)
YY, GY, GG = 7, 11, 15


def up_row(x):
    return pltpu.roll(x, N - 1, 0)


def down_row(x):
    return pltpu.roll(x, 1, 0)


def up_col(x):
    return pltpu.roll(x, N - 1, 1)


def down_col(x):
    return pltpu.roll(x, 1, 1)


def total(x):
    part = jnp.sum(x.reshape(N // 8, 8, N), axis=0)
    return jnp.sum(jnp.sum(part, axis=1, keepdims=True), axis=0, keepdims=True)


def far_first(size):
    return sorted(range(1, size), key=lambda j: abs(j - size // 2))


def kernel(
    npat,
    layers,
    group,
    strength,
    cond_in,
    wf_in,
    wa_in,
    elec_in,
    pats_in,
    obs_in,
    grad_out,
    pred_out,
    cond,
    warm,
    elec,
    pats,
    obs,
    sh,
    fh,
    xh,
    dh,
    wh,
    d0,
    w0,
    gd,
    gw,
    rb,
    sb,
    co,
    dg,
    di,
    acc,
    top,
    tile,
    red,
    kc,
    gb,
    lb_outer,
    lb_inner,
    half,
    grad,
    in_s,
    sig_s,
    sig_r,
    sig_rr,
    sig_rq,
    hs,
    hr,
    rr,
    rq,
    red_s,
    red_r,
    ls,
    lr,
):
    lb = (lb_outer, lb_inner)
    q = lax.axis_index("pat")
    v = lax.axis_index("vox")
    last = layers - 1
    has_lo = v > 0
    has_hi = v < last
    groups = layers // group
    rank = (lax.rem(v, group), v // group)
    sizes = (group, groups)
    data_weight = 0.1 * strength
    lower, upper = layers // 2 - 1, layers // 2
    middle = npat // 2
    inner = (q >= middle - 1) & (q <= middle) if npat > 2 else q == 0
    crossing = (
        (lower, upper, 0, inner),
        (upper, lower, last, jnp.logical_not(inner)),
    )

    local = [
        pltpu.make_async_copy(cond_in, cond, in_s.at[0]),
        pltpu.make_async_copy(wf_in, warm.at[0], in_s.at[1]),
        pltpu.make_async_copy(wa_in, warm.at[1], in_s.at[2]),
        pltpu.make_async_copy(elec_in, elec, in_s.at[3]),
        pltpu.make_async_copy(pats_in, pats, in_s.at[4]),
        pltpu.make_async_copy(obs_in, obs, in_s.at[5]),
    ]

    def member(stage, k):
        return (v // group) * group + k if stage == 0 else k * group + lax.rem(v, group)

    barrier = pltpu.get_barrier_semaphore()

    def greet(device):
        pl.semaphore_signal(barrier, inc=1, device_id=device, device_id_type=MESH)

    @pl.when(has_lo)
    def _():
        greet((q, v - 1))

    @pl.when(has_hi)
    def _():
        greet((q, v + 1))

    expected = has_lo.astype(jnp.int32) + has_hi.astype(jnp.int32)
    for source, target, via, taken in crossing:
        on_path = taken & ((v == source) | (v == target))

        @pl.when(on_path)
        def _():
            greet((q, via))

        @pl.when(taken & (v == via))
        def _():
            greet((q, source))
            greet((q, target))

        expected = expected + on_path.astype(jnp.int32)
        expected = expected + 2 * (taken & (v == via)).astype(jnp.int32)

    for stage in (1, 0):
        for j in far_first(sizes[stage]):
            greet((q, member(stage, lax.rem(rank[stage] + j, sizes[stage]))))
    below, above = q > 0, q < npat - 1

    @pl.when(below)
    def _():
        greet((q - 1, v))

    @pl.when(above)
    def _():
        greet((q + 1, v))

    expected = expected + below.astype(jnp.int32) + above.astype(jnp.int32)
    for copy in local:
        copy.start()

    rows = lax.broadcasted_iota(jnp.int32, (N, N), 0)
    cols = lax.broadcasted_iota(jnp.int32, (N, N), 1)
    cell = rows * N + cols
    trow = lax.broadcasted_iota(jnp.int32, (PC, N), 0)
    tcol = lax.broadcasted_iota(jnp.int32, (PC, N), 1)
    blank = jnp.zeros((N, N), jnp.float32)

    for d, outside in enumerate((jnp.logical_not(has_lo), jnp.logical_not(has_hi))):
        @pl.when(outside)
        def _():
            sh[d, 0] = blank
            sh[d, 1] = blank
            fh[d] = blank

            @pl.loop(0, PC)
            def _(p):
                for s in range(2):
                    for h in (xh, dh, wh):
                        h[s, d, p] = blank

    tile[...] = jnp.zeros((PC, N), jnp.float32)
    for k in range(7):
        acc[k] = blank

    def neighbour(d):
        return (q, v + 1 - 2 * d)

    def sig_ends(kind, d):
        if kind == 2:
            return di.at[2 + d], fh.at[d]
        plane = (1 - d, d)[kind]
        return cond.at[plane], sh.at[d, plane]

    def sig_copy(kind, d):
        src, dst = sig_ends(kind, d)
        return pltpu.make_async_remote_copy(
            src, dst, sig_s.at[kind, d], sig_r.at[kind, d],
            device_id=neighbour(d), device_id_type=MESH,
        )

    def sig_in(kind, d):
        return pltpu.make_async_remote_copy(
            sig_ends(kind, d)[0], sb.at[kind], sig_s.at[kind, d], sig_rr.at[kind],
            device_id=(q, crossing[d][2]), device_id_type=MESH,
        )

    def sig_out(kind, d):
        return pltpu.make_async_remote_copy(
            sb.at[kind], sig_ends(kind, d)[1], sig_rq.at[kind], sig_r.at[kind, d],
            device_id=(q, crossing[d][1]), device_id_type=MESH,
        )

    def outgoing(stage, s, d, p):
        plane = 1 - d
        if stage == 0:
            return warm.at[s, plane, p]
        return (d0 if stage == 1 else w0).at[s, p, plane]

    def incoming(stage, s, d, p):
        return (xh, dh, wh)[stage].at[s, d, p]

    def halo_copy(stage, s, d, p):
        return pltpu.make_async_remote_copy(
            outgoing(stage, s, d, p), incoming(stage, s, d, p),
            hs.at[stage, s, d, p], hr.at[stage, s, d, p],
            device_id=neighbour(d), device_id_type=MESH,
        )

    def detour_in(stage, s, d, p):
        at = s * PC + p
        return pltpu.make_async_remote_copy(
            outgoing(stage, s, d, p), rb.at[stage, at],
            hs.at[stage, s, d, p], rr.at[stage, at],
            device_id=(q, crossing[d][2]), device_id_type=MESH,
        )

    def detour_out(stage, s, d, p):
        at = s * PC + p
        return pltpu.make_async_remote_copy(
            rb.at[stage, at], incoming(stage, s, d, p),
            rq.at[stage, at], hr.at[stage, s, d, p],
            device_id=(q, crossing[d][1]), device_id_type=MESH,
        )

    exists = (has_hi, has_lo)

    def both(fn):
        for d in range(2):
            @pl.when(exists[d])
            def _():
                fn(d)

    def both_in(fn):
        for d in range(2):
            @pl.when(exists[1 - d])
            def _():
                fn(d)

    def send_sig(kind):
        for d in range(2):
            around = crossing[d][3] & (v == crossing[d][0])

            @pl.when(exists[d] & jnp.logical_not(around))
            def _():
                sig_copy(kind, d).start()

            @pl.when(around)
            def _():
                sig_in(kind, d).start()

    def pass_sig(kind):
        for d in range(2):
            @pl.when(crossing[d][3] & (v == crossing[d][2]))
            def _():
                sig_in(kind, d).wait_recv()
                sig_out(kind, d).start()

    def send_halo(stage, s, p):
        for d in range(2):
            around = crossing[d][3] & (v == crossing[d][0])

            @pl.when(exists[d] & jnp.logical_not(around))
            def _():
                halo_copy(stage, s, d, p).start()

            @pl.when(around)
            def _():
                detour_in(stage, s, d, p).start()

    def pass_on(stage, s, p):
        for d in range(2):
            @pl.when(crossing[d][3] & (v == crossing[d][2]))
            def _():
                detour_in(stage, s, d, p).wait_recv()
                detour_out(stage, s, d, p).start()

    def await_halo(stage, s, p):
        both_in(lambda d: halo_copy(stage, s, d, p).wait_recv())

    for copy in local:
        copy.wait()
    partners = (sizes[0] - 1) + (sizes[1] - 1)
    pl.semaphore_wait(barrier, partners + expected)

    send_sig(0)
    for s in range(2):
        @pl.loop(0, PC)
        def _(p):
            send_halo(0, s, p)
    pass_sig(0)

    lo_open = has_lo.astype(jnp.float32)
    hi_open = has_hi.astype(jnp.float32)

    def couple(k, s, below, above):
        xp = jnp.where(rows < N - 1, 0.5 * (s + up_row(s)), 0.0)
        yp = jnp.where(cols < N - 1, 0.5 * (s + up_col(s)), 0.0)
        xm, ym = down_row(xp), down_col(yp)
        diag = LEAK + (below + above) + (xp + xm) + (yp + ym)
        inv = 1.0 / diag
        for at, value in ((ZL, below), (ZH, above), (XM, xm), (XP, xp), (YM, ym), (YP, yp)):
            co[at, k] = value * inv
        if k in (1, 2):
            dg[k - 1] = diag
        di[k + 1] = inv

    both_in(lambda d: sig_copy(0, d).wait_recv())
    couple(1, cond[0], 0.5 * (cond[0] + sh[0, 1]) * lo_open, 0.5 * (cond[0] + cond[1]))
    couple(2, cond[1], 0.5 * (cond[0] + cond[1]), 0.5 * (cond[1] + sh[1, 0]) * hi_open)
    send_sig(1)
    send_sig(2)

    def apply(k, x, below, above):
        y = co[ZL, k] * below + co[ZH, k] * above
        y = y + co[XM, k] * down_row(x) + co[XP, k] * up_row(x)
        y = y + co[YM, k] * down_col(x) + co[YP, k] * up_col(x)
        return x - y

    def difference(p, first, second, plane, scale):
        here = (2 * v + plane) * PLANE
        plus = jnp.where(cell == elec[pats[first, p]] - here, scale, 0.0)
        return plus - jnp.where(cell == elec[pats[second, p]] - here, scale, 0.0)

    def probe(p, plane):
        return difference(p, 2, 3, plane, 1.0)

    def record(p, values):
        now = tile[...]
        for k, value in values:
            now = jnp.where((trow == p) & (tcol == k), value, now)
        tile[...] = now

    for s in range(2):
        @pl.loop(0, PC)
        def _(p):
            await_halo(0, s, p)
            a, b = warm[s, 0, p], warm[s, 1, p]
            e0 = -apply(1, a, xh[s, 0, p], b)
            e1 = -apply(2, b, a, xh[s, 1, p])
            if s == 0:
                e0 = e0 + difference(p, 0, 1, 0, strength) * di[2]
                e1 = e1 + difference(p, 0, 1, 1, strength) * di[3]
            d0[s, p, 0] = e0
            d0[s, p, 1] = e1
            send_halo(1, s, p)
            g0, g1 = probe(p, 0), probe(p, 1)
            rho = total(dg[0] * e0 * e0 + dg[1] * e1 * e1)
            ge = total(g0 * e0 + g1 * e1)
            if s == 0:
                record(p, ((F_RHO, rho), (F_D, ge), (F_X, total(g0 * a + g1 * b))))
            else:
                record(p, ((YY, rho), (GY, ge)))
            pass_on(0, s, p)

    pass_sig(1)
    pass_sig(2)
    both_in(lambda d: sig_copy(1, d).wait_recv())
    couple(0, sh[0, 1], 0.5 * (sh[0, 0] + sh[0, 1]), 0.5 * (cond[0] + sh[0, 1]) * lo_open)
    couple(3, sh[1, 0], 0.5 * (cond[1] + sh[1, 0]) * hi_open, 0.5 * (sh[1, 0] + sh[1, 1]))
    both_in(lambda d: sig_copy(2, d).wait_recv())
    di[0] = fh[0]
    di[5] = fh[1]

    @pl.loop(0, PC)
    def _(p):
        pass_on(1, 0, p)
        e = [probe(p, k - 2) * di[k] for k in range(6)]
        y = [apply(k, e[k + 1], e[k], e[k + 2]) for k in range(4)]
        for k in range(4):
            gd[p, k] = e[k + 1]
            gw[p, k] = y[k]
        z0, z1 = apply(1, y[1], y[0], y[2]), apply(2, y[2], y[1], y[3])
        g0, g1 = probe(p, 0), probe(p, 1)
        u0, u1 = dg[0] * y[1], dg[1] * y[2]
        record(p, (
            (GG, total(g0 * e[2] + g1 * e[3])),
            (GG + 1, total(g0 * y[1] + g1 * y[2])),
            (GG + 2, total(u0 * y[1] + u1 * y[2])),
            (GG + 3, total(u0 * z0 + u1 * z1)),
        ))

    for s in range(2):
        @pl.loop(0, PC)
        def _(p):
            await_halo(1, s, p)
            a, b = d0[s, p, 0], d0[s, p, 1]
            y0 = apply(1, a, dh[s, 0, p], b)
            y1 = apply(2, b, a, dh[s, 1, p])
            w0[s, p, 0] = y0
            w0[s, p, 1] = y1
            send_halo(2, s, p)
            u0, u1 = dg[0] * y0, dg[1] * y1
            mu = total(u0 * a + u1 * b)
            nu = total(u0 * y0 + u1 * y1)
            gy = total(probe(p, 0) * y0 + probe(p, 1) * y1)
            if s == 0:
                record(p, ((F_MU, mu), (F_NU, nu), (F_W, gy)))
            else:
                cross = total(u0 * gw[p, 1] + u1 * gw[p, 2])
                record(p, ((YY + 1, mu), (YY + 2, nu), (GY + 1, gy), (GY + 2, cross)))
            pass_on(1 + s, 1 - s, p)

    for s in range(2):
        @pl.loop(0, PC)
        def _(p):
            if s == 0:
                pass_on(2, 1, p)
            await_halo(2, s, p)
            a, b = w0[s, p, 0], w0[s, p, 1]
            u0 = dg[0] * apply(1, a, wh[s, 0, p], b)
            u1 = dg[1] * apply(2, b, a, wh[s, 1, p])
            xi = total(a * u0 + b * u1)
            if s == 0:
                record(p, ((F_XI, xi),))
            else:
                cross = total(u0 * gw[p, 1] + u1 * gw[p, 2])
                record(p, ((YY + 3, xi), (GY + 3, cross)))

    def sum_copy(stage, k, slot):
        return pltpu.make_async_remote_copy(
            red.at[stage, slot], red.at[stage, slot],
            red_s.at[stage, k], red_r.at[stage, slot],
            device_id=(q, member(stage, k)), device_id_type=MESH,
        )

    def halos_have_left():
        for kind in range(3):
            both(lambda d: sig_copy(kind, d).wait_send())
            for d in range(2):
                @pl.when(crossing[d][3] & (v == crossing[d][2]))
                def _():
                    sig_out(kind, d).wait_send()

        @pl.loop(0, PC)
        def _(p):
            for stage in range(3):
                for s in range(2):
                    both(lambda d: halo_copy(stage, s, d, p).wait_send())
                    for d in range(2):
                        @pl.when(crossing[d][3] & (v == crossing[d][2]))
                        def _():
                            detour_out(stage, s, d, p).wait_send()

    value = tile[...]
    for stage in range(2):
        mine, size = rank[stage], sizes[stage]
        red[stage, mine] = value
        for j in far_first(size):
            sum_copy(stage, lax.rem(mine + j, size), mine).start()
        if stage == 1:
            halos_have_left()
        for j in range(1, size):
            k = lax.rem(mine + j, size)
            sum_copy(stage, k, k).wait_recv()
        value = red[stage, 0]
        for k in range(1, size):
            value = value + red[stage, k]

    def column(k):
        return jnp.sum(jnp.where(tcol == k, value, 0.0), axis=1, keepdims=True)

    def steps(rho, mu, nu, xi):
        alpha = rho / mu
        rho1 = rho - 2.0 * alpha * mu + alpha * alpha * nu
        beta1 = 1.0 + rho1 / rho
        curve = beta1 * beta1 * mu - 2.0 * alpha * beta1 * nu + alpha * alpha * xi
        alpha1 = rho1 / curve
        return alpha + alpha1 * beta1, -alpha * alpha1

    c1, c2 = steps(column(F_RHO), column(F_MU), column(F_NU), column(F_XI))
    predicted = column(F_X) + c1 * column(F_D) + c2 * column(F_W)
    observed = jnp.zeros((PC, 1), jnp.float32)
    for p in range(PC):
        observed = jnp.where(trow[:, 0:1] == p, obs[p], observed)
    weight = data_weight * (predicted - observed)
    e1, e2 = steps(*(
        column(YY + k) + weight * (2.0 * column(GY + k) + weight * column(GG + k))
        for k in range(4)
    ))
    for k, factor in enumerate((c1, c2, e1, e2, e1 * weight, e2 * weight)):
        kc[k] = jnp.broadcast_to(factor, (PC, N))
    wide = jnp.where(trow == tcol, predicted, 0.0)
    pred_out[...] = jnp.sum(wide, axis=0, keepdims=True)[:, :PC]

    is_outer = (q == 0) | (q == npat - 1) if npat > 2 else q < 0
    is_inner = jnp.logical_not(is_outer)
    outward = jnp.where(q < middle, q - 1, q + 1)
    inward = jnp.where(q < middle, q + 1, q - 1)
    height = N // (PIECES // 2)

    def line_copy(leg, j):
        at = (j // (PIECES // 2), pl.ds(j % (PIECES // 2) * height, height))
        src = (gb, half, grad)[leg].at[at]
        dst = (lb[0], lb[1], grad)[leg].at[at]
        return pltpu.make_async_remote_copy(
            src, dst, ls.at[leg, j], lr.at[leg, j],
            device_id=(outward if leg == 2 else inward, v), device_id_type=MESH,
        )

    def piece(j):
        return j // (PIECES // 2), slice(j % (PIECES // 2) * height, (j % (PIECES // 2) + 1) * height)

    def field(p, s, k):
        if k in (0, 3):
            x, d, w = (h[s, k // 3, p] for h in (xh, dh, wh))
        else:
            x, d, w = warm[s, k - 1, p], d0[s, p, k - 1], w0[s, p, k - 1]
        out = x + kc[2 * s, pl.ds(p, 1), :] * d + kc[2 * s + 1, pl.ds(p, 1), :] * w
        if s == 1:
            out = out + kc[4, pl.ds(p, 1), :] * gd[p, k] + kc[5, pl.ds(p, 1), :] * gw[p, k]
        return out

    def within(plane, x, y):
        acc[3 + plane] += (up_row(x) - x) * (up_row(y) - y)
        acc[5 + plane] += (up_col(x) - x) * (up_col(y) - y)

    def finish(plane):
        lo, hi = acc[plane], acc[plane + 1]
        lo = lo * lo_open if plane == 0 else lo
        hi = hi * hi_open if plane == 1 else hi
        px = jnp.where(rows < N - 1, acc[3 + plane], 0.0)
        py = jnp.where(cols < N - 1, acc[5 + plane], 0.0)
        gb[plane] = -0.5 * ((lo + hi) + (px + down_row(px)) + (py + down_col(py)))

        @pl.when(is_outer)
        def _():
            for j in range(plane * PIECES // 2, (plane + 1) * PIECES // 2):
                line_copy(0, j).start()

    @pl.loop(0, PC)
    def _(p):
        f = [field(p, 0, k) for k in range(3)]
        a = [field(p, 1, k) for k in range(3)]
        top[0, p] = f[2]
        top[1, p] = a[2]
        for k in range(2):
            acc[k] += (f[k + 1] - f[k]) * (a[k + 1] - a[k])
        within(0, f[1], a[1])

    finish(0)

    @pl.loop(0, PC)
    def _(p):
        x, y = top[0, p], top[1, p]
        acc[2] += (field(p, 0, 3) - x) * (field(p, 1, 3) - y)
        within(1, x, y)

    finish(1)

    @pl.when(is_outer)
    def _():
        for j in range(PIECES):
            line_copy(2, j).wait_recv()
        for j in range(PIECES):
            line_copy(0, j).wait_send()

    @pl.when(is_inner)
    def _():
        for j in range(PIECES):
            at = piece(j)
            if npat > 2:
                line_copy(0, j).wait_recv()
                half[at] = gb[at] + lb[0][at]
            else:
                half[at] = gb[at]
            line_copy(1, j).start()
        for j in range(PIECES):
            at = piece(j)
            line_copy(1, j).wait_recv()
            grad[at] = half[at] + lb[1][at]
            if npat > 2:
                line_copy(2, j).start()
        for j in range(PIECES):
            line_copy(1, j).wait_send()
            if npat > 2:
                line_copy(2, j).wait_send()

    grad_out[...] = grad[...]

    for stage in range(2):
        for j in range(1, sizes[stage]):
            sum_copy(stage, lax.rem(rank[stage] + j, sizes[stage]), rank[stage]).wait_send()


def solution(mesh):
    npat, layers = mesh.shape["pat"], mesh.shape["vox"]
    group = 8 if layers >= 64 else 2

    def per_device(conductivity, warm_forward, warm_adjoint, electrodes, patterns, observed):
        planes = conductivity.shape[0]
        strength = 2.0 * math.sqrt(layers * planes * PLANE)
        vmem = pl.BlockSpec(memory_space=pltpu.VMEM)
        hbm = pl.BlockSpec(memory_space=pltpu.HBM)
        f32 = jnp.float32
        dma = pltpu.SemaphoreType.DMA
        groups = layers // group
        widest = max(group, groups)
        gradient, predicted = pl.pallas_call(
            functools.partial(kernel, npat, layers, group, strength),
            out_shape=(
                jax.ShapeDtypeStruct((2, N, N), f32),
                jax.ShapeDtypeStruct((1, PC), f32),
            ),
            in_specs=[hbm] * 6,
            out_specs=(vmem, vmem),
            scratch_shapes=[
                pltpu.VMEM((2, N, N), f32),
                pltpu.VMEM((2, 2, PC, N, N), f32),
                pltpu.SMEM(electrodes.shape, jnp.int32),
                pltpu.SMEM((4, PC), jnp.int32),
                pltpu.SMEM((PC,), f32),
                pltpu.VMEM((2, 2, N, N), f32),
                pltpu.VMEM((2, N, N), f32),
                pltpu.VMEM((2, 2, PC, N, N), f32),
                pltpu.VMEM((2, 2, PC, N, N), f32),
                pltpu.VMEM((2, 2, PC, N, N), f32),
                pltpu.VMEM((2, PC, 2, N, N), f32),
                pltpu.VMEM((2, PC, 2, N, N), f32),
                pltpu.VMEM((PC, 4, N, N), f32),
                pltpu.VMEM((PC, 4, N, N), f32),
                pltpu.VMEM((3, 2 * PC, N, N), f32),
                pltpu.VMEM((3, N, N), f32),
                pltpu.VMEM((6, 4, N, N), f32),
                pltpu.VMEM((2, N, N), f32),
                pltpu.VMEM((6, N, N), f32),
                pltpu.VMEM((7, N, N), f32),
                pltpu.VMEM((2, PC, N, N), f32),
                pltpu.VMEM((PC, N), f32),
                pltpu.VMEM((2, widest, PC, N), f32),
                pltpu.VMEM((6, PC, N), f32),
                pltpu.VMEM((2, N, N), f32),
                pltpu.VMEM((2, N, N), f32),
                pltpu.VMEM((2, N, N), f32),
                pltpu.VMEM((2, N, N), f32),
                pltpu.VMEM((2, N, N), f32),
                dma((6,)),
                dma((3, 2)),
                dma((3, 2)),
                dma((3,)),
                dma((3,)),
                dma((3, 2, 2, PC)),
                dma((3, 2, 2, PC)),
                dma((3, 2 * PC)),
                dma((3, 2 * PC)),
                dma((2, widest)),
                dma((2, widest)),
                dma((3, PIECES)),
                dma((3, PIECES)),
            ],
            compiler_params=pltpu.CompilerParams(
                collective_id=0, has_side_effects=True, vmem_limit_bytes=48 * 2**20
            ),
            name="ert_gradient",
        )(*(
            pltpu.with_memory_space_constraint(x, pltpu.HBM)
            for x in (conductivity, warm_forward, warm_adjoint, electrodes, patterns.T, observed)
        ))
        return gradient, predicted.reshape(PC)

    in_specs = (
        P("vox", None, None),
        P("vox", "pat", None, None),
        P("vox", "pat", None, None),
        P(),
        P("pat", None),
        P("pat"),
    )
    return jax.shard_map(
        per_device,
        mesh=mesh,
        in_specs=in_specs,
        out_specs=(P("vox", None, None), P("pat")),
        check_vma=False,
    )
```

```python
import functools
import math

import jax
import jax.numpy as jnp
from jax import lax
from jax.experimental import pallas as pl
from jax.experimental.pallas import tpu as pltpu
from jax.sharding import PartitionSpec as P

MESH = pl.DeviceIdType.MESH
LEAK = 0.05
N = 128
PLANE = N * N
PC = 8
PIECES = 4

ZL, ZH, XM, XP, YM, YP = range(6)
F_RHO, F_MU, F_NU, F_XI, F_X, F_D, F_W = range(7)
YY, GY, GG = 7, 11, 15


def up_row(x):
    return pltpu.roll(x, N - 1, 0)


def down_row(x):
    return pltpu.roll(x, 1, 0)


def up_col(x):
    return pltpu.roll(x, N - 1, 1)


def down_col(x):
    return pltpu.roll(x, 1, 1)


def total(x):
    part = jnp.sum(x.reshape(N // 8, 8, N), axis=0)
    return jnp.sum(jnp.sum(part, axis=1, keepdims=True), axis=0, keepdims=True)


def far_first(size):
    return sorted(range(1, size), key=lambda j: abs(j - size // 2))


def kernel(
    npat,
    layers,
    group,
    strength,
    cond_in,
    wf_in,
    wa_in,
    elec_in,
    pats_in,
    obs_in,
    grad_out,
    pred_out,
    cond,
    warm,
    elec,
    pats,
    obs,
    sh,
    fh,
    xh,
    dh,
    wh,
    d0,
    w0,
    gd,
    gw,
    rb,
    sb,
    co,
    dg,
    di,
    acc,
    top,
    tile,
    red,
    kc,
    gb,
    lb_outer,
    lb_inner,
    half,
    grad,
    in_s,
    sig_s,
    sig_r,
    sig_rr,
    sig_rq,
    hs,
    hr,
    rr,
    rq,
    red_s,
    red_r,
    ls,
    lr,
):
    lb = (lb_outer, lb_inner)
    q = lax.axis_index("pat")
    v = lax.axis_index("vox")
    last = layers - 1
    has_lo = v > 0
    has_hi = v < last
    groups = layers // group
    rank = (lax.rem(v, group), v // group)
    sizes = (group, groups)
    data_weight = 0.1 * strength
    lower, upper = layers // 2 - 1, layers // 2
    middle = npat // 2
    inner = (q >= middle - 1) & (q <= middle) if npat > 2 else q == 0
    crossing = (
        (lower, upper, 0, inner),
        (upper, lower, last, jnp.logical_not(inner)),
    )

    local = [
        pltpu.make_async_copy(cond_in, cond, in_s.at[0]),
        pltpu.make_async_copy(wf_in, warm.at[0], in_s.at[1]),
        pltpu.make_async_copy(wa_in, warm.at[1], in_s.at[2]),
        pltpu.make_async_copy(elec_in, elec, in_s.at[3]),
        pltpu.make_async_copy(pats_in, pats, in_s.at[4]),
        pltpu.make_async_copy(obs_in, obs, in_s.at[5]),
    ]

    def member(stage, k):
        return (v // group) * group + k if stage == 0 else k * group + lax.rem(v, group)

    barrier = pltpu.get_barrier_semaphore()

    def greet(device):
        pl.semaphore_signal(barrier, inc=1, device_id=device, device_id_type=MESH)

    @pl.when(has_lo)
    def _():
        greet((q, v - 1))

    @pl.when(has_hi)
    def _():
        greet((q, v + 1))

    expected = has_lo.astype(jnp.int32) + has_hi.astype(jnp.int32)
    for source, target, via, taken in crossing:
        on_path = taken & ((v == source) | (v == target))

        @pl.when(on_path)
        def _():
            greet((q, via))

        @pl.when(taken & (v == via))
        def _():
            greet((q, source))
            greet((q, target))

        expected = expected + on_path.astype(jnp.int32)
        expected = expected + 2 * (taken & (v == via)).astype(jnp.int32)

    for stage in (1, 0):
        for j in far_first(sizes[stage]):
            greet((q, member(stage, lax.rem(rank[stage] + j, sizes[stage]))))
    below, above = q > 0, q < npat - 1

    @pl.when(below)
    def _():
        greet((q - 1, v))

    @pl.when(above)
    def _():
        greet((q + 1, v))

    expected = expected + below.astype(jnp.int32) + above.astype(jnp.int32)
    for copy in local:
        copy.start()

    rows = lax.broadcasted_iota(jnp.int32, (N, N), 0)
    cols = lax.broadcasted_iota(jnp.int32, (N, N), 1)
    cell = rows * N + cols
    trow = lax.broadcasted_iota(jnp.int32, (PC, N), 0)
    tcol = lax.broadcasted_iota(jnp.int32, (PC, N), 1)
    blank = jnp.zeros((N, N), jnp.float32)

    for d, outside in enumerate((jnp.logical_not(has_lo), jnp.logical_not(has_hi))):
        @pl.when(outside)
        def _():
            sh[d, 0] = blank
            sh[d, 1] = blank
            fh[d] = blank

            @pl.loop(0, PC)
            def _(p):
                for s in range(2):
                    for h in (xh, dh, wh):
                        h[s, d, p] = blank

    tile[...] = jnp.zeros((PC, N), jnp.float32)
    for k in range(7):
        acc[k] = blank

    def neighbour(d):
        return (q, v + 1 - 2 * d)

    def sig_ends(kind, d):
        if kind == 2:
            return di.at[2 + d], fh.at[d]
        plane = (1 - d, d)[kind]
        return cond.at[plane], sh.at[d, plane]

    def sig_copy(kind, d):
        src, dst = sig_ends(kind, d)
        return pltpu.make_async_remote_copy(
            src, dst, sig_s.at[kind, d], sig_r.at[kind, d],
            device_id=neighbour(d), device_id_type=MESH,
        )

    def sig_in(kind, d):
        return pltpu.make_async_remote_copy(
            sig_ends(kind, d)[0], sb.at[kind], sig_s.at[kind, d], sig_rr.at[kind],
            device_id=(q, crossing[d][2]), device_id_type=MESH,
        )

    def sig_out(kind, d):
        return pltpu.make_async_remote_copy(
            sb.at[kind], sig_ends(kind, d)[1], sig_rq.at[kind], sig_r.at[kind, d],
            device_id=(q, crossing[d][1]), device_id_type=MESH,
        )

    def outgoing(stage, s, d, p):
        plane = 1 - d
        if stage == 0:
            return warm.at[s, plane, p]
        return (d0 if stage == 1 else w0).at[s, p, plane]

    def incoming(stage, s, d, p):
        return (xh, dh, wh)[stage].at[s, d, p]

    def halo_copy(stage, s, d, p):
        return pltpu.make_async_remote_copy(
            outgoing(stage, s, d, p), incoming(stage, s, d, p),
            hs.at[stage, s, d, p], hr.at[stage, s, d, p],
            device_id=neighbour(d), device_id_type=MESH,
        )

    def detour_in(stage, s, d, p):
        at = s * PC + p
        return pltpu.make_async_remote_copy(
            outgoing(stage, s, d, p), rb.at[stage, at],
            hs.at[stage, s, d, p], rr.at[stage, at],
            device_id=(q, crossing[d][2]), device_id_type=MESH,
        )

    def detour_out(stage, s, d, p):
        at = s * PC + p
        return pltpu.make_async_remote_copy(
            rb.at[stage, at], incoming(stage, s, d, p),
            rq.at[stage, at], hr.at[stage, s, d, p],
            device_id=(q, crossing[d][1]), device_id_type=MESH,
        )

    exists = (has_hi, has_lo)

    def both(fn):
        for d in range(2):
            @pl.when(exists[d])
            def _():
                fn(d)

    def both_in(fn):
        for d in range(2):
            @pl.when(exists[1 - d])
            def _():
                fn(d)

    def send_sig(kind):
        for d in range(2):
            around = crossing[d][3] & (v == crossing[d][0])

            @pl.when(exists[d] & jnp.logical_not(around))
            def _():
                sig_copy(kind, d).start()

            @pl.when(around)
            def _():
                sig_in(kind, d).start()

    def pass_sig(kind):
        for d in range(2):
            @pl.when(crossing[d][3] & (v == crossing[d][2]))
            def _():
                sig_in(kind, d).wait_recv()
                sig_out(kind, d).start()

    def send_halo(stage, s, p):
        for d in range(2):
            around = crossing[d][3] & (v == crossing[d][0])

            @pl.when(exists[d] & jnp.logical_not(around))
            def _():
                halo_copy(stage, s, d, p).start()

            @pl.when(around)
            def _():
                detour_in(stage, s, d, p).start()

    def pass_on(stage, s, p):
        for d in range(2):
            @pl.when(crossing[d][3] & (v == crossing[d][2]))
            def _():
                detour_in(stage, s, d, p).wait_recv()
                detour_out(stage, s, d, p).start()

    def await_halo(stage, s, p):
        both_in(lambda d: halo_copy(stage, s, d, p).wait_recv())

    for copy in local:
        copy.wait()
    partners = (sizes[0] - 1) + (sizes[1] - 1)
    pl.semaphore_wait(barrier, partners + expected)

    send_sig(0)
    for s in range(2):
        @pl.loop(0, PC)
        def _(p):
            send_halo(0, s, p)
    pass_sig(0)

    lo_open = has_lo.astype(jnp.float32)
    hi_open = has_hi.astype(jnp.float32)

    def couple(k, s, below, above):
        xp = jnp.where(rows < N - 1, 0.5 * (s + up_row(s)), 0.0)
        yp = jnp.where(cols < N - 1, 0.5 * (s + up_col(s)), 0.0)
        xm, ym = down_row(xp), down_col(yp)
        diag = LEAK + (below + above) + (xp + xm) + (yp + ym)
        inv = 1.0 / diag
        for at, value in ((ZL, below), (ZH, above), (XM, xm), (XP, xp), (YM, ym), (YP, yp)):
            co[at, k] = value * inv
        if k in (1, 2):
            dg[k - 1] = diag
        di[k + 1] = inv

    both_in(lambda d: sig_copy(0, d).wait_recv())
    couple(1, cond[0], 0.5 * (cond[0] + sh[0, 1]) * lo_open, 0.5 * (cond[0] + cond[1]))
    couple(2, cond[1], 0.5 * (cond[0] + cond[1]), 0.5 * (cond[1] + sh[1, 0]) * hi_open)
    send_sig(1)
    send_sig(2)

    def apply(k, x, below, above):
        y = co[ZL, k] * below + co[ZH, k] * above
        y = y + co[XM, k] * down_row(x) + co[XP, k] * up_row(x)
        y = y + co[YM, k] * down_col(x) + co[YP, k] * up_col(x)
        return x - y

    def difference(p, first, second, plane, scale):
        here = (2 * v + plane) * PLANE
        plus = jnp.where(cell == elec[pats[first, p]] - here, scale, 0.0)
        return plus - jnp.where(cell == elec[pats[second, p]] - here, scale, 0.0)

    def probe(p, plane):
        return difference(p, 2, 3, plane, 1.0)

    def record(p, values):
        now = tile[...]
        for k, value in values:
            now = jnp.where((trow == p) & (tcol == k), value, now)
        tile[...] = now

    for s in range(2):
        @pl.loop(0, PC)
        def _(p):
            await_halo(0, s, p)
            a, b = warm[s, 0, p], warm[s, 1, p]
            e0 = -apply(1, a, xh[s, 0, p], b)
            e1 = -apply(2, b, a, xh[s, 1, p])
            if s == 0:
                e0 = e0 + difference(p, 0, 1, 0, strength) * di[2]
                e1 = e1 + difference(p, 0, 1, 1, strength) * di[3]
            d0[s, p, 0] = e0
            d0[s, p, 1] = e1
            send_halo(1, s, p)
            g0, g1 = probe(p, 0), probe(p, 1)
            rho = total(dg[0] * e0 * e0 + dg[1] * e1 * e1)
            ge = total(g0 * e0 + g1 * e1)
            if s == 0:
                record(p, ((F_RHO, rho), (F_D, ge), (F_X, total(g0 * a + g1 * b))))
            else:
                record(p, ((YY, rho), (GY, ge)))
            pass_on(0, s, p)

    pass_sig(1)
    pass_sig(2)
    both_in(lambda d: sig_copy(1, d).wait_recv())
    couple(0, sh[0, 1], 0.5 * (sh[0, 0] + sh[0, 1]), 0.5 * (cond[0] + sh[0, 1]) * lo_open)
    couple(3, sh[1, 0], 0.5 * (cond[1] + sh[1, 0]) * hi_open, 0.5 * (sh[1, 0] + sh[1, 1]))
    both_in(lambda d: sig_copy(2, d).wait_recv())
    di[0] = fh[0]
    di[5] = fh[1]

    @pl.loop(0, PC)
    def _(p):
        pass_on(1, 0, p)
        e = [probe(p, k - 2) * di[k] for k in range(6)]
        y = [apply(k, e[k + 1], e[k], e[k + 2]) for k in range(4)]
        for k in range(4):
            gd[p, k] = e[k + 1]
            gw[p, k] = y[k]
        z0, z1 = apply(1, y[1], y[0], y[2]), apply(2, y[2], y[1], y[3])
        g0, g1 = probe(p, 0), probe(p, 1)
        u0, u1 = dg[0] * y[1], dg[1] * y[2]
        record(p, (
            (GG, total(g0 * e[2] + g1 * e[3])),
            (GG + 1, total(g0 * y[1] + g1 * y[2])),
            (GG + 2, total(u0 * y[1] + u1 * y[2])),
            (GG + 3, total(u0 * z0 + u1 * z1)),
        ))

    for s in range(2):
        @pl.loop(0, PC)
        def _(p):
            await_halo(1, s, p)
            a, b = d0[s, p, 0], d0[s, p, 1]
            y0 = apply(1, a, dh[s, 0, p], b)
            y1 = apply(2, b, a, dh[s, 1, p])
            w0[s, p, 0] = y0
            w0[s, p, 1] = y1
            send_halo(2, s, p)
            u0, u1 = dg[0] * y0, dg[1] * y1
            mu = total(u0 * a + u1 * b)
            nu = total(u0 * y0 + u1 * y1)
            gy = total(probe(p, 0) * y0 + probe(p, 1) * y1)
            if s == 0:
                record(p, ((F_MU, mu), (F_NU, nu), (F_W, gy)))
            else:
                cross = total(u0 * gw[p, 1] + u1 * gw[p, 2])
                record(p, ((YY + 1, mu), (YY + 2, nu), (GY + 1, gy), (GY + 2, cross)))
            pass_on(1 + s, 1 - s, p)

    for s in range(2):
        @pl.loop(0, PC)
        def _(p):
            if s == 0:
                pass_on(2, 1, p)
            await_halo(2, s, p)
            a, b = w0[s, p, 0], w0[s, p, 1]
            u0 = dg[0] * apply(1, a, wh[s, 0, p], b)
            u1 = dg[1] * apply(2, b, a, wh[s, 1, p])
            xi = total(a * u0 + b * u1)
            if s == 0:
                record(p, ((F_XI, xi),))
            else:
                cross = total(u0 * gw[p, 1] + u1 * gw[p, 2])
                record(p, ((YY + 3, xi), (GY + 3, cross)))

    def sum_copy(stage, k, slot):
        return pltpu.make_async_remote_copy(
            red.at[stage, slot], red.at[stage, slot],
            red_s.at[stage, k], red_r.at[stage, slot],
            device_id=(q, member(stage, k)), device_id_type=MESH,
        )

    def halos_have_left():
        for kind in range(3):
            both(lambda d: sig_copy(kind, d).wait_send())
            for d in range(2):
                @pl.when(crossing[d][3] & (v == crossing[d][2]))
                def _():
                    sig_out(kind, d).wait_send()

        @pl.loop(0, PC)
        def _(p):
            for stage in range(3):
                for s in range(2):
                    both(lambda d: halo_copy(stage, s, d, p).wait_send())
                    for d in range(2):
                        @pl.when(crossing[d][3] & (v == crossing[d][2]))
                        def _():
                            detour_out(stage, s, d, p).wait_send()

    value = tile[...]
    for stage in range(2):
        mine, size = rank[stage], sizes[stage]
        red[stage, mine] = value
        for j in far_first(size):
            sum_copy(stage, lax.rem(mine + j, size), mine).start()
        if stage == 1:
            halos_have_left()
        for j in range(1, size):
            k = lax.rem(mine + j, size)
            sum_copy(stage, k, k).wait_recv()
        value = red[stage, 0]
        for k in range(1, size):
            value = value + red[stage, k]

    def column(k):
        return jnp.sum(jnp.where(tcol == k, value, 0.0), axis=1, keepdims=True)

    def steps(rho, mu, nu, xi):
        alpha = rho / mu
        rho1 = rho - 2.0 * alpha * mu + alpha * alpha * nu
        beta1 = 1.0 + rho1 / rho
        curve = beta1 * beta1 * mu - 2.0 * alpha * beta1 * nu + alpha * alpha * xi
        alpha1 = rho1 / curve
        return alpha + alpha1 * beta1, -alpha * alpha1

    c1, c2 = steps(column(F_RHO), column(F_MU), column(F_NU), column(F_XI))
    predicted = column(F_X) + c1 * column(F_D) + c2 * column(F_W)
    observed = jnp.zeros((PC, 1), jnp.float32)
    for p in range(PC):
        observed = jnp.where(trow[:, 0:1] == p, obs[p], observed)
    weight = data_weight * (predicted - observed)
    e1, e2 = steps(*(
        column(YY + k) + weight * (2.0 * column(GY + k) + weight * column(GG + k))
        for k in range(4)
    ))
    for k, factor in enumerate((c1, c2, e1, e2, e1 * weight, e2 * weight)):
        kc[k] = jnp.broadcast_to(factor, (PC, N))
    wide = jnp.where(trow == tcol, predicted, 0.0)
    pred_out[...] = jnp.sum(wide, axis=0, keepdims=True)[:, :PC]

    is_outer = (q == 0) | (q == npat - 1) if npat > 2 else q < 0
    is_inner = jnp.logical_not(is_outer)
    outward = jnp.where(q < middle, q - 1, q + 1)
    inward = jnp.where(q < middle, q + 1, q - 1)
    height = N // (PIECES // 2)

    def line_copy(leg, j):
        at = (j // (PIECES // 2), pl.ds(j % (PIECES // 2) * height, height))
        src = (gb, half, grad)[leg].at[at]
        dst = (lb[0], lb[1], grad)[leg].at[at]
        return pltpu.make_async_remote_copy(
            src, dst, ls.at[leg, j], lr.at[leg, j],
            device_id=(outward if leg == 2 else inward, v), device_id_type=MESH,
        )

    def piece(j):
        return j // (PIECES // 2), slice(j % (PIECES // 2) * height, (j % (PIECES // 2) + 1) * height)

    def field(p, s, k):
        if k in (0, 3):
            x, d, w = (h[s, k // 3, p] for h in (xh, dh, wh))
        else:
            x, d, w = warm[s, k - 1, p], d0[s, p, k - 1], w0[s, p, k - 1]
        out = x + kc[2 * s, pl.ds(p, 1), :] * d + kc[2 * s + 1, pl.ds(p, 1), :] * w
        if s == 1:
            out = out + kc[4, pl.ds(p, 1), :] * gd[p, k] + kc[5, pl.ds(p, 1), :] * gw[p, k]
        return out

    def within(plane, x, y):
        acc[3 + plane] += (up_row(x) - x) * (up_row(y) - y)
        acc[5 + plane] += (up_col(x) - x) * (up_col(y) - y)

    def finish(plane):
        lo, hi = acc[plane], acc[plane + 1]
        lo = lo * lo_open if plane == 0 else lo
        hi = hi * hi_open if plane == 1 else hi
        px = jnp.where(rows < N - 1, acc[3 + plane], 0.0)
        py = jnp.where(cols < N - 1, acc[5 + plane], 0.0)
        gb[plane] = -0.5 * ((lo + hi) + (px + down_row(px)) + (py + down_col(py)))

        @pl.when(is_outer)
        def _():
            for j in range(plane * PIECES // 2, (plane + 1) * PIECES // 2):
                line_copy(0, j).start()

    @pl.loop(0, PC)
    def _(p):
        f = [field(p, 0, k) for k in range(3)]
        a = [field(p, 1, k) for k in range(3)]
        top[0, p] = f[2]
        top[1, p] = a[2]
        for k in range(2):
            acc[k] += (f[k + 1] - f[k]) * (a[k + 1] - a[k])
        within(0, f[1], a[1])

    finish(0)

    @pl.loop(0, PC)
    def _(p):
        x, y = top[0, p], top[1, p]
        acc[2] += (field(p, 0, 3) - x) * (field(p, 1, 3) - y)
        within(1, x, y)

    finish(1)

    @pl.when(is_outer)
    def _():
        for j in range(PIECES):
            line_copy(2, j).wait_recv()
        for j in range(PIECES):
            line_copy(0, j).wait_send()

    @pl.when(is_inner)
    def _():
        for j in range(PIECES):
            at = piece(j)
            if npat > 2:
                line_copy(0, j).wait_recv()
                half[at] = gb[at] + lb[0][at]
            else:
                half[at] = gb[at]
            line_copy(1, j).start()
        for j in range(PIECES):
            at = piece(j)
            line_copy(1, j).wait_recv()
            grad[at] = half[at] + lb[1][at]
            if npat > 2:
                line_copy(2, j).start()
        for j in range(PIECES):
            line_copy(1, j).wait_send()
            if npat > 2:
                line_copy(2, j).wait_send()

    grad_out[...] = grad[...]

    for stage in range(2):
        for j in range(1, sizes[stage]):
            sum_copy(stage, lax.rem(rank[stage] + j, sizes[stage]), rank[stage]).wait_send()


def solution(mesh):
    npat, layers = mesh.shape["pat"], mesh.shape["vox"]
    group = 8 if layers >= 64 else 2

    def per_device(conductivity, warm_forward, warm_adjoint, electrodes, patterns, observed):
        planes = conductivity.shape[0]
        strength = 2.0 * math.sqrt(layers * planes * PLANE)
        vmem = pl.BlockSpec(memory_space=pltpu.VMEM)
        hbm = pl.BlockSpec(memory_space=pltpu.HBM)
        f32 = jnp.float32
        dma = pltpu.SemaphoreType.DMA
        groups = layers // group
        widest = max(group, groups)
        gradient, predicted = pl.pallas_call(
            functools.partial(kernel, npat, layers, group, strength),
            out_shape=(
                jax.ShapeDtypeStruct((2, N, N), f32),
                jax.ShapeDtypeStruct((1, PC), f32),
            ),
            in_specs=[hbm] * 6,
            out_specs=(vmem, vmem),
            scratch_shapes=[
                pltpu.VMEM((2, N, N), f32),
                pltpu.VMEM((2, 2, PC, N, N), f32),
                pltpu.SMEM(electrodes.shape, jnp.int32),
                pltpu.SMEM((4, PC), jnp.int32),
                pltpu.SMEM((PC,), f32),
                pltpu.VMEM((2, 2, N, N), f32),
                pltpu.VMEM((2, N, N), f32),
                pltpu.VMEM((2, 2, PC, N, N), f32),
                pltpu.VMEM((2, 2, PC, N, N), f32),
                pltpu.VMEM((2, 2, PC, N, N), f32),
                pltpu.VMEM((2, PC, 2, N, N), f32),
                pltpu.VMEM((2, PC, 2, N, N), f32),
                pltpu.VMEM((PC, 4, N, N), f32),
                pltpu.VMEM((PC, 4, N, N), f32),
                pltpu.VMEM((3, 2 * PC, N, N), f32),
                pltpu.VMEM((3, N, N), f32),
                pltpu.VMEM((6, 4, N, N), f32),
                pltpu.VMEM((2, N, N), f32),
                pltpu.VMEM((6, N, N), f32),
                pltpu.VMEM((7, N, N), f32),
                pltpu.VMEM((2, PC, N, N), f32),
                pltpu.VMEM((PC, N), f32),
                pltpu.VMEM((2, widest, PC, N), f32),
                pltpu.VMEM((6, PC, N), f32),
                pltpu.VMEM((2, N, N), f32),
                pltpu.VMEM((2, N, N), f32),
                pltpu.VMEM((2, N, N), f32),
                pltpu.VMEM((2, N, N), f32),
                pltpu.VMEM((2, N, N), f32),
                dma((6,)),
                dma((3, 2)),
                dma((3, 2)),
                dma((3,)),
                dma((3,)),
                dma((3, 2, 2, PC)),
                dma((3, 2, 2, PC)),
                dma((3, 2 * PC)),
                dma((3, 2 * PC)),
                dma((2, widest)),
                dma((2, widest)),
                dma((3, PIECES)),
                dma((3, PIECES)),
            ],
            compiler_params=pltpu.CompilerParams(
                collective_id=0, has_side_effects=True, vmem_limit_bytes=48 * 2**20
            ),
            name="ert_gradient",
        )(*(
            pltpu.with_memory_space_constraint(x, pltpu.HBM)
            for x in (conductivity, warm_forward, warm_adjoint, electrodes, patterns.T, observed)
        ))
        return gradient, predicted.reshape(PC)

    in_specs = (
        P("vox", None, None),
        P("vox", "pat", None, None),
        P("vox", "pat", None, None),
        P(),
        P("pat", None),
        P("pat"),
    )
    return jax.shard_map(
        per_device,
        mesh=mesh,
        in_specs=in_specs,
        out_specs=(P("vox", None, None), P("pat")),
        check_vma=False,
    )
```

```python
import functools
import math

import jax
import jax.numpy as jnp
from jax import lax
from jax.experimental import pallas as pl
from jax.experimental.pallas import tpu as pltpu
from jax.sharding import PartitionSpec as P

MESH = pl.DeviceIdType.MESH
LEAK = 0.05
N = 128
PLANE = N * N
PC = 8
PIECES = 8

ZL, ZH, XM, XP, YM, YP = range(6)
F_RHO, F_MU, F_NU, F_XI, F_X, F_D, F_W = range(7)
YY, GY, GG = 7, 11, 15


def up_row(x):
    return pltpu.roll(x, N - 1, 0)


def down_row(x):
    return pltpu.roll(x, 1, 0)


def up_col(x):
    return pltpu.roll(x, N - 1, 1)


def down_col(x):
    return pltpu.roll(x, 1, 1)


def total(x):
    part = jnp.sum(x.reshape(N // 8, 8, N), axis=0)
    return jnp.sum(jnp.sum(part, axis=1, keepdims=True), axis=0, keepdims=True)


def kernel(
    npat,
    layers,
    group,
    strength,
    cond_in,
    wf_in,
    wa_in,
    elec_in,
    pats_in,
    obs_in,
    grad_out,
    pred_out,
    cond,
    warm,
    elec,
    pats,
    obs,
    sh,
    fh,
    xh,
    dh,
    wh,
    d0,
    w0,
    gd,
    gw,
    rb,
    sb,
    co,
    dg,
    di,
    acc,
    top,
    tile,
    red,
    kc,
    gb,
    lb_outer,
    lb_inner,
    half,
    grad,
    in_s,
    sig_s,
    sig_r,
    sig_rr,
    sig_rq,
    hs,
    hr,
    rr,
    rq,
    red_s,
    red_r,
    ls,
    lr,
):
    lb = (lb_outer, lb_inner)
    q = lax.axis_index("pat")
    v = lax.axis_index("vox")
    last = layers - 1
    has_lo = v > 0
    has_hi = v < last
    groups = layers // group
    rank = (lax.rem(v, group), v // group)
    sizes = (group, groups)
    data_weight = 0.1 * strength
    lower, upper = layers // 2 - 1, layers // 2
    middle = npat // 2
    inner = (q >= middle - 1) & (q <= middle) if npat > 2 else q == 0
    crossing = (
        (lower, upper, 0, inner),
        (upper, lower, last, jnp.logical_not(inner)),
    )

    local = [
        pltpu.make_async_copy(cond_in, cond, in_s.at[0]),
        pltpu.make_async_copy(wf_in, warm.at[0], in_s.at[1]),
        pltpu.make_async_copy(wa_in, warm.at[1], in_s.at[2]),
        pltpu.make_async_copy(elec_in, elec, in_s.at[3]),
        pltpu.make_async_copy(pats_in, pats, in_s.at[4]),
        pltpu.make_async_copy(obs_in, obs, in_s.at[5]),
    ]

    def member(stage, k):
        return (v // group) * group + k if stage == 0 else k * group + lax.rem(v, group)

    barrier = pltpu.get_barrier_semaphore()

    def greet(device):
        pl.semaphore_signal(barrier, inc=1, device_id=device, device_id_type=MESH)

    @pl.when(has_lo)
    def _():
        greet((q, v - 1))

    @pl.when(has_hi)
    def _():
        greet((q, v + 1))

    expected = has_lo.astype(jnp.int32) + has_hi.astype(jnp.int32)
    for source, target, via, taken in crossing:
        on_path = taken & ((v == source) | (v == target))

        @pl.when(on_path)
        def _():
            greet((q, via))

        @pl.when(taken & (v == via))
        def _():
            greet((q, source))
            greet((q, target))

        expected = expected + on_path.astype(jnp.int32)
        expected = expected + 2 * (taken & (v == via)).astype(jnp.int32)

    for stage in range(2):
        for j in range(1, sizes[stage]):
            greet((q, member(stage, lax.rem(rank[stage] + j, sizes[stage]))))
    below, above = q > 0, q < npat - 1

    @pl.when(below)
    def _():
        greet((q - 1, v))

    @pl.when(above)
    def _():
        greet((q + 1, v))

    expected = expected + below.astype(jnp.int32) + above.astype(jnp.int32)
    for copy in local:
        copy.start()

    rows = lax.broadcasted_iota(jnp.int32, (N, N), 0)
    cols = lax.broadcasted_iota(jnp.int32, (N, N), 1)
    cell = rows * N + cols
    trow = lax.broadcasted_iota(jnp.int32, (PC, N), 0)
    tcol = lax.broadcasted_iota(jnp.int32, (PC, N), 1)
    blank = jnp.zeros((N, N), jnp.float32)

    for d, outside in enumerate((jnp.logical_not(has_lo), jnp.logical_not(has_hi))):
        @pl.when(outside)
        def _():
            sh[d, 0] = blank
            sh[d, 1] = blank
            fh[d] = blank

            @pl.loop(0, PC)
            def _(p):
                for s in range(2):
                    for h in (xh, dh, wh):
                        h[s, d, p] = blank

    tile[...] = jnp.zeros((PC, N), jnp.float32)
    for k in range(7):
        acc[k] = blank

    def neighbour(d):
        return (q, v + 1 - 2 * d)

    def sig_ends(kind, d):
        if kind == 2:
            return di.at[2 + d], fh.at[d]
        plane = (1 - d, d)[kind]
        return cond.at[plane], sh.at[d, plane]

    def sig_copy(kind, d):
        src, dst = sig_ends(kind, d)
        return pltpu.make_async_remote_copy(
            src, dst, sig_s.at[kind, d], sig_r.at[kind, d],
            device_id=neighbour(d), device_id_type=MESH,
        )

    def sig_in(kind, d):
        return pltpu.make_async_remote_copy(
            sig_ends(kind, d)[0], sb.at[kind], sig_s.at[kind, d], sig_rr.at[kind],
            device_id=(q, crossing[d][2]), device_id_type=MESH,
        )

    def sig_out(kind, d):
        return pltpu.make_async_remote_copy(
            sb.at[kind], sig_ends(kind, d)[1], sig_rq.at[kind], sig_r.at[kind, d],
            device_id=(q, crossing[d][1]), device_id_type=MESH,
        )

    def outgoing(stage, s, d, p):
        plane = 1 - d
        if stage == 0:
            return warm.at[s, plane, p]
        return (d0 if stage == 1 else w0).at[s, p, plane]

    def incoming(stage, s, d, p):
        return (xh, dh, wh)[stage].at[s, d, p]

    def halo_copy(stage, s, d, p):
        return pltpu.make_async_remote_copy(
            outgoing(stage, s, d, p), incoming(stage, s, d, p),
            hs.at[stage, s, d, p], hr.at[stage, s, d, p],
            device_id=neighbour(d), device_id_type=MESH,
        )

    def detour_in(stage, s, d, p):
        at = s * PC + p
        return pltpu.make_async_remote_copy(
            outgoing(stage, s, d, p), rb.at[stage, at],
            hs.at[stage, s, d, p], rr.at[stage, at],
            device_id=(q, crossing[d][2]), device_id_type=MESH,
        )

    def detour_out(stage, s, d, p):
        at = s * PC + p
        return pltpu.make_async_remote_copy(
            rb.at[stage, at], incoming(stage, s, d, p),
            rq.at[stage, at], hr.at[stage, s, d, p],
            device_id=(q, crossing[d][1]), device_id_type=MESH,
        )

    exists = (has_hi, has_lo)

    def both(fn):
        for d in range(2):
            @pl.when(exists[d])
            def _():
                fn(d)

    def both_in(fn):
        for d in range(2):
            @pl.when(exists[1 - d])
            def _():
                fn(d)

    def send_sig(kind):
        for d in range(2):
            around = crossing[d][3] & (v == crossing[d][0])

            @pl.when(exists[d] & jnp.logical_not(around))
            def _():
                sig_copy(kind, d).start()

            @pl.when(around)
            def _():
                sig_in(kind, d).start()

    def pass_sig(kind):
        for d in range(2):
            @pl.when(crossing[d][3] & (v == crossing[d][2]))
            def _():
                sig_in(kind, d).wait_recv()
                sig_out(kind, d).start()

    def send_halo(stage, s, p):
        for d in range(2):
            around = crossing[d][3] & (v == crossing[d][0])

            @pl.when(exists[d] & jnp.logical_not(around))
            def _():
                halo_copy(stage, s, d, p).start()

            @pl.when(around)
            def _():
                detour_in(stage, s, d, p).start()

    def pass_on(stage, s, p):
        for d in range(2):
            @pl.when(crossing[d][3] & (v == crossing[d][2]))
            def _():
                detour_in(stage, s, d, p).wait_recv()
                detour_out(stage, s, d, p).start()

    def await_halo(stage, s, p):
        both_in(lambda d: halo_copy(stage, s, d, p).wait_recv())

    for copy in local:
        copy.wait()
    partners = (sizes[0] - 1) + (sizes[1] - 1)
    pl.semaphore_wait(barrier, partners + expected)

    send_sig(0)
    for s in range(2):
        @pl.loop(0, PC)
        def _(p):
            send_halo(0, s, p)
    pass_sig(0)

    lo_open = has_lo.astype(jnp.float32)
    hi_open = has_hi.astype(jnp.float32)

    def couple(k, s, below, above):
        xp = jnp.where(rows < N - 1, 0.5 * (s + up_row(s)), 0.0)
        yp = jnp.where(cols < N - 1, 0.5 * (s + up_col(s)), 0.0)
        xm, ym = down_row(xp), down_col(yp)
        diag = LEAK + (below + above) + (xp + xm) + (yp + ym)
        inv = 1.0 / diag
        for at, value in ((ZL, below), (ZH, above), (XM, xm), (XP, xp), (YM, ym), (YP, yp)):
            co[at, k] = value * inv
        if k in (1, 2):
            dg[k - 1] = diag
        di[k + 1] = inv

    both_in(lambda d: sig_copy(0, d).wait_recv())
    couple(1, cond[0], 0.5 * (cond[0] + sh[0, 1]) * lo_open, 0.5 * (cond[0] + cond[1]))
    couple(2, cond[1], 0.5 * (cond[0] + cond[1]), 0.5 * (cond[1] + sh[1, 0]) * hi_open)
    send_sig(1)
    send_sig(2)

    def apply(k, x, below, above):
        y = co[ZL, k] * below + co[ZH, k] * above
        y = y + co[XM, k] * down_row(x) + co[XP, k] * up_row(x)
        y = y + co[YM, k] * down_col(x) + co[YP, k] * up_col(x)
        return x - y

    def difference(p, first, second, plane, scale):
        here = (2 * v + plane) * PLANE
        plus = jnp.where(cell == elec[pats[first, p]] - here, scale, 0.0)
        return plus - jnp.where(cell == elec[pats[second, p]] - here, scale, 0.0)

    def probe(p, plane):
        return difference(p, 2, 3, plane, 1.0)

    def record(p, values):
        now = tile[...]
        for k, value in values:
            now = jnp.where((trow == p) & (tcol == k), value, now)
        tile[...] = now

    for s in range(2):
        @pl.loop(0, PC)
        def _(p):
            await_halo(0, s, p)
            a, b = warm[s, 0, p], warm[s, 1, p]
            e0 = -apply(1, a, xh[s, 0, p], b)
            e1 = -apply(2, b, a, xh[s, 1, p])
            if s == 0:
                e0 = e0 + difference(p, 0, 1, 0, strength) * di[2]
                e1 = e1 + difference(p, 0, 1, 1, strength) * di[3]
            d0[s, p, 0] = e0
            d0[s, p, 1] = e1
            send_halo(1, s, p)
            pass_on(0, s, p)
            g0, g1 = probe(p, 0), probe(p, 1)
            rho = total(dg[0] * e0 * e0 + dg[1] * e1 * e1)
            ge = total(g0 * e0 + g1 * e1)
            if s == 0:
                record(p, ((F_RHO, rho), (F_D, ge), (F_X, total(g0 * a + g1 * b))))
            else:
                record(p, ((YY, rho), (GY, ge)))

    pass_sig(1)
    pass_sig(2)
    both_in(lambda d: sig_copy(1, d).wait_recv())
    couple(0, sh[0, 1], 0.5 * (sh[0, 0] + sh[0, 1]), 0.5 * (cond[0] + sh[0, 1]) * lo_open)
    couple(3, sh[1, 0], 0.5 * (cond[1] + sh[1, 0]) * hi_open, 0.5 * (sh[1, 0] + sh[1, 1]))
    both_in(lambda d: sig_copy(2, d).wait_recv())
    di[0] = fh[0]
    di[5] = fh[1]

    @pl.loop(0, PC)
    def _(p):
        pass_on(1, 0, p)
        e = [probe(p, k - 2) * di[k] for k in range(6)]
        y = [apply(k, e[k + 1], e[k], e[k + 2]) for k in range(4)]
        for k in range(4):
            gd[p, k] = e[k + 1]
            gw[p, k] = y[k]
        z0, z1 = apply(1, y[1], y[0], y[2]), apply(2, y[2], y[1], y[3])
        g0, g1 = probe(p, 0), probe(p, 1)
        u0, u1 = dg[0] * y[1], dg[1] * y[2]
        record(p, (
            (GG, total(g0 * e[2] + g1 * e[3])),
            (GG + 1, total(g0 * y[1] + g1 * y[2])),
            (GG + 2, total(u0 * y[1] + u1 * y[2])),
            (GG + 3, total(u0 * z0 + u1 * z1)),
        ))

    for s in range(2):
        @pl.loop(0, PC)
        def _(p):
            await_halo(1, s, p)
            a, b = d0[s, p, 0], d0[s, p, 1]
            y0 = apply(1, a, dh[s, 0, p], b)
            y1 = apply(2, b, a, dh[s, 1, p])
            w0[s, p, 0] = y0
            w0[s, p, 1] = y1
            send_halo(2, s, p)
            pass_on(1 + s, 1 - s, p)
            u0, u1 = dg[0] * y0, dg[1] * y1
            mu = total(u0 * a + u1 * b)
            nu = total(u0 * y0 + u1 * y1)
            gy = total(probe(p, 0) * y0 + probe(p, 1) * y1)
            if s == 0:
                record(p, ((F_MU, mu), (F_NU, nu), (F_W, gy)))
            else:
                record(p, ((YY + 1, mu), (YY + 2, nu), (GY + 1, gy)))

    for s in range(2):
        @pl.loop(0, PC)
        def _(p):
            if s == 0:
                pass_on(2, 1, p)
            await_halo(2, s, p)
            a, b = w0[s, p, 0], w0[s, p, 1]
            u0 = dg[0] * apply(1, a, wh[s, 0, p], b)
            u1 = dg[1] * apply(2, b, a, wh[s, 1, p])
            xi = total(a * u0 + b * u1)
            if s == 0:
                record(p, ((F_XI, xi),))
            else:
                k0, k1 = gw[p, 1], gw[p, 2]
                near = total(dg[0] * a * k0 + dg[1] * b * k1)
                record(p, ((YY + 3, xi), (GY + 2, near), (GY + 3, total(u0 * k0 + u1 * k1))))

    def sum_copy(stage, k, slot):
        return pltpu.make_async_remote_copy(
            red.at[stage, slot], red.at[stage, slot],
            red_s.at[stage, k], red_r.at[stage, slot],
            device_id=(q, member(stage, k)), device_id_type=MESH,
        )

    def halos_have_left():
        for kind in range(3):
            both(lambda d: sig_copy(kind, d).wait_send())
            for d in range(2):
                @pl.when(crossing[d][3] & (v == crossing[d][2]))
                def _():
                    sig_out(kind, d).wait_send()

        @pl.loop(0, PC)
        def _(p):
            for stage in range(3):
                for s in range(2):
                    both(lambda d: halo_copy(stage, s, d, p).wait_send())
                    for d in range(2):
                        @pl.when(crossing[d][3] & (v == crossing[d][2]))
                        def _():
                            detour_out(stage, s, d, p).wait_send()

    value = tile[...]
    for stage in range(2):
        mine, size = rank[stage], sizes[stage]
        red[stage, mine] = value
        for j in range(1, size):
            sum_copy(stage, lax.rem(mine + j, size), mine).start()
        if stage == 1:
            halos_have_left()
        for j in range(1, size):
            k = lax.rem(mine + j, size)
            sum_copy(stage, k, k).wait_recv()
        value = red[stage, 0]
        for k in range(1, size):
            value = value + red[stage, k]

    def column(k):
        return jnp.sum(jnp.where(tcol == k, value, 0.0), axis=1, keepdims=True)

    def steps(rho, mu, nu, xi):
        alpha = rho / mu
        rho1 = rho - 2.0 * alpha * mu + alpha * alpha * nu
        beta1 = 1.0 + rho1 / rho
        curve = beta1 * beta1 * mu - 2.0 * alpha * beta1 * nu + alpha * alpha * xi
        alpha1 = rho1 / curve
        return alpha + alpha1 * beta1, -alpha * alpha1

    c1, c2 = steps(column(F_RHO), column(F_MU), column(F_NU), column(F_XI))
    predicted = column(F_X) + c1 * column(F_D) + c2 * column(F_W)
    observed = jnp.zeros((PC, 1), jnp.float32)
    for p in range(PC):
        observed = jnp.where(trow[:, 0:1] == p, obs[p], observed)
    weight = data_weight * (predicted - observed)
    e1, e2 = steps(*(
        column(YY + k) + weight * (2.0 * column(GY + k) + weight * column(GG + k))
        for k in range(4)
    ))
    for k, factor in enumerate((c1, c2, e1, e2, e1 * weight, e2 * weight)):
        kc[k] = jnp.broadcast_to(factor, (PC, N))
    wide = jnp.where(trow == tcol, predicted, 0.0)
    pred_out[...] = jnp.sum(wide, axis=0, keepdims=True)[:, :PC]

    is_outer = (q == 0) | (q == npat - 1) if npat > 2 else q < 0
    is_inner = jnp.logical_not(is_outer)
    outward = jnp.where(q < middle, q - 1, q + 1)
    inward = jnp.where(q < middle, q + 1, q - 1)
    height = N // (PIECES // 2)

    def line_copy(leg, j):
        at = (j // (PIECES // 2), pl.ds(j % (PIECES // 2) * height, height))
        src = (gb, half, grad)[leg].at[at]
        dst = (lb[0], lb[1], grad)[leg].at[at]
        return pltpu.make_async_remote_copy(
            src, dst, ls.at[leg, j], lr.at[leg, j],
            device_id=(outward if leg == 2 else inward, v), device_id_type=MESH,
        )

    def piece(j):
        return j // (PIECES // 2), slice(j % (PIECES // 2) * height, (j % (PIECES // 2) + 1) * height)

    def field(p, s, k):
        if k in (0, 3):
            x, d, w = (h[s, k // 3, p] for h in (xh, dh, wh))
        else:
            x, d, w = warm[s, k - 1, p], d0[s, p, k - 1], w0[s, p, k - 1]
        out = x + kc[2 * s, pl.ds(p, 1), :] * d + kc[2 * s + 1, pl.ds(p, 1), :] * w
        if s == 1:
            out = out + kc[4, pl.ds(p, 1), :] * gd[p, k] + kc[5, pl.ds(p, 1), :] * gw[p, k]
        return out

    def within(plane, x, y):
        acc[3 + plane] += (up_row(x) - x) * (up_row(y) - y)
        acc[5 + plane] += (up_col(x) - x) * (up_col(y) - y)

    def finish(plane):
        lo, hi = acc[plane], acc[plane + 1]
        lo = lo * lo_open if plane == 0 else lo
        hi = hi * hi_open if plane == 1 else hi
        px = jnp.where(rows < N - 1, acc[3 + plane], 0.0)
        py = jnp.where(cols < N - 1, acc[5 + plane], 0.0)
        gb[plane] = -0.5 * ((lo + hi) + (px + down_row(px)) + (py + down_col(py)))

        @pl.when(is_outer)
        def _():
            for j in range(plane * PIECES // 2, (plane + 1) * PIECES // 2):
                line_copy(0, j).start()

    @pl.loop(0, PC)
    def _(p):
        f = [field(p, 0, k) for k in range(3)]
        a = [field(p, 1, k) for k in range(3)]
        top[0, p] = f[2]
        top[1, p] = a[2]
        for k in range(2):
            acc[k] += (f[k + 1] - f[k]) * (a[k + 1] - a[k])
        within(0, f[1], a[1])

    finish(0)

    @pl.loop(0, PC)
    def _(p):
        x, y = top[0, p], top[1, p]
        acc[2] += (field(p, 0, 3) - x) * (field(p, 1, 3) - y)
        within(1, x, y)

    finish(1)

    @pl.when(is_outer)
    def _():
        for j in range(PIECES):
            line_copy(2, j).wait_recv()
        for j in range(PIECES):
            line_copy(0, j).wait_send()

    @pl.when(is_inner)
    def _():
        for j in range(PIECES):
            at = piece(j)
            if npat > 2:
                line_copy(0, j).wait_recv()
                half[at] = gb[at] + lb[0][at]
            else:
                half[at] = gb[at]
            line_copy(1, j).start()
        for j in range(PIECES):
            at = piece(j)
            line_copy(1, j).wait_recv()
            grad[at] = half[at] + lb[1][at]
            if npat > 2:
                line_copy(2, j).start()
        for j in range(PIECES):
            line_copy(1, j).wait_send()
            if npat > 2:
                line_copy(2, j).wait_send()

    grad_out[...] = grad[...]

    for stage in range(2):
        for j in range(1, sizes[stage]):
            sum_copy(stage, lax.rem(rank[stage] + j, sizes[stage]), rank[stage]).wait_send()


def solution(mesh):
    npat, layers = mesh.shape["pat"], mesh.shape["vox"]
    group = 8 if layers >= 64 else 2

    def per_device(conductivity, warm_forward, warm_adjoint, electrodes, patterns, observed):
        planes = conductivity.shape[0]
        strength = 2.0 * math.sqrt(layers * planes * PLANE)
        vmem = pl.BlockSpec(memory_space=pltpu.VMEM)
        hbm = pl.BlockSpec(memory_space=pltpu.HBM)
        f32 = jnp.float32
        dma = pltpu.SemaphoreType.DMA
        groups = layers // group
        widest = max(group, groups)
        gradient, predicted = pl.pallas_call(
            functools.partial(kernel, npat, layers, group, strength),
            out_shape=(
                jax.ShapeDtypeStruct((2, N, N), f32),
                jax.ShapeDtypeStruct((1, PC), f32),
            ),
            in_specs=[hbm] * 6,
            out_specs=(vmem, vmem),
            scratch_shapes=[
                pltpu.VMEM((2, N, N), f32),
                pltpu.VMEM((2, 2, PC, N, N), f32),
                pltpu.SMEM(electrodes.shape, jnp.int32),
                pltpu.SMEM((4, PC), jnp.int32),
                pltpu.SMEM((PC,), f32),
                pltpu.VMEM((2, 2, N, N), f32),
                pltpu.VMEM((2, N, N), f32),
                pltpu.VMEM((2, 2, PC, N, N), f32),
                pltpu.VMEM((2, 2, PC, N, N), f32),
                pltpu.VMEM((2, 2, PC, N, N), f32),
                pltpu.VMEM((2, PC, 2, N, N), f32),
                pltpu.VMEM((2, PC, 2, N, N), f32),
                pltpu.VMEM((PC, 4, N, N), f32),
                pltpu.VMEM((PC, 4, N, N), f32),
                pltpu.VMEM((3, 2 * PC, N, N), f32),
                pltpu.VMEM((3, N, N), f32),
                pltpu.VMEM((6, 4, N, N), f32),
                pltpu.VMEM((2, N, N), f32),
                pltpu.VMEM((6, N, N), f32),
                pltpu.VMEM((7, N, N), f32),
                pltpu.VMEM((2, PC, N, N), f32),
                pltpu.VMEM((PC, N), f32),
                pltpu.VMEM((2, widest, PC, N), f32),
                pltpu.VMEM((6, PC, N), f32),
                pltpu.VMEM((2, N, N), f32),
                pltpu.VMEM((2, N, N), f32),
                pltpu.VMEM((2, N, N), f32),
                pltpu.VMEM((2, N, N), f32),
                pltpu.VMEM((2, N, N), f32),
                dma((6,)),
                dma((3, 2)),
                dma((3, 2)),
                dma((3,)),
                dma((3,)),
                dma((3, 2, 2, PC)),
                dma((3, 2, 2, PC)),
                dma((3, 2 * PC)),
                dma((3, 2 * PC)),
                dma((2, widest)),
                dma((2, widest)),
                dma((3, PIECES)),
                dma((3, PIECES)),
            ],
            compiler_params=pltpu.CompilerParams(
                collective_id=0, has_side_effects=True, vmem_limit_bytes=48 * 2**20
            ),
            name="ert_gradient",
        )(*(
            pltpu.with_memory_space_constraint(x, pltpu.HBM)
            for x in (conductivity, warm_forward, warm_adjoint, electrodes, patterns.T, observed)
        ))
        return gradient, predicted.reshape(PC)

    in_specs = (
        P("vox", None, None),
        P("vox", "pat", None, None),
        P("vox", "pat", None, None),
        P(),
        P("pat", None),
        P("pat"),
    )
    return jax.shard_map(
        per_device,
        mesh=mesh,
        in_specs=in_specs,
        out_specs=(P("vox", None, None), P("pat")),
        check_vma=False,
    )
```
